32 devices in a mesh: dp: 16 (over z, x, core), mp: 2 (over y).
Axes of the slice: x: 2, y: 2, z: 4, core: 2. Of those that a mesh axis runs over, the one named last changes fastest.
Arguments:
- text_tokens: bfloat16 [256, 64, 768], P('dp', 'mp'), may hold values from -6 to 6
- image_tokens: bfloat16 [256, 576, 768], P('dp'), may hold values from -6 to 6
- resolution: int32 [256], P('dp'), may hold values 0 or 1
- query_self: bfloat16 [768, 768], P('dp', 'mp'), may hold values from -0.21875 to 0.21875
- key_self: bfloat16 [768, 768], P('dp', 'mp'), may hold values from -0.21875 to 0.21875
- value_self: bfloat16 [768, 768], P('dp', 'mp'), may hold values from -0.21875 to 0.21875
- mix_self: bfloat16 [768, 768], P('mp', 'dp'), may hold values from -0.875 to 0.875
- query_cross: bfloat16 [768, 768], P('dp', 'mp'), may hold values from -0.21875 to 0.21875
- key_cross: bfloat16 [768, 768], P('dp', 'mp'), may hold values from -0.21875 to 0.21875
- value_cross: bfloat16 [768, 768], P('dp', 'mp'), may hold values from -0.21875 to 0.21875
- mix_cross: bfloat16 [768, 768], P('mp', 'dp'), may hold values from -1.75 to 1.75
- expand: bfloat16 [768, 3072], P('dp', 'mp'), may hold values from -0.21875 to 0.21875
- contract: bfloat16 [3072, 768], P('mp', 'dp'), may hold values from -0.109375 to 0.109375
- first_gain: float32 [768], replicated, may hold values from 0.25 to 1.75
- first_shift: float32 [768], replicated, may hold values from -3 to 3
- second_gain: float32 [768], replicated, may hold values from 0.25 to 1.75
- second_shift: float32 [768], replicated, may hold values from -3 to 3
- third_gain: float32 [768], replicated, may hold values from 0.25 to 1.75
- third_shift: float32 [768], replicated, may hold values from -3 to 3
- cotangent: bfloat16 [256, 64, 768], P('dp', 'mp'), may hold values from -6 to 6
Outputs:
- layer_out: bfloat16 [256, 64, 768], P('dp', 'mp')
- text_grad: float32 [256, 64, 768], P('dp', 'mp')
- image_grad: float32 [256, 576, 768], P('dp', 'mp')
- grad_query_self: float32 [768, 768], P('dp', 'mp')
- grad_key_self: float32 [768, 768], P('dp', 'mp')
- grad_value_self: float32 [768, 768], P('dp', 'mp')
- grad_mix_self: float32 [768, 768], P('mp', 'dp')
- grad_query_cross: float32 [768, 768], P('dp', 'mp')
- grad_key_cross: float32 [768, 768], P('dp', 'mp')
- grad_value_cross: float32 [768, 768], P('dp', 'mp')
- grad_mix_cross: float32 [768, 768], P('mp', 'dp')
- grad_expand: float32 [768, 3072], P('dp', 'mp')
- grad_contract: float32 [3072, 768], P('mp', 'dp')
- grad_first_gain: float32 [768], replicated
- grad_first_shift: float32 [768], replicated
- grad_second_gain: float32 [768], replicated
- grad_second_shift: float32 [768], replicated
- grad_third_gain: float32 [768], replicated
- grad_third_shift: float32 [768], replicated
The draws below stay inside these ranges and needn't reach their ends.
Inputs may be any that keep to these rules, and one draw needn't show every extreme that they name: `resolution`: 1 marks an image of 576 patches, 0 one of 196; patch slots at or past the count are padding.
All inputs are finite; a program needn't handle non-finite values. No bound on the sum of `resolution` on one device may be relied on, other than what follows from the above.
Results may differ from the reference program's by a relative error of at most 0.02.
Values may be sent and summed in bfloat16 or wider, within the bound.
A program may use at most 256 MiB of HBM per device.

```python
import jax
import jax.numpy as jnp
from jax import lax

HD = 64
FF = 3072
D = 768
LEN = 64
PATCH = 576
SMALLP = 196
MICRO = 2
CAPS = 8
CAPTIONS = 256


def with_ends(drawn, stream_key, least, top_value):
    longest = drawn.shape.index(max(drawn.shape))
    spots = []
    for shift in (0, 1):
        where = [jax.random.randint(jax.random.fold_in(stream_key, axis), (), 0, length) for axis, length in enumerate(drawn.shape)]
        where[longest] = (where[longest] + shift) % drawn.shape[longest]
        spots.append(tuple(where))
    return drawn.at[spots[0]].set(least).at[spots[1]].set(top_value)


def level_of(own_key, dims, pieces, smallest, largest):
    def one(position, blocks):
        steps = jax.random.uniform(jax.random.fold_in(jax.random.fold_in(own_key, 6), position), (blocks,), jnp.float32, smallest / len(pieces), largest / len(pieces))
        return jnp.repeat(jnp.exp(steps), dims[position] // blocks).reshape((-1,) + (1,) * (len(dims) - position - 1))

    level = one(*pieces[0])
    for cut in pieces[1:]:
        level = level * one(*cut)
    return level


def scatter_about(rng, dims, deviation, limit, shards=(), held_as=jnp.bfloat16):
    drawn = deviation * jax.random.normal(rng, dims, jnp.float32)
    if shards:
        drawn = drawn * level_of(rng, dims, shards, -0.22, 0.18)
    return jnp.clip(drawn, -limit, limit).astype(held_as)


def setup_inputs(seed: int = 0) -> dict:
    arg_keys = jax.random.split(jax.random.key(seed), 21)
    return {
        "text_tokens": scatter_about(arg_keys[0], (CAPTIONS, LEN, D), 1.0, 6.0, ((0, 16), (1, 2))),
        "image_tokens": scatter_about(arg_keys[1], (CAPTIONS, PATCH, D), 1.0, 6.0, ((0, 16),)),
        "resolution": with_ends((jax.random.randint(arg_keys[2], (CAPTIONS,), 0, 3) < 1).astype(jnp.int32), jax.random.fold_in(arg_keys[2], 1), 0, 1),
        "query_self": scatter_about(arg_keys[3], (D, D), D ** -0.5, 0.21875, ((0, 16), (1, 2))),
        "key_self": scatter_about(arg_keys[4], (D, D), D ** -0.5, 0.21875, ((0, 16), (1, 2))),
        "value_self": scatter_about(arg_keys[5], (D, D), D ** -0.5, 0.21875, ((0, 16), (1, 2))),
        "mix_self": scatter_about(arg_keys[6], (D, D), (D // 16) ** -0.5, 0.875, ((0, 2), (1, 16))),
        "query_cross": scatter_about(arg_keys[7], (D, D), D ** -0.5, 0.21875, ((0, 16), (1, 2))),
        "key_cross": scatter_about(arg_keys[8], (D, D), D ** -0.5, 0.21875, ((0, 16), (1, 2))),
        "value_cross": scatter_about(arg_keys[9], (D, D), D ** -0.5, 0.21875, ((0, 16), (1, 2))),
        "mix_cross": scatter_about(arg_keys[10], (D, D), (D // 64) ** -0.5, 1.75, ((0, 2), (1, 16))),
        "expand": scatter_about(arg_keys[11], (D, FF), D ** -0.5, 0.21875, ((0, 16), (1, 2))),
        "contract": scatter_about(arg_keys[12], (FF, D), FF ** -0.5, 0.109375, ((0, 2), (1, 16))),
        "first_gain": jnp.clip(1.0 + 0.15 * jax.random.normal(arg_keys[13], (D,), jnp.float32), 0.25, 1.75),
        "first_shift": scatter_about(arg_keys[14], (D,), 0.5, 3.0, (), jnp.float32),
        "second_gain": jnp.clip(1.0 + 0.15 * jax.random.normal(arg_keys[15], (D,), jnp.float32), 0.25, 1.75),
        "second_shift": scatter_about(arg_keys[16], (D,), 0.5, 3.0, (), jnp.float32),
        "third_gain": jnp.clip(1.0 + 0.15 * jax.random.normal(arg_keys[17], (D,), jnp.float32), 0.25, 1.75),
        "third_shift": scatter_about(arg_keys[18], (D,), 0.5, 3.0, (), jnp.float32),
        "cotangent": scatter_about(arg_keys[19], (CAPTIONS, LEN, D), 1.0, 6.0, ((0, 16), (1, 2))),
    }


epsilon = 1e-05
masked_score = -1000000000.0
precise = lax.Precision.HIGHEST

@jax.custom_vjp
def low(v):
    return lax.optimization_barrier(v.astype(jnp.bfloat16)).astype(jnp.float32)

@jax.custom_vjp
def low_back(v):
    return v

def low_keep(v):
    return (low(v), None)

def low_pass(kept, grad):
    return (grad,)

def back_keep(v):
    return (v, None)

def back_low(kept, grad):
    return (low(grad),)
low.defvjp(low_keep, low_pass)
low_back.defvjp(back_keep, back_low)

def layer_norm(value, gain, shift):
    average = lax.optimization_barrier(jnp.mean(value, axis=-1, keepdims=True))
    centred = value - average
    spread = lax.optimization_barrier(jnp.mean(centred * centred, axis=-1, keepdims=True))
    return centred * lax.rsqrt(spread + epsilon) * gain + shift

def project(left, right):
    return jnp.einsum('...d,de->...e', left, right, precision=precise)

def attend(queries, key_rows, value_rows, allowed):
    captions, length, width = queries.shape
    heads = width // HD
    query_heads = queries.reshape(captions, length, heads, HD)
    key_heads = key_rows.reshape(captions, key_rows.shape[1], heads, HD)
    value_heads = value_rows.reshape(captions, value_rows.shape[1], heads, HD)
    scores = low_back(jnp.einsum('clhd,ckhd->chlk', query_heads, key_heads, precision=precise) * HD ** (-0.5))
    scores = jnp.where(allowed, scores, masked_score)
    attn_prob = low(jax.nn.softmax(scores, axis=-1))
    mixture = jnp.einsum('chlk,ckhd->clhd', attn_prob, value_heads, precision=precise)
    return low_back(low(mixture.reshape(captions, length, width)))

def block_forward(params, stream, patches, flags_block):
    query_self, key_self, value_self, mix_self, query_cross, key_cross, value_cross, mix_cross, expand, contract, first_gain, first_shift, second_gain, second_shift, third_gain, third_shift = params
    causal = (jnp.arange(LEN)[:, None] >= jnp.arange(LEN)[None, :])[None, None]
    valid_count = SMALLP + (PATCH - SMALLP) * flags_block
    visible = (jnp.arange(PATCH)[None, :] < valid_count[:, None])[:, None, None, :]
    normed = low(layer_norm(stream, first_gain, first_shift))
    queries = low_back(low(project(normed, query_self)))
    key_rows = low_back(low(project(normed, key_self)))
    value_rows = low_back(low(project(normed, value_self)))
    mixture = attend(queries, key_rows, value_rows, causal)
    stream = stream + low_back(project(mixture, mix_self))
    normed = low(layer_norm(stream, second_gain, second_shift))
    queries = low_back(low(project(normed, query_cross)))
    key_rows = low_back(low(project(patches, key_cross)))
    value_rows = low_back(low(project(patches, value_cross)))
    mixture = attend(queries, key_rows, value_rows, visible)
    stream = stream + low_back(project(mixture, mix_cross))
    normed = low(layer_norm(stream, third_gain, third_shift))
    pre_act = low_back(project(normed, expand))
    hidden = low(jax.nn.gelu(pre_act, approximate=True))
    return stream + low_back(project(hidden, contract))

def reference(text_tokens, image_tokens, resolution, query_self, key_self, value_self, mix_self, query_cross, key_cross, value_cross, mix_cross, expand, contract, first_gain, first_shift, second_gain, second_shift, third_gain, third_shift, cotangent):
    params = tuple((argument.astype(jnp.float32) for argument in (query_self, key_self, value_self, mix_self, query_cross, key_cross, value_cross, mix_cross, expand, contract, first_gain, first_shift, second_gain, second_shift, third_gain, third_shift)))
    group = MICRO * CAPS
    blocks = text_tokens.shape[0] // group
    flag_blocks = resolution.reshape(blocks, group)

    def forward(weights, stream, patches):

        def one_block(inputs):
            return block_forward(weights, inputs[0], inputs[1], inputs[2])
        block_outs = lax.map(jax.checkpoint(one_block), (stream.reshape(blocks, group, LEN, stream.shape[-1]), patches.reshape(blocks, group, PATCH, patches.shape[-1]), flag_blocks))
        return block_outs.reshape(stream.shape)
    result, pullback = jax.vjp(forward, params, text_tokens.astype(jnp.float32), image_tokens.astype(jnp.float32))
    grad_params, text_grad, image_grad = pullback(cotangent.astype(jnp.float32))
    return (result.astype(jnp.bfloat16), text_grad, image_grad, grad_params[0], grad_params[1], grad_params[2], grad_params[3], grad_params[4], grad_params[5], grad_params[6], grad_params[7], grad_params[8], grad_params[9], grad_params[10], grad_params[11], grad_params[12], grad_params[13], grad_params[14], grad_params[15])
```

```python
import jax
import jax.numpy as jnp
from jax import lax
from jax.sharding import PartitionSpec as P

HD = 64
LEN = 64
PATCH = 576
SMALLP = 196
BOTH = ("dp", "mp")

epsilon = 1e-05
masked_score = -1000000000.0
bf16 = jnp.bfloat16
f32 = jnp.float32


def dot(left, right, left_dim, right_dim):
    return lax.dot_general(left, right, (((left_dim,), (right_dim,)), ((), ())), preferred_element_type=f32)


def matmul(left, right):
    return dot(left, right, 1, 0)


def matmul_t(left, right):
    return dot(left, right, 1, 1)


def weight_grad(left, right):
    return dot(left, right, 0, 0)


def norm_stats(value):
    average = jnp.mean(value, axis=-1, keepdims=True)
    centred = value - average
    spread = jnp.mean(centred * centred, axis=-1, keepdims=True)
    inverse = lax.rsqrt(spread + epsilon)
    return centred * inverse, inverse


def norm_back(normal, inverse, gain, grad):
    scaled = grad * gain
    mean_one = jnp.mean(scaled, axis=-1, keepdims=True)
    mean_two = jnp.mean(scaled * normal, axis=-1, keepdims=True)
    grad_value = (scaled - mean_one - normal * mean_two) * inverse
    return grad_value, jnp.sum(grad * normal, axis=0), jnp.sum(grad, axis=0)


def heads(rows, count):
    return rows.reshape(count, rows.shape[0] // count, rows.shape[1] // HD, HD)


def attend(queries, keys, values, allowed, count):
    scores = jnp.einsum("clhd,ckhd->chlk", heads(queries, count), heads(keys, count), preferred_element_type=f32) * HD ** (-0.5)
    scores = jnp.where(allowed, scores, masked_score)
    highest = jnp.max(scores, axis=-1, keepdims=True)
    exponent = jnp.exp(scores - highest)
    probs = exponent / jnp.sum(exponent, axis=-1, keepdims=True)
    mixed = jnp.einsum("chlk,ckhd->clhd", probs.astype(bf16), heads(values, count), preferred_element_type=f32)
    return mixed.reshape(queries.shape).astype(bf16), probs


def attend_back(queries, keys, values, probs, grad_mix, count):
    scale = HD ** (-0.5)
    mix_heads = heads(grad_mix, count)
    grad_prob = jnp.einsum("clhd,ckhd->chlk", mix_heads, heads(values, count), preferred_element_type=f32)
    grad_values = jnp.einsum("chlk,clhd->ckhd", probs.astype(bf16), mix_heads, preferred_element_type=f32)
    inner = jnp.sum(probs * grad_prob, axis=-1, keepdims=True)
    grad_score = (probs * (grad_prob - inner)).astype(bf16)
    grad_queries = jnp.einsum("chlk,ckhd->clhd", grad_score, heads(keys, count), preferred_element_type=f32) * scale
    grad_keys = jnp.einsum("chlk,clhd->ckhd", grad_score, heads(queries, count), preferred_element_type=f32) * scale
    return (
        grad_queries.reshape(queries.shape).astype(bf16),
        grad_keys.reshape(keys.shape).astype(bf16),
        grad_values.reshape(keys.shape).astype(bf16),
    )


def gelu_parts(value):
    inner = 0.7978845608028654 * (value + 0.044715 * value * value * value)
    bent = jnp.tanh(inner)
    hidden = 0.5 * value * (1.0 + bent)
    slope = 0.5 * (1.0 + bent) + 0.5 * value * (1.0 - bent * bent) * 0.7978845608028654 * (1.0 + 3 * 0.044715 * value * value)
    return hidden, slope


def layer(weights, norms, text, cotangent, patches, resolution):
    count = text.shape[0] // LEN
    query_self, key_self, value_self, mix_self, query_cross, key_cross, value_cross, mix_cross = (weights[i] for i in range(8))
    first_gain, first_shift, second_gain, second_shift, third_gain, third_shift = norms
    causal = (jnp.arange(LEN)[:, None] >= jnp.arange(LEN)[None, :])[None, None]
    valid = SMALLP + (PATCH - SMALLP) * resolution
    visible = (jnp.arange(PATCH)[None, :] < valid[:, None])[:, None, None, :]
    stream = text.astype(f32)
    normal_one, inverse_one = norm_stats(stream)
    normed_one = (normal_one * first_gain + first_shift).astype(bf16)
    queries_one = matmul(normed_one, query_self).astype(bf16)
    keys_one = matmul(normed_one, key_self).astype(bf16)
    values_one = matmul(normed_one, value_self).astype(bf16)
    mixed_one, probs_one = attend(queries_one, keys_one, values_one, causal, count)
    stream_one = stream + matmul_t(mixed_one, mix_self)
    normal_two, inverse_two = norm_stats(stream_one)
    normed_two = (normal_two * second_gain + second_shift).astype(bf16)
    queries_two = matmul(normed_two, query_cross).astype(bf16)
    keys_two = matmul(patches, key_cross).astype(bf16)
    values_two = matmul(patches, value_cross).astype(bf16)
    mixed_two, probs_two = attend(queries_two, keys_two, values_two, visible, count)
    stream_two = stream_one + matmul_t(mixed_two, mix_cross)
    normal_three, inverse_three = norm_stats(stream_two)
    normed_three = (normal_three * third_gain + third_shift).astype(bf16)
    layer_out = stream_two
    grad_normed = 0.0
    grads = [None] * 16
    chunks = (weights.shape[0] - 8) // 2
    for j in range(chunks):
        expand, contract = weights[8 + j], weights[8 + chunks + j]
        hidden, slope = gelu_parts(matmul(normed_three, expand))
        hidden = hidden.astype(bf16)
        layer_out = layer_out + matmul_t(hidden, contract)
        grads[8 + chunks + j] = weight_grad(cotangent, hidden)
        grad_pre = (slope * matmul(cotangent, contract)).astype(bf16)
        grads[8 + j] = weight_grad(normed_three, grad_pre)
        grad_normed = grad_normed + matmul_t(grad_pre, expand)
    grad_input, gain_three, shift_three = norm_back(normal_three, inverse_three, third_gain, grad_normed)
    grad_stream = cotangent.astype(f32) + grad_input
    grad_rows = grad_stream.astype(bf16)
    grads[7] = weight_grad(grad_rows, mixed_two)
    grad_mixed = matmul(grad_rows, mix_cross).astype(bf16)
    grad_queries, grad_keys, grad_values = attend_back(queries_two, keys_two, values_two, probs_two, grad_mixed, count)
    grads[4] = weight_grad(normed_two, grad_queries)
    grads[5] = weight_grad(patches, grad_keys)
    grads[6] = weight_grad(patches, grad_values)
    patch_grad = (matmul_t(grad_keys, key_cross) + matmul_t(grad_values, value_cross)).astype(bf16)
    grad_normed = matmul_t(grad_queries, query_cross)
    grad_input, gain_two, shift_two = norm_back(normal_two, inverse_two, second_gain, grad_normed)
    grad_stream = grad_stream + grad_input
    grad_rows = grad_stream.astype(bf16)
    grads[3] = weight_grad(grad_rows, mixed_one)
    grad_mixed = matmul(grad_rows, mix_self).astype(bf16)
    grad_queries, grad_keys, grad_values = attend_back(queries_one, keys_one, values_one, probs_one, grad_mixed, count)
    grads[0] = weight_grad(normed_one, grad_queries)
    grads[1] = weight_grad(normed_one, grad_keys)
    grads[2] = weight_grad(normed_one, grad_values)
    grad_normed = matmul_t(grad_queries, query_self) + matmul_t(grad_keys, key_self) + matmul_t(grad_values, value_self)
    grad_input, gain_one, shift_one = norm_back(normal_one, inverse_one, first_gain, grad_normed)
    text_grad = (grad_stream + grad_input).astype(bf16)
    grads = jnp.stack([g.astype(bf16) for g in grads])
    norm_grads = jnp.stack([gain_one, shift_one, gain_two, shift_two, gain_three, shift_three])
    return layer_out.astype(bf16), text_grad, patch_grad, grads, norm_grads


def swap(rows):
    return lax.ppermute(rows, "mp", [(0, 1), (1, 0)])


def to_captions(rows, side):
    half = rows.shape[0] // 2
    mine = lax.dynamic_slice_in_dim(rows, side * half, half, 0)
    other = swap(lax.dynamic_slice_in_dim(rows, (1 - side) * half, half, 0))
    low = jnp.where(side == 0, mine, other)
    high = jnp.where(side == 0, other, mine)
    return jnp.concatenate([low, high], axis=1)


def to_positions(rows, side):
    length = rows.shape[1] // 2
    mine = lax.dynamic_slice_in_dim(rows, side * length, length, 1)
    other = swap(lax.dynamic_slice_in_dim(rows, (1 - side) * length, length, 1))
    low = jnp.where(side == 0, mine, other)
    high = jnp.where(side == 0, other, mine)
    return jnp.concatenate([low, high], axis=0)


def pack(shards):
    narrow = shards[0].shape[1]
    parts = []
    for shard, turned in zip(shards, TURNED):
        flat = shard.T if turned else shard
        for j in range(flat.shape[1] // narrow):
            parts.append(flat[:, j * narrow : (j + 1) * narrow])
    return jnp.stack(parts)


def unpack(packed):
    chunks = (packed.shape[0] - 8) // 2
    groups = [[packed[i]] for i in range(8)]
    groups.append([packed[8 + j] for j in range(chunks)])
    groups.append([packed[8 + chunks + j] for j in range(chunks)])
    outs = []
    for group, turned in zip(groups, TURNED):
        flat = group[0] if len(group) == 1 else jnp.concatenate(group, axis=1)
        outs.append(flat.T if turned else flat)
    return tuple(outs)


TURNED = (False, False, False, True, False, False, False, True, False, True)


def gather_weights(packed):
    full = lax.all_gather(packed, "dp", axis=1, tiled=True)
    return lax.all_gather(full, "mp", axis=2, tiled=True)


def scatter_grads(grads):
    half = lax.psum_scatter(grads, "mp", scatter_dimension=2, tiled=True)
    return lax.psum_scatter(half, "dp", scatter_dimension=1, tiled=True).astype(f32)


def body(text_tokens, image_tokens, resolution, *rest):
    shards, norms, cotangent = rest[:10], rest[10:16], rest[16]
    side = lax.axis_index("mp")
    half = text_tokens.shape[0] // 2
    width = text_tokens.shape[2]
    weights = gather_weights(pack(shards))
    text = to_captions(text_tokens, side)
    grad_out = to_captions(cotangent, side)
    patches = lax.dynamic_slice_in_dim(image_tokens, side * half, half, 0)
    flags = lax.dynamic_slice_in_dim(resolution, side * half, half, 0)
    layer_out, text_grad, patch_grad, grads, norm_grads = layer(
        weights, norms, text.reshape(-1, width), grad_out.reshape(-1, width), patches.reshape(-1, width), flags
    )
    weight_outs = unpack(scatter_grads(grads))
    norm_outs = lax.psum(norm_grads, BOTH)
    return (
        to_positions(layer_out.reshape(half, LEN, width), side),
        to_positions(text_grad.reshape(half, LEN, width), side).astype(f32),
        to_positions(patch_grad.reshape(half, PATCH, width), side).astype(f32),
        *weight_outs,
        *(norm_outs[i] for i in range(6)),
    )


def solution(mesh):
    tokens = P("dp", "mp", None)
    rows, columns = P("dp", "mp"), P("mp", "dp")
    kinds = (rows, rows, rows, columns, rows, rows, rows, columns, rows, columns)
    in_specs = (tokens, P("dp", None, None), P("dp"), *kinds, *([P()] * 6), tokens)
    out_specs = (tokens, tokens, tokens, *kinds, *([P()] * 6))
    return jax.shard_map(body, mesh=mesh, in_specs=in_specs, out_specs=out_specs, check_vma=False)
```

```python
import jax
import jax.numpy as jnp
from jax import lax
from jax.sharding import PartitionSpec as P

HD = 64
LEN = 64
PATCH = 576
SMALLP = 196
BOTH = ("dp", "mp")

epsilon = 1e-05
masked_score = -1000000000.0
bf16 = jnp.bfloat16
f32 = jnp.float32


def dot(left, right, left_dim, right_dim):
    return lax.dot_general(left, right, (((left_dim,), (right_dim,)), ((), ())), preferred_element_type=f32)


def matmul(left, right):
    return dot(left, right, 1, 0)


def matmul_t(left, right):
    return dot(left, right, 1, 1)


def weight_grad(left, right):
    return dot(left, right, 0, 0)


def norm_stats(value):
    average = jnp.mean(value, axis=-1, keepdims=True)
    centred = value - average
    spread = jnp.mean(centred * centred, axis=-1, keepdims=True)
    inverse = lax.rsqrt(spread + epsilon)
    return centred * inverse, inverse


def norm_back(normal, inverse, gain, grad):
    scaled = grad * gain
    mean_one = jnp.mean(scaled, axis=-1, keepdims=True)
    mean_two = jnp.mean(scaled * normal, axis=-1, keepdims=True)
    grad_value = (scaled - mean_one - normal * mean_two) * inverse
    return grad_value, jnp.sum(grad * normal, axis=0), jnp.sum(grad, axis=0)


def heads(rows, count):
    return rows.reshape(count, rows.shape[0] // count, rows.shape[1] // HD, HD)


def attend(queries, keys, values, allowed, count):
    scores = jnp.einsum("clhd,ckhd->chlk", heads(queries, count), heads(keys, count), preferred_element_type=f32) * HD ** (-0.5)
    scores = jnp.where(allowed, scores, masked_score)
    highest = jnp.max(scores, axis=-1, keepdims=True)
    exponent = jnp.exp(scores - highest)
    probs = exponent / jnp.sum(exponent, axis=-1, keepdims=True)
    mixed = jnp.einsum("chlk,ckhd->clhd", probs.astype(bf16), heads(values, count), preferred_element_type=f32)
    return mixed.reshape(queries.shape).astype(bf16), probs


def attend_back(queries, keys, values, probs, grad_mix, count):
    scale = HD ** (-0.5)
    mix_heads = heads(grad_mix, count)
    grad_prob = jnp.einsum("clhd,ckhd->chlk", mix_heads, heads(values, count), preferred_element_type=f32)
    grad_values = jnp.einsum("chlk,clhd->ckhd", probs.astype(bf16), mix_heads, preferred_element_type=f32)
    inner = jnp.sum(probs * grad_prob, axis=-1, keepdims=True)
    grad_score = (probs * (grad_prob - inner)).astype(bf16)
    grad_queries = jnp.einsum("chlk,ckhd->clhd", grad_score, heads(keys, count), preferred_element_type=f32) * scale
    grad_keys = jnp.einsum("chlk,clhd->ckhd", grad_score, heads(queries, count), preferred_element_type=f32) * scale
    return (
        grad_queries.reshape(queries.shape).astype(bf16),
        grad_keys.reshape(keys.shape).astype(bf16),
        grad_values.reshape(keys.shape).astype(bf16),
    )


def gelu_parts(value):
    inner = 0.7978845608028654 * (value + 0.044715 * value * value * value)
    bent = jnp.tanh(inner)
    hidden = 0.5 * value * (1.0 + bent)
    slope = 0.5 * (1.0 + bent) + 0.5 * value * (1.0 - bent * bent) * 0.7978845608028654 * (1.0 + 3 * 0.044715 * value * value)
    return hidden, slope


def layer(weights, forward, norms, text, cotangent, patches, resolution):
    count = text.shape[0] // LEN
    query_self, key_self, value_self, mix_self, query_cross, key_cross, value_cross, mix_cross = (weights[i] for i in range(8))
    first_gain, first_shift, second_gain, second_shift, third_gain, third_shift = norms
    causal = (jnp.arange(LEN)[:, None] >= jnp.arange(LEN)[None, :])[None, None]
    valid = SMALLP + (PATCH - SMALLP) * resolution
    visible = (jnp.arange(PATCH)[None, :] < valid[:, None])[:, None, None, :]
    stream = text.astype(f32)
    normal_one, inverse_one = norm_stats(stream)
    normed_one = (normal_one * first_gain + first_shift).astype(bf16)
    queries_one = matmul(normed_one, query_self).astype(bf16)
    keys_one = matmul(normed_one, key_self).astype(bf16)
    values_one = matmul(normed_one, value_self).astype(bf16)
    mixed_one, probs_one = attend(queries_one, keys_one, values_one, causal, count)
    stream_one = stream + matmul_t(mixed_one, mix_self)
    normal_two, inverse_two = norm_stats(stream_one)
    normed_two = (normal_two * second_gain + second_shift).astype(bf16)
    queries_two = matmul(normed_two, query_cross).astype(bf16)
    keys_two = matmul(patches, key_cross).astype(bf16)
    values_two = matmul(patches, value_cross).astype(bf16)
    mixed_two, probs_two = attend(queries_two, keys_two, values_two, visible, count)
    stream_two = stream_one + matmul_t(mixed_two, mix_cross)
    normal_three, inverse_three = norm_stats(stream_two)
    normed_three = (normal_three * third_gain + third_shift).astype(bf16)
    layer_out = stream_two
    grad_normed = 0.0
    grads = [None] * 16
    chunks = forward.shape[0] // 2
    for j in range(chunks):
        expand, contract = forward[j], forward[chunks + j]
        hidden, slope = gelu_parts(matmul(normed_three, expand))
        hidden = hidden.astype(bf16)
        layer_out = layer_out + matmul_t(hidden, contract)
        grads[8 + chunks + j] = weight_grad(cotangent, hidden)
        grad_pre = (slope * matmul(cotangent, contract)).astype(bf16)
        grads[8 + j] = weight_grad(normed_three, grad_pre)
        grad_normed = grad_normed + matmul_t(grad_pre, expand)
    grad_input, gain_three, shift_three = norm_back(normal_three, inverse_three, third_gain, grad_normed)
    grad_stream = cotangent.astype(f32) + grad_input
    grad_rows = grad_stream.astype(bf16)
    grads[7] = weight_grad(grad_rows, mixed_two)
    grad_mixed = matmul(grad_rows, mix_cross).astype(bf16)
    grad_queries, grad_keys, grad_values = attend_back(queries_two, keys_two, values_two, probs_two, grad_mixed, count)
    grads[4] = weight_grad(normed_two, grad_queries)
    grads[5] = weight_grad(patches, grad_keys)
    grads[6] = weight_grad(patches, grad_values)
    patch_grad = (matmul_t(grad_keys, key_cross) + matmul_t(grad_values, value_cross)).astype(bf16)
    grad_normed = matmul_t(grad_queries, query_cross)
    grad_input, gain_two, shift_two = norm_back(normal_two, inverse_two, second_gain, grad_normed)
    grad_stream = grad_stream + grad_input
    grad_rows = grad_stream.astype(bf16)
    grads[3] = weight_grad(grad_rows, mixed_one)
    grad_mixed = matmul(grad_rows, mix_self).astype(bf16)
    grad_queries, grad_keys, grad_values = attend_back(queries_one, keys_one, values_one, probs_one, grad_mixed, count)
    grads[0] = weight_grad(normed_one, grad_queries)
    grads[1] = weight_grad(normed_one, grad_keys)
    grads[2] = weight_grad(normed_one, grad_values)
    grad_normed = matmul_t(grad_queries, query_self) + matmul_t(grad_keys, key_self) + matmul_t(grad_values, value_self)
    grad_input, gain_one, shift_one = norm_back(normal_one, inverse_one, first_gain, grad_normed)
    text_grad = (grad_stream + grad_input).astype(bf16)
    grads = [jnp.stack([g.astype(bf16) for g in part]) for part in (grads[:8], grads[8:])]
    norm_grads = jnp.stack([gain_one, shift_one, gain_two, shift_two, gain_three, shift_three])
    return layer_out.astype(bf16), text_grad, patch_grad, grads, norm_grads


def swap(rows):
    return lax.ppermute(rows, "mp", [(0, 1), (1, 0)])


def to_captions(rows, side):
    half = rows.shape[0] // 2
    mine = lax.dynamic_slice_in_dim(rows, side * half, half, 0)
    other = swap(lax.dynamic_slice_in_dim(rows, (1 - side) * half, half, 0))
    low = jnp.where(side == 0, mine, other)
    high = jnp.where(side == 0, other, mine)
    return jnp.concatenate([low, high], axis=1)


def to_positions(rows, side):
    length = rows.shape[1] // 2
    mine = lax.dynamic_slice_in_dim(rows, side * length, length, 1)
    other = swap(lax.dynamic_slice_in_dim(rows, (1 - side) * length, length, 1))
    low = jnp.where(side == 0, mine, other)
    high = jnp.where(side == 0, other, mine)
    return jnp.concatenate([low, high], axis=0)


def pack(shards):
    narrow = shards[0].shape[1]
    parts = []
    for shard, turned in zip(shards, TURNED):
        flat = shard.T if turned else shard
        for j in range(flat.shape[1] // narrow):
            parts.append(flat[:, j * narrow : (j + 1) * narrow])
    return jnp.stack(parts)


def unpack(packed):
    chunks = (packed.shape[0] - 8) // 2
    groups = [[packed[i]] for i in range(8)]
    groups.append([packed[8 + j] for j in range(chunks)])
    groups.append([packed[8 + chunks + j] for j in range(chunks)])
    outs = []
    for group, turned in zip(groups, TURNED):
        flat = group[0] if len(group) == 1 else jnp.concatenate(group, axis=1)
        outs.append(flat.T if turned else flat)
    return tuple(outs)


TURNED = (False, False, False, True, False, False, False, True, False, True)


def gather_weights(packed):
    full = lax.all_gather(packed, ("mp", "dp"), axis=1, tiled=True)
    count, rows, width = full.shape
    sides = full.reshape(count, 2, rows // 2, width)
    return jnp.concatenate([sides[:, 0], sides[:, 1]], axis=2)


def scatter_grads(grads):
    width = grads.shape[2] // 2
    sides = jnp.concatenate([grads[:, :, :width], grads[:, :, width:]], axis=1)
    return lax.psum_scatter(sides, ("mp", "dp"), scatter_dimension=1, tiled=True).astype(f32)


def body(text_tokens, image_tokens, resolution, *rest):
    shards, norms, cotangent = rest[:10], rest[10:16], rest[16]
    side = lax.axis_index("mp")
    half = text_tokens.shape[0] // 2
    width = text_tokens.shape[2]
    packed = pack(shards)
    attention = gather_weights(packed[:8])
    forward = gather_weights(packed[8:])
    text = to_captions(text_tokens, side)
    grad_out = to_captions(cotangent, side)
    patches = lax.dynamic_slice_in_dim(image_tokens, side * half, half, 0)
    flags = lax.dynamic_slice_in_dim(resolution, side * half, half, 0)
    layer_out, text_grad, patch_grad, grads, norm_grads = layer(
        attention, forward, norms, text.reshape(-1, width), grad_out.reshape(-1, width), patches.reshape(-1, width), flags
    )
    weight_outs = unpack(jnp.concatenate([scatter_grads(part) for part in grads]))
    norm_outs = lax.psum(norm_grads, BOTH)
    return (
        to_positions(layer_out.reshape(half, LEN, width), side),
        to_positions(text_grad.reshape(half, LEN, width), side).astype(f32),
        to_positions(patch_grad.reshape(half, PATCH, width), side).astype(f32),
        *weight_outs,
        *(norm_outs[i] for i in range(6)),
    )


def solution(mesh):
    tokens = P("dp", "mp", None)
    rows, columns = P("dp", "mp"), P("mp", "dp")
    kinds = (rows, rows, rows, columns, rows, rows, rows, columns, rows, columns)
    in_specs = (tokens, P("dp", None, None), P("dp"), *kinds, *([P()] * 6), tokens)
    out_specs = (tokens, tokens, tokens, *kinds, *([P()] * 6))
    return jax.shard_map(body, mesh=mesh, in_specs=in_specs, out_specs=out_specs, check_vma=False)
```

```python
import functools

import jax
import jax.numpy as jnp
from jax import lax
from jax.experimental import pallas as pl
from jax.experimental.pallas import tpu as pltpu
from jax.sharding import PartitionSpec as P

HD = 64
D = 768
GROUP = 256
LEN = 64
PATCH = 576
SMALLP = 196
BOTH = ("dp", "mp")

epsilon = 1e-05
masked_score = -1000000000.0
bf16 = jnp.bfloat16
f32 = jnp.float32


def dot(left, right, left_dim, right_dim):
    return lax.dot_general(left, right, (((left_dim,), (right_dim,)), ((), ())), preferred_element_type=f32)


def matmul(left, right):
    return dot(left, right, 1, 0)


def matmul_t(left, right):
    return dot(left, right, 1, 1)


def weight_grad(left, right):
    return dot(left, right, 0, 0)


def norm_stats(value):
    average = jnp.mean(value, axis=-1, keepdims=True)
    centred = value - average
    spread = jnp.mean(centred * centred, axis=-1, keepdims=True)
    inverse = lax.rsqrt(spread + epsilon)
    return centred * inverse, inverse


def norm_back(normal, inverse, gain, grad):
    scaled = grad * gain
    mean_one = jnp.mean(scaled, axis=-1, keepdims=True)
    mean_two = jnp.mean(scaled * normal, axis=-1, keepdims=True)
    grad_value = (scaled - mean_one - normal * mean_two) * inverse
    return grad_value, jnp.sum(grad * normal, axis=0), jnp.sum(grad, axis=0)


def spread(rows):
    head = lax.broadcasted_iota(jnp.int32, rows.shape, 1) // HD
    zero = jnp.zeros_like(rows)
    return jnp.concatenate([jnp.where(head == h, rows, zero) for h in range(rows.shape[1] // HD)], axis=0)


def collect(blocks):
    count = blocks.shape[1] // HD
    length = blocks.shape[0] // count
    head = lax.broadcasted_iota(jnp.int32, (length, blocks.shape[1]), 1) // HD
    total = blocks[:length]
    for h in range(1, count):
        total = jnp.where(head == h, blocks[h * length : (h + 1) * length], total)
    return total


def groups(width):
    return [slice(start, start + GROUP) for start in range(0, width, GROUP)]


def attend_kernel(causal, flag_ref, query_ref, key_ref, value_ref, mix_ref, prob_ref):
    keys = key_ref.shape[0]
    shape = (keys, GROUP // HD * LEN)
    row = lax.broadcasted_iota(jnp.int32, shape, 0)
    if causal:
        allowed = row <= lax.broadcasted_iota(jnp.int32, shape, 1) % LEN
    else:
        allowed = row < SMALLP + (PATCH - SMALLP) * flag_ref[pl.program_id(0)]
    for part in groups(query_ref.shape[1]):
        queries = spread(query_ref[:, part]) * jnp.asarray(HD ** (-0.5), bf16)
        scores = jnp.where(allowed, dot(key_ref[:, part], queries, 1, 1), masked_score)
        exponent = jnp.exp(scores - jnp.max(scores, axis=0, keepdims=True))
        probs = (exponent * (1.0 / jnp.sum(exponent, axis=0, keepdims=True))).astype(bf16)
        prob_ref[:, part] = probs
        mix_ref[:, part] = collect(dot(probs, value_ref[:, part], 0, 0)).astype(bf16)


def attend_back_kernel(query_ref, key_ref, value_ref, prob_ref, grad_ref, *outs):
    width = query_ref.shape[1]
    joined = outs[-1]
    query_out, shift = (outs[0], 0) if len(outs) == 2 else (joined, width)
    for part in groups(width):
        queries = spread(query_ref[:, part]) * jnp.asarray(HD ** (-0.5), bf16)
        grads = spread(grad_ref[:, part])
        probs_low = prob_ref[:, part]
        probs = probs_low.astype(f32)
        grad_prob = dot(value_ref[:, part], grads, 1, 1)
        inner = jnp.sum(probs * grad_prob, axis=0, keepdims=True)
        grad_score = (probs * (grad_prob - inner)).astype(bf16)
        key_part = slice(shift + part.start, shift + part.stop)
        value_part = slice(shift + width + part.start, shift + width + part.stop)
        joined[:, value_part] = dot(probs_low, grads, 1, 0).astype(bf16)
        joined[:, key_part] = dot(grad_score, queries, 1, 0).astype(bf16)
        query_out[:, part] = (collect(dot(grad_score, key_ref[:, part], 0, 0)) * HD ** (-0.5)).astype(bf16)


def column(rows, width, index):
    return pl.BlockSpec((rows, width), lambda i: (i, index))


def attend_cost(queries, count, keys, products):
    flops = 2 * products * queries.shape[0] * keys * queries.shape[1] * GROUP // HD
    return pl.CostEstimate(flops=flops, bytes_accessed=products * 2 * count * keys * queries.shape[1], transcendentals=0)


def attend(queries, query_at, sources, key_at, value_at, flags, count, causal):
    keys = sources.shape[0] // count
    width = D
    grid_spec = pltpu.PrefetchScalarGridSpec(
        num_scalar_prefetch=1,
        grid=(count,),
        in_specs=[
            pl.BlockSpec((LEN, width), lambda i, flag: (i, query_at)),
            pl.BlockSpec((keys, width), lambda i, flag: (i, key_at)),
            pl.BlockSpec((keys, width), lambda i, flag: (i, value_at)),
        ],
        out_specs=[
            pl.BlockSpec((LEN, width), lambda i, flag: (i, 0)),
            pl.BlockSpec((keys, width), lambda i, flag: (i, 0)),
        ],
    )
    return pl.pallas_call(
        functools.partial(attend_kernel, causal),
        grid_spec=grid_spec,
        out_shape=(
            jax.ShapeDtypeStruct((count * LEN, width), bf16),
            jax.ShapeDtypeStruct((count * keys, width), bf16),
        ),
        cost_estimate=attend_cost(queries, count, keys, 2),
    )(flags, queries, sources, sources)


def attend_back(queries, query_at, sources, key_at, value_at, probs, grad_mix, count, whole):
    keys = sources.shape[0] // count
    width = D
    widths = [(keys, 3 * width)] if whole else [(LEN, width), (keys, 2 * width)]
    return pl.pallas_call(
        attend_back_kernel,
        grid=(count,),
        in_specs=[
            column(LEN, width, query_at),
            column(keys, width, key_at),
            column(keys, width, value_at),
            column(keys, width, 0),
            column(LEN, width, 0),
        ],
        out_specs=[column(rows, wide, 0) for rows, wide in widths],
        out_shape=[jax.ShapeDtypeStruct((count * rows, wide), bf16) for rows, wide in widths],
        cost_estimate=attend_cost(queries, count, keys, 4),
    )(queries, sources, sources, probs, grad_mix)


def gelu_parts(value):
    inner = 0.7978845608028654 * (value + 0.044715 * value * value * value)
    bent = jnp.tanh(inner)
    hidden = 0.5 * value * (1.0 + bent)
    slope = 0.5 * (1.0 + bent) + 0.5 * value * (1.0 - bent * bent) * 0.7978845608028654 * (1.0 + 3 * 0.044715 * value * value)
    return hidden, slope


def layer(weights, norms, text, cotangent, patches, resolution):
    count = text.shape[0] // LEN
    project_self, mix_self, query_cross, project_patch, mix_cross, expand, contract = weights
    first_gain, first_shift, second_gain, second_shift, third_gain, third_shift = norms
    stream = text.astype(f32)
    normal_one, inverse_one = norm_stats(stream)
    normed_one = (normal_one * first_gain + first_shift).astype(bf16)
    rows_one = matmul(normed_one, project_self).astype(bf16)
    mixed_one, probs_one = attend(rows_one, 0, rows_one, 1, 2, resolution, count, True)
    stream_one = stream + matmul_t(mixed_one, mix_self)
    normal_two, inverse_two = norm_stats(stream_one)
    normed_two = (normal_two * second_gain + second_shift).astype(bf16)
    queries_two = matmul(normed_two, query_cross).astype(bf16)
    rows_two = matmul(patches, project_patch).astype(bf16)
    mixed_two, probs_two = attend(queries_two, 0, rows_two, 0, 1, resolution, count, False)
    stream_two = stream_one + matmul_t(mixed_two, mix_cross)
    normal_three, inverse_three = norm_stats(stream_two)
    normed_three = (normal_three * third_gain + third_shift).astype(bf16)
    hidden, slope = gelu_parts(matmul(normed_three, expand))
    hidden = hidden.astype(bf16)
    layer_out = stream_two + matmul_t(hidden, contract)
    grad_pre = (slope * matmul(cotangent, contract)).astype(bf16)
    forward_grads = scatter_grads([weight_grad(normed_three, grad_pre), weight_grad(cotangent, hidden)])
    grad_normed = matmul_t(grad_pre, expand)
    grad_input, gain_three, shift_three = norm_back(normal_three, inverse_three, third_gain, grad_normed)
    grad_stream = cotangent.astype(f32) + grad_input
    grad_rows = grad_stream.astype(bf16)
    grad_mix_cross = weight_grad(grad_rows, mixed_two)
    grad_mixed = matmul(grad_rows, mix_cross).astype(bf16)
    grad_queries, grad_sources = attend_back(queries_two, 0, rows_two, 0, 1, probs_two, grad_mixed, count, False)
    patch_grad = matmul_t(grad_sources, project_patch).astype(bf16)
    grad_query_cross = weight_grad(normed_two, grad_queries)
    grad_patch = weight_grad(patches, grad_sources)
    grad_normed = matmul_t(grad_queries, query_cross)
    grad_input, gain_two, shift_two = norm_back(normal_two, inverse_two, second_gain, grad_normed)
    grad_stream = grad_stream + grad_input
    grad_rows = grad_stream.astype(bf16)
    grad_mix_self = weight_grad(grad_rows, mixed_one)
    grad_mixed = matmul(grad_rows, mix_self).astype(bf16)
    (grad_one,) = attend_back(rows_one, 0, rows_one, 1, 2, probs_one, grad_mixed, count, True)
    grad_self = weight_grad(normed_one, grad_one)
    grad_normed = matmul_t(grad_one, project_self)
    grad_input, gain_one, shift_one = norm_back(normal_one, inverse_one, first_gain, grad_normed)
    text_grad = (grad_stream + grad_input).astype(bf16)
    norm_grads = jnp.stack([gain_one, shift_one, gain_two, shift_two, gain_three, shift_three])
    attention_grads = [grad_self, grad_mix_self, grad_query_cross, grad_patch, grad_mix_cross]
    return layer_out.astype(bf16), text_grad, patch_grad, attention_grads, forward_grads, norm_grads


def swap(rows):
    return lax.ppermute(rows, "mp", [(0, 1), (1, 0)])


def to_captions(rows, side):
    half = rows.shape[0] // 2
    mine = lax.dynamic_slice_in_dim(rows, side * half, half, 0)
    other = swap(lax.dynamic_slice_in_dim(rows, (1 - side) * half, half, 0))
    low = jnp.where(side == 0, mine, other)
    high = jnp.where(side == 0, other, mine)
    return jnp.concatenate([low, high], axis=1)


def to_positions(rows, side):
    length = rows.shape[1] // 2
    mine = lax.dynamic_slice_in_dim(rows, side * length, length, 1)
    other = swap(lax.dynamic_slice_in_dim(rows, (1 - side) * length, length, 1))
    low = jnp.where(side == 0, mine, other)
    high = jnp.where(side == 0, other, mine)
    return jnp.concatenate([low, high], axis=0)


def pack(shards):
    narrow = shards[0].shape[1]
    parts = []
    for shard, turned in zip(shards, TURNED):
        flat = shard.T if turned else shard
        for j in range(flat.shape[1] // narrow):
            parts.append(flat[:, j * narrow : (j + 1) * narrow])
    return jnp.stack(parts)


def unpack(packed):
    chunks = (packed.shape[0] - 8) // 2
    groups = [[packed[i]] for i in range(8)]
    groups.append([packed[8 + j] for j in range(chunks)])
    groups.append([packed[8 + chunks + j] for j in range(chunks)])
    outs = []
    for group, turned in zip(groups, TURNED):
        flat = group[0] if len(group) == 1 else jnp.concatenate(group, axis=1)
        outs.append(flat.T if turned else flat)
    return tuple(outs)


TURNED = (False, False, False, True, False, False, False, True, False, True)


def gather_weights(packed, counts):
    full = lax.all_gather(packed, ("mp", "dp"), axis=1, tiled=True)
    outs, start = [], 0
    for count in counts:
        sides = full[start : start + count].reshape(count, 2, D, -1)
        outs.append(sides.transpose(2, 0, 1, 3).reshape(D, -1))
        start += count
    return outs


def scatter_grads(grads):
    sides = [g.astype(bf16).reshape(D, g.shape[1] // D, 2, D // 2).transpose(1, 2, 0, 3) for g in grads]
    stacked = jnp.concatenate(sides).reshape(-1, 2 * D, D // 2)
    return lax.psum_scatter(stacked, ("mp", "dp"), scatter_dimension=1, tiled=True).astype(f32)


def body(text_tokens, image_tokens, resolution, *rest):
    shards, norms, cotangent = rest[:10], rest[10:16], rest[16]
    side = lax.axis_index("mp")
    half = text_tokens.shape[0] // 2
    width = text_tokens.shape[2]
    packed = pack(shards)
    chunks = (packed.shape[0] - 8) // 2
    weights = gather_weights(packed[:8], (3, 1, 1, 2, 1)) + gather_weights(packed[8:], (chunks, chunks))
    text = to_captions(text_tokens, side)
    grad_out = to_captions(cotangent, side)
    patches = lax.dynamic_slice_in_dim(image_tokens, side * half, half, 0)
    flags = lax.dynamic_slice_in_dim(resolution, side * half, half, 0)
    layer_out, text_grad, patch_grad, attention_grads, forward_grads, norm_grads = layer(
        weights, norms, text.reshape(-1, width), grad_out.reshape(-1, width), patches.reshape(-1, width), flags
    )
    weight_outs = unpack(jnp.concatenate([scatter_grads(attention_grads), forward_grads]))
    norm_outs = lax.psum(norm_grads, BOTH)
    return (
        to_positions(layer_out.reshape(half, LEN, width), side),
        to_positions(text_grad.reshape(half, LEN, width), side).astype(f32),
        to_positions(patch_grad.reshape(half, PATCH, width), side).astype(f32),
        *weight_outs,
        *(norm_outs[i] for i in range(6)),
    )


def solution(mesh):
    tokens = P("dp", "mp", None)
    rows, columns = P("dp", "mp"), P("mp", "dp")
    kinds = (rows, rows, rows, columns, rows, rows, rows, columns, rows, columns)
    in_specs = (tokens, P("dp", None, None), P("dp"), *kinds, *([P()] * 6), tokens)
    out_specs = (tokens, tokens, tokens, *kinds, *([P()] * 6))
    return jax.shard_map(body, mesh=mesh, in_specs=in_specs, out_specs=out_specs, check_vma=False)
```

```python
import functools

import jax
import jax.numpy as jnp
from jax import lax
from jax.experimental import pallas as pl
from jax.experimental.pallas import tpu as pltpu
from jax.sharding import PartitionSpec as P

HD = 64
D = 768
GROUP = 256
LEN = 64
PATCH = 576
SMALLP = 196
BOTH = ("dp", "mp")

epsilon = 1e-05
masked_score = -1000000000.0
bf16 = jnp.bfloat16
f32 = jnp.float32


def dot(left, right, left_dim, right_dim):
    return lax.dot_general(left, right, (((left_dim,), (right_dim,)), ((), ())), preferred_element_type=f32)


def matmul(left, right):
    return dot(left, right, 1, 0)


def matmul_t(left, right):
    return dot(left, right, 1, 1)


def weight_grad(left, right):
    return dot(left, right, 0, 0)


def norm_stats(value):
    average = jnp.mean(value, axis=-1, keepdims=True)
    centred = value - average
    spread = jnp.mean(centred * centred, axis=-1, keepdims=True)
    inverse = lax.rsqrt(spread + epsilon)
    return centred * inverse, inverse


def norm_back(normal, inverse, gain, grad):
    scaled = grad * gain
    mean_one = jnp.mean(scaled, axis=-1, keepdims=True)
    mean_two = jnp.mean(scaled * normal, axis=-1, keepdims=True)
    grad_value = (scaled - mean_one - normal * mean_two) * inverse
    return grad_value, jnp.sum(grad * normal, axis=0), jnp.sum(grad, axis=0)


def spread(rows):
    head = lax.broadcasted_iota(jnp.int32, rows.shape, 1) // HD
    zero = jnp.zeros_like(rows)
    return jnp.concatenate([jnp.where(head == h, rows, zero) for h in range(rows.shape[1] // HD)], axis=0)


def collect(blocks):
    count = blocks.shape[1] // HD
    length = blocks.shape[0] // count
    head = lax.broadcasted_iota(jnp.int32, (length, blocks.shape[1]), 1) // HD
    total = blocks[:length]
    for h in range(1, count):
        total = jnp.where(head == h, blocks[h * length : (h + 1) * length], total)
    return total


def groups(width):
    return [slice(start, start + GROUP) for start in range(0, width, GROUP)]


def attend_kernel(causal, flag_ref, query_ref, key_ref, value_ref, mix_ref, prob_ref):
    keys = key_ref.shape[0]
    shape = (keys, GROUP // HD * LEN)
    row = lax.broadcasted_iota(jnp.int32, shape, 0)
    if causal:
        allowed = row <= lax.broadcasted_iota(jnp.int32, shape, 1) % LEN
    else:
        allowed = row < SMALLP + (PATCH - SMALLP) * flag_ref[pl.program_id(0)]
    for part in groups(query_ref.shape[1]):
        queries = spread(query_ref[:, part]) * jnp.asarray(HD ** (-0.5), bf16)
        scores = jnp.where(allowed, dot(key_ref[:, part], queries, 1, 1), masked_score)
        exponent = jnp.exp(scores - jnp.max(scores, axis=0, keepdims=True))
        probs = (exponent * (1.0 / jnp.sum(exponent, axis=0, keepdims=True))).astype(bf16)
        prob_ref[:, part] = probs
        mix_ref[:, part] = collect(dot(probs, value_ref[:, part], 0, 0)).astype(bf16)


def attend_back_kernel(query_ref, key_ref, value_ref, prob_ref, grad_ref, *outs):
    width = query_ref.shape[1]
    joined = outs[-1]
    query_out, shift = (outs[0], 0) if len(outs) == 2 else (joined, width)
    for part in groups(width):
        queries = spread(query_ref[:, part]) * jnp.asarray(HD ** (-0.5), bf16)
        grads = spread(grad_ref[:, part])
        probs_low = prob_ref[:, part]
        probs = probs_low.astype(f32)
        grad_prob = dot(value_ref[:, part], grads, 1, 1)
        inner = jnp.sum(probs * grad_prob, axis=0, keepdims=True)
        grad_score = (probs * (grad_prob - inner)).astype(bf16)
        key_part = slice(shift + part.start, shift + part.stop)
        value_part = slice(shift + width + part.start, shift + width + part.stop)
        joined[:, value_part] = dot(probs_low, grads, 1, 0).astype(bf16)
        joined[:, key_part] = dot(grad_score, queries, 1, 0).astype(bf16)
        query_out[:, part] = (collect(dot(grad_score, key_ref[:, part], 0, 0)) * HD ** (-0.5)).astype(bf16)


def column(rows, width, index):
    return pl.BlockSpec((rows, width), lambda i: (i, index))


def attend_cost(queries, count, keys, products):
    flops = 2 * products * queries.shape[0] * keys * queries.shape[1] * GROUP // HD
    return pl.CostEstimate(flops=flops, bytes_accessed=products * 2 * count * keys * queries.shape[1], transcendentals=0)


def attend(queries, query_at, sources, key_at, value_at, flags, count, causal):
    keys = sources.shape[0] // count
    width = D
    grid_spec = pltpu.PrefetchScalarGridSpec(
        num_scalar_prefetch=1,
        grid=(count,),
        in_specs=[
            pl.BlockSpec((LEN, width), lambda i, flag: (i, query_at)),
            pl.BlockSpec((keys, width), lambda i, flag: (i, key_at)),
            pl.BlockSpec((keys, width), lambda i, flag: (i, value_at)),
        ],
        out_specs=[
            pl.BlockSpec((LEN, width), lambda i, flag: (i, 0)),
            pl.BlockSpec((keys, width), lambda i, flag: (i, 0)),
        ],
    )
    return pl.pallas_call(
        functools.partial(attend_kernel, causal),
        grid_spec=grid_spec,
        out_shape=(
            jax.ShapeDtypeStruct((count * LEN, width), bf16),
            jax.ShapeDtypeStruct((count * keys, width), bf16),
        ),
        cost_estimate=attend_cost(queries, count, keys, 2),
    )(flags, queries, sources, sources)


def attend_back(queries, query_at, sources, key_at, value_at, probs, grad_mix, count, whole):
    keys = sources.shape[0] // count
    width = D
    widths = [(keys, 3 * width)] if whole else [(LEN, width), (keys, 2 * width)]
    return pl.pallas_call(
        attend_back_kernel,
        grid=(count,),
        in_specs=[
            column(LEN, width, query_at),
            column(keys, width, key_at),
            column(keys, width, value_at),
            column(keys, width, 0),
            column(LEN, width, 0),
        ],
        out_specs=[column(rows, wide, 0) for rows, wide in widths],
        out_shape=[jax.ShapeDtypeStruct((count * rows, wide), bf16) for rows, wide in widths],
        cost_estimate=attend_cost(queries, count, keys, 4),
    )(queries, sources, sources, probs, grad_mix)


def gelu_parts(value):
    inner = 0.7978845608028654 * (value + 0.044715 * value * value * value)
    bent = jnp.tanh(inner)
    hidden = 0.5 * value * (1.0 + bent)
    slope = 0.5 * (1.0 + bent) + 0.5 * value * (1.0 - bent * bent) * 0.7978845608028654 * (1.0 + 3 * 0.044715 * value * value)
    return hidden, slope


def layer(weights, norms, text, cotangent, patches, resolution):
    count = text.shape[0] // LEN
    project_self, mix_self, query_cross, project_patch, mix_cross, expand, contract = weights
    first_gain, first_shift, second_gain, second_shift, third_gain, third_shift = norms
    stream = text.astype(f32)
    normal_one, inverse_one = norm_stats(stream)
    normed_one = (normal_one * first_gain + first_shift).astype(bf16)
    rows_one = matmul(normed_one, project_self).astype(bf16)
    mixed_one, probs_one = attend(rows_one, 0, rows_one, 1, 2, resolution, count, True)
    stream_one = stream + matmul_t(mixed_one, mix_self)
    normal_two, inverse_two = norm_stats(stream_one)
    normed_two = (normal_two * second_gain + second_shift).astype(bf16)
    queries_two = matmul(normed_two, query_cross).astype(bf16)
    rows_two = matmul(patches, project_patch).astype(bf16)
    mixed_two, probs_two = attend(queries_two, 0, rows_two, 0, 1, resolution, count, False)
    stream_two = stream_one + matmul_t(mixed_two, mix_cross)
    normal_three, inverse_three = norm_stats(stream_two)
    normed_three = (normal_three * third_gain + third_shift).astype(bf16)
    hidden, slope = gelu_parts(matmul(normed_three, expand))
    hidden = hidden.astype(bf16)
    layer_out = stream_two + matmul_t(hidden, contract)
    grad_pre = (slope * matmul(cotangent, contract)).astype(bf16)
    forward_grads = scatter_grads([weight_grad(normed_three, grad_pre), weight_grad(cotangent, hidden)], True)
    grad_normed = matmul_t(grad_pre, expand)
    grad_input, gain_three, shift_three = norm_back(normal_three, inverse_three, third_gain, grad_normed)
    grad_stream = cotangent.astype(f32) + grad_input
    grad_rows = grad_stream.astype(bf16)
    grad_mix_cross = weight_grad(grad_rows, mixed_two)
    grad_mixed = matmul(grad_rows, mix_cross).astype(bf16)
    grad_queries, grad_sources = attend_back(queries_two, 0, rows_two, 0, 1, probs_two, grad_mixed, count, False)
    patch_grad = matmul_t(grad_sources, project_patch).astype(bf16)
    grad_query_cross = weight_grad(normed_two, grad_queries)
    grad_patch = weight_grad(patches, grad_sources)
    grad_normed = matmul_t(grad_queries, query_cross)
    grad_input, gain_two, shift_two = norm_back(normal_two, inverse_two, second_gain, grad_normed)
    grad_stream = grad_stream + grad_input
    grad_rows = grad_stream.astype(bf16)
    grad_mix_self = weight_grad(grad_rows, mixed_one)
    grad_mixed = matmul(grad_rows, mix_self).astype(bf16)
    (grad_one,) = attend_back(rows_one, 0, rows_one, 1, 2, probs_one, grad_mixed, count, True)
    grad_self = weight_grad(normed_one, grad_one)
    grad_normed = matmul_t(grad_one, project_self)
    grad_input, gain_one, shift_one = norm_back(normal_one, inverse_one, first_gain, grad_normed)
    text_grad = (grad_stream + grad_input).astype(bf16)
    norm_grads = jnp.stack([gain_one, shift_one, gain_two, shift_two, gain_three, shift_three])
    attention_grads = [grad_self, grad_mix_self, grad_query_cross, grad_patch, grad_mix_cross]
    return layer_out.astype(bf16), text_grad, patch_grad, attention_grads, forward_grads, norm_grads


def swap(rows):
    return lax.ppermute(rows, "mp", [(0, 1), (1, 0)])


def to_captions(rows, side):
    half = rows.shape[0] // 2
    mine = lax.dynamic_slice_in_dim(rows, side * half, half, 0)
    other = swap(lax.dynamic_slice_in_dim(rows, (1 - side) * half, half, 0))
    low = jnp.where(side == 0, mine, other)
    high = jnp.where(side == 0, other, mine)
    return jnp.concatenate([low, high], axis=1)


def to_positions(rows, side):
    length = rows.shape[1] // 2
    mine = lax.dynamic_slice_in_dim(rows, side * length, length, 1)
    other = swap(lax.dynamic_slice_in_dim(rows, (1 - side) * length, length, 1))
    low = jnp.where(side == 0, mine, other)
    high = jnp.where(side == 0, other, mine)
    return jnp.concatenate([low, high], axis=0)


def unpack(packed):
    chunks = (packed.shape[0] - 8) // 2
    groups = [[packed[i]] for i in range(8)]
    groups.append([packed[8 + j] for j in range(chunks)])
    groups.append([packed[8 + chunks + j] for j in range(chunks)])
    outs = []
    for group, turned in zip(groups, TURNED):
        flat = group[0] if len(group) == 1 else jnp.concatenate(group, axis=1)
        outs.append(flat.T if turned else flat)
    return tuple(outs)


TURNED = (False, False, False, True, False, False, False, True, False, True)


MESH = pl.DeviceIdType.MESH
DEPTH = 4
BUNDLE = 4


def place():
    index = lax.axis_index("dp")
    return index // 4, index // 2 % 2, index % 2, lax.axis_index("mp")


def greet(z, x, c, y):
    barrier = pltpu.get_barrier_semaphore()

    def hello(z_to, x_to, c_to, y_to):
        pl.semaphore_signal(barrier, inc=1, device_id=(z_to * 4 + x_to * 2 + c_to, y_to), device_id_type=MESH)

    hello(z, 1 - x, c, y)
    hello(z, x, 1 - c, y)
    hello(z, x, c, 1 - y)

    @pl.when(z > 0)
    def _():
        hello(z - 1, x, c, y)

    @pl.when(z < DEPTH - 1)
    def _():
        hello(z + 1, x, c, y)

    pl.semaphore_wait(barrier, 3 + jnp.where(z > 0, 1, 0) + jnp.where(z < DEPTH - 1, 1, 0))


def gather_kernel(att_in, exp_in, con_in, att, exp, con, own_sem, side_send, up_send, down_send, far_send, mate_send, recv, mate_recv):
    z, x, c, y = place()
    half, wide = att_in.shape[2], exp_in.shape[1]
    greet(z, x, c, y)

    def stream(index):
        early = index % 2 == 0
        part = index // 2

        def own():
            if early:
                return att_in.at[pl.ds(part * BUNDLE, BUNDLE)]
            return (exp_in, con_in)[part].at[...]

        def region(w, z_from, u, core):
            x_from = (x + (w if early else u)) % 2
            y_from = (y + (u if early else w)) % 2
            row = z_from * 4 + x_from * 2 + core
            if early:
                return att.at[pl.ds(part * BUNDLE, BUNDLE), row, :, pl.ds(pl.multiple_of(y_from * half, 128), half)]
            return (exp, con)[part].at[row, :, pl.ds(pl.multiple_of(y_from * wide, 128), wide)]

        if early:
            beside, far = (z * 4 + (1 - x) * 2 + c, y), (z * 4 + x * 2 + c, 1 - y)
        else:
            beside, far = (z * 4 + x * 2 + c, 1 - y), (z * 4 + (1 - x) * 2 + c, y)

        def copy(src, dst, send, receive, device):
            return pltpu.make_async_remote_copy(
                src_ref=src, dst_ref=dst, send_sem=send, recv_sem=receive, device_id=device, device_id_type=MESH
            )

        mine = z * 4 + x * 2 + c

        def to_beside():
            return copy(own(), region(0, z, 0, c), side_send.at[index], recv.at[index, 1, z, 0], beside)

        def to_up(w, z_from, src):
            return copy(src, region(w, z_from, 0, c), up_send.at[index, w, z_from], recv.at[index, w, z_from, 0], (mine + 4, y))

        def to_down(w, z_from, src):
            return copy(src, region(w, z_from, 0, c), down_send.at[index, w, z_from], recv.at[index, w, z_from, 0], (mine - 4, y))

        def to_far(w, z_from, src):
            return copy(src, region(w, z_from, 0, c), far_send.at[index, w, z_from], recv.at[index, w, z_from, 1], far)

        def to_mate(w, z_from, u, src):
            return copy(
                src,
                region(w, z_from, u, c),
                mate_send.at[index, w, z_from, u],
                mate_recv.at[index, w, z_from, u],
                (z * 4 + x * 2 + 1 - c, y),
            )

        def keep():
            return pltpu.make_async_copy(own(), region(0, z, 0, c), own_sem.at[index])

        def arrive(w, z_from, u):
            spot = region(w, z_from, u, c)
            copy(spot, spot, far_send.at[index, w, z_from], recv.at[index, w, z_from, u], far).wait_recv()

        def arrive_mate(w, z_from, u):
            spot = region(w, z_from, u, 1 - c)
            copy(spot, spot, far_send.at[index, w, z_from], mate_recv.at[index, w, z_from, u], far).wait_recv()

        def pass_on(w, z_from, src, up, down):
            @pl.when(up)
            def _():
                to_up(w, z_from, src).start()

            @pl.when(down)
            def _():
                to_down(w, z_from, src).start()

            to_far(w, z_from, src).start()
            to_mate(w, z_from, 0, src).start()

        def first():
            to_beside().start()
            pass_on(0, z, own(), z < DEPTH - 1, z > 0)
            keep().start()

        def second():
            arrive(1, z, 0)
            pass_on(1, z, region(1, z, 0, c), z < DEPTH - 1, z > 0)

        def along(w, distance):
            @pl.when(z >= distance)
            def _():
                z_from = z - distance
                arrive(w, z_from, 0)
                pass_on(w, z_from, region(w, z_from, 0, c), z < DEPTH - 1, z < 0)

            @pl.when(z + distance < DEPTH)
            def _():
                z_from = z + distance
                arrive(w, z_from, 0)
                pass_on(w, z_from, region(w, z_from, 0, c), z < 0, z > 0)

        def across(w, z_from):
            arrive(w, z_from, 1)
            to_mate(w, z_from, 1, region(w, z_from, 1, c)).start()

        def across_at(w, distance):
            if distance == 0:
                across(w, z)
                return

            @pl.when(z >= distance)
            def _():
                across(w, z - distance)

            @pl.when(z + distance < DEPTH)
            def _():
                across(w, z + distance)

        def finish():
            keep().wait()
            to_beside().wait_send()

            def each(number, _):
                w, z_from = number // DEPTH, number % DEPTH
                spot = region(w, z_from, 0, c)

                @pl.when((z < DEPTH - 1) & (z_from <= z))
                def _():
                    to_up(w, z_from, spot).wait_send()

                @pl.when((z > 0) & (z_from >= z))
                def _():
                    to_down(w, z_from, spot).wait_send()

                to_far(w, z_from, spot).wait_send()
                for u in range(2):
                    to_mate(w, z_from, u, spot).wait_send()
                    arrive_mate(w, z_from, u)
                return 0

            lax.fori_loop(0, 2 * DEPTH, each, 0)

        return first, second, along, across_at, finish

    streams = [stream(index) for index in range(4)]
    for first, _, _, _, _ in streams:
        first()
    for _, second, _, _, _ in streams:
        second()
    for distance in range(1, DEPTH + 1):
        for w in range(2):
            for _, _, along, across_at, _ in streams:
                if distance < DEPTH:
                    along(w, distance)
                across_at(w, distance - 1)
    for streamed in streams:
        streamed[4]()


def gather_near(att, exp, con):
    dp = lax.axis_size("dp")
    rows, half, wide = att.shape[1], att.shape[2], exp.shape[1]
    vmem = pl.BlockSpec(memory_space=pltpu.VMEM)
    anywhere = pl.BlockSpec(memory_space=pl.ANY)
    dma = pltpu.SemaphoreType.DMA
    return pl.pallas_call(
        gather_kernel,
        in_specs=[vmem] * 3,
        out_specs=[anywhere] * 3,
        out_shape=[
            jax.ShapeDtypeStruct((att.shape[0], dp, rows, 2 * half), bf16),
            jax.ShapeDtypeStruct((dp, rows, 2 * wide), bf16),
            jax.ShapeDtypeStruct((dp, rows, 2 * wide), bf16),
        ],
        scratch_shapes=[
            dma((4,)),
            dma((4,)),
            dma((4, 2, DEPTH)),
            dma((4, 2, DEPTH)),
            dma((4, 2, DEPTH)),
            dma((4, 2, DEPTH, 2)),
            dma((4, 2, DEPTH, 2)),
            dma((4, 2, DEPTH, 2)),
        ],
        compiler_params=pltpu.CompilerParams(collective_id=0, has_side_effects=True),
    )(att, exp, con)


def gather_weights(att, exp, con):
    count, width = att.shape[0], D
    if lax.axis_size("dp") == 4 * DEPTH:
        att, exp, con = gather_near(att, exp, con)
        att = att.reshape(count, width, -1)
        exp, con = exp.reshape(width, -1), con.reshape(width, -1)
    else:
        chunks = exp.shape[1] // att.shape[2]
        narrow = [g[:, j * att.shape[2] : (j + 1) * att.shape[2]] for g in (exp, con) for j in range(chunks)]
        sides = lax.all_gather(att, ("mp", "dp"), axis=1, tiled=True).reshape(count, 2, width, -1)
        att = sides.transpose(0, 2, 1, 3).reshape(count, width, -1)
        sides = lax.all_gather(jnp.stack(narrow), ("mp", "dp"), axis=1, tiled=True).reshape(2, chunks, 2, width, -1)
        exp, con = sides.transpose(0, 3, 2, 1, 4).reshape(2, width, -1)
    project_self = jnp.concatenate([att[0], att[1], att[2]], axis=1)
    project_patch = jnp.concatenate([att[5], att[6]], axis=1)
    return project_self, att[3], att[4], project_patch, att[7], exp, con


def scatter_grads(grads, natural):
    sides = []
    for g in grads:
        if natural:
            sides.append(g.astype(bf16).reshape(D, 2, g.shape[1] // D, D // 2).transpose(2, 1, 0, 3))
        else:
            sides.append(g.astype(bf16).reshape(D, g.shape[1] // D, 2, D // 2).transpose(1, 2, 0, 3))
    stacked = jnp.concatenate(sides).reshape(-1, 2 * D, D // 2)
    return lax.psum_scatter(stacked, ("mp", "dp"), scatter_dimension=1, tiled=True).astype(f32)


def body(text_tokens, image_tokens, resolution, *rest):
    shards, norms, cotangent = rest[:10], rest[10:16], rest[16]
    side = lax.axis_index("mp")
    half = text_tokens.shape[0] // 2
    width = text_tokens.shape[2]
    flat = [shard.T if turned else shard for shard, turned in zip(shards, TURNED)]
    weights = gather_weights(jnp.stack(flat[:8]), flat[8], flat[9])
    text = to_captions(text_tokens, side)
    grad_out = to_captions(cotangent, side)
    patches = lax.dynamic_slice_in_dim(image_tokens, side * half, half, 0)
    flags = lax.dynamic_slice_in_dim(resolution, side * half, half, 0)
    layer_out, text_grad, patch_grad, attention_grads, forward_grads, norm_grads = layer(
        weights, norms, text.reshape(-1, width), grad_out.reshape(-1, width), patches.reshape(-1, width), flags
    )
    weight_outs = unpack(jnp.concatenate([scatter_grads(attention_grads, False), forward_grads]))
    norm_outs = lax.psum(norm_grads, BOTH)
    return (
        to_positions(layer_out.reshape(half, LEN, width), side),
        to_positions(text_grad.reshape(half, LEN, width), side).astype(f32),
        to_positions(patch_grad.reshape(half, PATCH, width), side).astype(f32),
        *weight_outs,
        *(norm_outs[i] for i in range(6)),
    )


def solution(mesh):
    tokens = P("dp", "mp", None)
    rows, columns = P("dp", "mp"), P("mp", "dp")
    kinds = (rows, rows, rows, columns, rows, rows, rows, columns, rows, columns)
    in_specs = (tokens, P("dp", None, None), P("dp"), *kinds, *([P()] * 6), tokens)
    out_specs = (tokens, tokens, tokens, *kinds, *([P()] * 6))
    return jax.shard_map(body, mesh=mesh, in_specs=in_specs, out_specs=out_specs, check_vma=False)
```

```python
import functools

import jax
import jax.numpy as jnp
from jax import lax
from jax.experimental import pallas as pl
from jax.experimental.pallas import tpu as pltpu
from jax.sharding import PartitionSpec as P

HD = 64
D = 768
GROUP = 256
LEN = 64
PATCH = 576
SMALLP = 196
BOTH = ("dp", "mp")

epsilon = 1e-05
masked_score = -1000000000.0
bf16 = jnp.bfloat16
f32 = jnp.float32


def dot(left, right, left_dim, right_dim):
    return lax.dot_general(left, right, (((left_dim,), (right_dim,)), ((), ())), preferred_element_type=f32)


def matmul(left, right):
    return dot(left, right, 1, 0)


def matmul_t(left, right):
    return dot(left, right, 1, 1)


def weight_grad(left, right):
    return dot(left, right, 0, 0)


def norm_stats(value):
    average = jnp.mean(value, axis=-1, keepdims=True)
    centred = value - average
    spread = jnp.mean(centred * centred, axis=-1, keepdims=True)
    inverse = lax.rsqrt(spread + epsilon)
    return centred * inverse, inverse


def norm_back(normal, inverse, gain, grad):
    scaled = grad * gain
    mean_one = jnp.mean(scaled, axis=-1, keepdims=True)
    mean_two = jnp.mean(scaled * normal, axis=-1, keepdims=True)
    grad_value = (scaled - mean_one - normal * mean_two) * inverse
    return grad_value, jnp.sum(grad * normal, axis=0), jnp.sum(grad, axis=0)


def spread(rows):
    head = lax.broadcasted_iota(jnp.int32, rows.shape, 1) // HD
    zero = jnp.zeros_like(rows)
    return jnp.concatenate([jnp.where(head == h, rows, zero) for h in range(rows.shape[1] // HD)], axis=0)


def collect(blocks):
    count = blocks.shape[1] // HD
    length = blocks.shape[0] // count
    head = lax.broadcasted_iota(jnp.int32, (length, blocks.shape[1]), 1) // HD
    total = blocks[:length]
    for h in range(1, count):
        total = jnp.where(head == h, blocks[h * length : (h + 1) * length], total)
    return total


def groups(width):
    return [slice(start, start + GROUP) for start in range(0, width, GROUP)]


def attend_kernel(causal, flag_ref, query_ref, key_ref, value_ref, mix_ref, prob_ref):
    keys = key_ref.shape[0]
    shape = (keys, GROUP // HD * LEN)
    row = lax.broadcasted_iota(jnp.int32, shape, 0)
    if causal:
        allowed = row <= lax.broadcasted_iota(jnp.int32, shape, 1) % LEN
    else:
        allowed = row < SMALLP + (PATCH - SMALLP) * flag_ref[pl.program_id(0)]
    for part in groups(query_ref.shape[1]):
        queries = spread(query_ref[:, part]) * jnp.asarray(HD ** (-0.5), bf16)
        scores = jnp.where(allowed, dot(key_ref[:, part], queries, 1, 1), masked_score)
        exponent = jnp.exp(scores - jnp.max(scores, axis=0, keepdims=True))
        probs = (exponent * (1.0 / jnp.sum(exponent, axis=0, keepdims=True))).astype(bf16)
        prob_ref[:, part] = probs
        mix_ref[:, part] = collect(dot(probs, value_ref[:, part], 0, 0)).astype(bf16)


def attend_back_kernel(query_ref, key_ref, value_ref, prob_ref, grad_ref, *outs):
    width = query_ref.shape[1]
    joined = outs[-1]
    query_out, shift = (outs[0], 0) if len(outs) == 2 else (joined, width)
    for part in groups(width):
        queries = spread(query_ref[:, part]) * jnp.asarray(HD ** (-0.5), bf16)
        grads = spread(grad_ref[:, part])
        probs_low = prob_ref[:, part]
        probs = probs_low.astype(f32)
        grad_prob = dot(value_ref[:, part], grads, 1, 1)
        inner = jnp.sum(probs * grad_prob, axis=0, keepdims=True)
        grad_score = (probs * (grad_prob - inner)).astype(bf16)
        key_part = slice(shift + part.start, shift + part.stop)
        value_part = slice(shift + width + part.start, shift + width + part.stop)
        joined[:, value_part] = dot(probs_low, grads, 1, 0).astype(bf16)
        joined[:, key_part] = dot(grad_score, queries, 1, 0).astype(bf16)
        query_out[:, part] = (collect(dot(grad_score, key_ref[:, part], 0, 0)) * HD ** (-0.5)).astype(bf16)


def column(rows, width, index):
    return pl.BlockSpec((rows, width), lambda i: (i, index))


def attend_cost(queries, count, keys, products):
    flops = 2 * products * queries.shape[0] * keys * queries.shape[1] * GROUP // HD
    return pl.CostEstimate(flops=flops, bytes_accessed=products * 2 * count * keys * queries.shape[1], transcendentals=0)


def attend(queries, query_at, sources, key_at, value_at, flags, count, causal):
    keys = sources.shape[0] // count
    width = D
    grid_spec = pltpu.PrefetchScalarGridSpec(
        num_scalar_prefetch=1,
        grid=(count,),
        in_specs=[
            pl.BlockSpec((LEN, width), lambda i, flag: (i, query_at)),
            pl.BlockSpec((keys, width), lambda i, flag: (i, key_at)),
            pl.BlockSpec((keys, width), lambda i, flag: (i, value_at)),
        ],
        out_specs=[
            pl.BlockSpec((LEN, width), lambda i, flag: (i, 0)),
            pl.BlockSpec((keys, width), lambda i, flag: (i, 0)),
        ],
    )
    return pl.pallas_call(
        functools.partial(attend_kernel, causal),
        grid_spec=grid_spec,
        out_shape=(
            jax.ShapeDtypeStruct((count * LEN, width), bf16),
            jax.ShapeDtypeStruct((count * keys, width), bf16),
        ),
        cost_estimate=attend_cost(queries, count, keys, 2),
    )(flags, queries, sources, sources)


def attend_back(queries, query_at, sources, key_at, value_at, probs, grad_mix, count, whole):
    keys = sources.shape[0] // count
    width = D
    widths = [(keys, 3 * width)] if whole else [(LEN, width), (keys, 2 * width)]
    return pl.pallas_call(
        attend_back_kernel,
        grid=(count,),
        in_specs=[
            column(LEN, width, query_at),
            column(keys, width, key_at),
            column(keys, width, value_at),
            column(keys, width, 0),
            column(LEN, width, 0),
        ],
        out_specs=[column(rows, wide, 0) for rows, wide in widths],
        out_shape=[jax.ShapeDtypeStruct((count * rows, wide), bf16) for rows, wide in widths],
        cost_estimate=attend_cost(queries, count, keys, 4),
    )(queries, sources, sources, probs, grad_mix)


def gelu_parts(value):
    inner = 0.7978845608028654 * (value + 0.044715 * value * value * value)
    bent = jnp.tanh(inner)
    hidden = 0.5 * value * (1.0 + bent)
    slope = 0.5 * (1.0 + bent) + 0.5 * value * (1.0 - bent * bent) * 0.7978845608028654 * (1.0 + 3 * 0.044715 * value * value)
    return hidden, slope


def layer(weights, norms, text, cotangent, patches, resolution):
    count = text.shape[0] // LEN
    project_self, mix_self, query_cross, project_patch, mix_cross, expand, contract = weights
    first_gain, first_shift, second_gain, second_shift, third_gain, third_shift = norms
    stream = text.astype(f32)
    normal_one, inverse_one = norm_stats(stream)
    normed_one = (normal_one * first_gain + first_shift).astype(bf16)
    rows_one = matmul(normed_one, project_self).astype(bf16)
    mixed_one, probs_one = attend(rows_one, 0, rows_one, 1, 2, resolution, count, True)
    stream_one = stream + matmul_t(mixed_one, mix_self)
    normal_two, inverse_two = norm_stats(stream_one)
    normed_two = (normal_two * second_gain + second_shift).astype(bf16)
    queries_two = matmul(normed_two, query_cross).astype(bf16)
    rows_two = matmul(patches, project_patch).astype(bf16)
    mixed_two, probs_two = attend(queries_two, 0, rows_two, 0, 1, resolution, count, False)
    stream_two = stream_one + matmul_t(mixed_two, mix_cross)
    normal_three, inverse_three = norm_stats(stream_two)
    normed_three = (normal_three * third_gain + third_shift).astype(bf16)
    hidden, slope = gelu_parts(matmul(normed_three, expand))
    hidden = hidden.astype(bf16)
    layer_out = stream_two + matmul_t(hidden, contract)
    grad_pre = (slope * matmul(cotangent, contract)).astype(bf16)
    grad_expand = weight_grad(normed_three, grad_pre)
    grad_contract = weight_grad(cotangent, hidden)
    grad_normed = matmul_t(grad_pre, expand)
    grad_input, gain_three, shift_three = norm_back(normal_three, inverse_three, third_gain, grad_normed)
    grad_stream = cotangent.astype(f32) + grad_input
    grad_rows = grad_stream.astype(bf16)
    grad_mix_cross = weight_grad(grad_rows, mixed_two)
    grad_mixed = matmul(grad_rows, mix_cross).astype(bf16)
    grad_queries, grad_sources = attend_back(queries_two, 0, rows_two, 0, 1, probs_two, grad_mixed, count, False)
    patch_grad = matmul_t(grad_sources, project_patch).astype(bf16)
    grad_query_cross = weight_grad(normed_two, grad_queries)
    grad_patch = weight_grad(patches, grad_sources)
    grad_normed = matmul_t(grad_queries, query_cross)
    grad_input, gain_two, shift_two = norm_back(normal_two, inverse_two, second_gain, grad_normed)
    grad_stream = grad_stream + grad_input
    grad_rows = grad_stream.astype(bf16)
    grad_mix_self = weight_grad(grad_rows, mixed_one)
    grad_mixed = matmul(grad_rows, mix_self).astype(bf16)
    (grad_one,) = attend_back(rows_one, 0, rows_one, 1, 2, probs_one, grad_mixed, count, True)
    grad_self = weight_grad(normed_one, grad_one)
    grad_normed = matmul_t(grad_one, project_self)
    grad_input, gain_one, shift_one = norm_back(normal_one, inverse_one, first_gain, grad_normed)
    text_grad = (grad_stream + grad_input).astype(bf16)
    norm_grads = jnp.stack([gain_one, shift_one, gain_two, shift_two, gain_three, shift_three])
    grads = [grad_expand, grad_contract, grad_self, grad_mix_self, grad_query_cross, grad_patch, grad_mix_cross]
    return layer_out.astype(bf16), text_grad, patch_grad, [g.astype(bf16) for g in grads], norm_grads


def swap(rows):
    return lax.ppermute(rows, "mp", [(0, 1), (1, 0)])


def to_captions(rows, side):
    half = rows.shape[0] // 2
    mine = lax.dynamic_slice_in_dim(rows, side * half, half, 0)
    other = swap(lax.dynamic_slice_in_dim(rows, (1 - side) * half, half, 0))
    low = jnp.where(side == 0, mine, other)
    high = jnp.where(side == 0, other, mine)
    return jnp.concatenate([low, high], axis=1)


def to_positions(rows, side):
    length = rows.shape[1] // 2
    mine = lax.dynamic_slice_in_dim(rows, side * length, length, 1)
    other = swap(lax.dynamic_slice_in_dim(rows, (1 - side) * length, length, 1))
    low = jnp.where(side == 0, mine, other)
    high = jnp.where(side == 0, other, mine)
    return jnp.concatenate([low, high], axis=0)


TURNED = (False, False, False, True, False, False, False, True, False, True)


MESH = pl.DeviceIdType.MESH
DEPTH = 4
BUNDLE = 4


def place():
    index = lax.axis_index("dp")
    return index // 4, index // 2 % 2, index % 2, lax.axis_index("mp")


def greet(z, x, c, y):
    barrier = pltpu.get_barrier_semaphore()

    def hello(z_to, x_to, c_to, y_to):
        pl.semaphore_signal(barrier, inc=1, device_id=(z_to * 4 + x_to * 2 + c_to, y_to), device_id_type=MESH)

    hello(z, 1 - x, c, y)
    hello(z, x, 1 - c, y)
    hello(z, x, c, 1 - y)

    @pl.when(z > 0)
    def _():
        hello(z - 1, x, c, y)

    @pl.when(z < DEPTH - 1)
    def _():
        hello(z + 1, x, c, y)

    pl.semaphore_wait(barrier, 3 + jnp.where(z > 0, 1, 0) + jnp.where(z < DEPTH - 1, 1, 0))


def gather_kernel(att_in, exp_in, con_in, att, exp, con, own_sem, side_send, up_send, down_send, far_send, mate_send, recv, mate_recv):
    z, x, c, y = place()
    half, wide = att_in.shape[2], exp_in.shape[1]
    greet(z, x, c, y)

    def stream(index):
        early = index % 2 == 0
        part = index // 2

        def own():
            if early:
                return att_in.at[pl.ds(part * BUNDLE, BUNDLE)]
            return (exp_in, con_in)[part].at[...]

        def region(w, z_from, u, core):
            x_from = (x + (w if early else u)) % 2
            y_from = (y + (u if early else w)) % 2
            row = z_from * 4 + x_from * 2 + core
            if early:
                return att.at[pl.ds(part * BUNDLE, BUNDLE), row, :, pl.ds(pl.multiple_of(y_from * half, 128), half)]
            return (exp, con)[part].at[row, :, pl.ds(pl.multiple_of(y_from * wide, 128), wide)]

        if early:
            beside, far = (z * 4 + (1 - x) * 2 + c, y), (z * 4 + x * 2 + c, 1 - y)
        else:
            beside, far = (z * 4 + x * 2 + c, 1 - y), (z * 4 + (1 - x) * 2 + c, y)

        def copy(src, dst, send, receive, device):
            return pltpu.make_async_remote_copy(
                src_ref=src, dst_ref=dst, send_sem=send, recv_sem=receive, device_id=device, device_id_type=MESH
            )

        mine = z * 4 + x * 2 + c

        def to_beside():
            return copy(own(), region(0, z, 0, c), side_send.at[index], recv.at[index, 1, z, 0], beside)

        def to_up(w, z_from, src):
            return copy(src, region(w, z_from, 0, c), up_send.at[index, w, z_from], recv.at[index, w, z_from, 0], (mine + 4, y))

        def to_down(w, z_from, src):
            return copy(src, region(w, z_from, 0, c), down_send.at[index, w, z_from], recv.at[index, w, z_from, 0], (mine - 4, y))

        def to_far(w, z_from, src):
            return copy(src, region(w, z_from, 0, c), far_send.at[index, w, z_from], recv.at[index, w, z_from, 1], far)

        def to_mate(w, z_from, u, src):
            return copy(
                src,
                region(w, z_from, u, c),
                mate_send.at[index, w, z_from, u],
                mate_recv.at[index, w, z_from, u],
                (z * 4 + x * 2 + 1 - c, y),
            )

        def keep():
            return pltpu.make_async_copy(own(), region(0, z, 0, c), own_sem.at[index])

        def arrive(w, z_from, u):
            spot = region(w, z_from, u, c)
            copy(spot, spot, far_send.at[index, w, z_from], recv.at[index, w, z_from, u], far).wait_recv()

        def arrive_mate(w, z_from, u):
            spot = region(w, z_from, u, 1 - c)
            copy(spot, spot, far_send.at[index, w, z_from], mate_recv.at[index, w, z_from, u], far).wait_recv()

        def pass_on(w, z_from, src, up, down):
            @pl.when(up)
            def _():
                to_up(w, z_from, src).start()

            @pl.when(down)
            def _():
                to_down(w, z_from, src).start()

            to_far(w, z_from, src).start()
            to_mate(w, z_from, 0, src).start()

        def first():
            to_beside().start()
            pass_on(0, z, own(), z < DEPTH - 1, z > 0)
            keep().start()

        def second():
            arrive(1, z, 0)
            pass_on(1, z, region(1, z, 0, c), z < DEPTH - 1, z > 0)

        def along(w, distance):
            @pl.when(z >= distance)
            def _():
                z_from = z - distance
                arrive(w, z_from, 0)
                pass_on(w, z_from, region(w, z_from, 0, c), z < DEPTH - 1, z < 0)

            @pl.when(z + distance < DEPTH)
            def _():
                z_from = z + distance
                arrive(w, z_from, 0)
                pass_on(w, z_from, region(w, z_from, 0, c), z < 0, z > 0)

        def across(w, z_from):
            arrive(w, z_from, 1)
            to_mate(w, z_from, 1, region(w, z_from, 1, c)).start()

        def across_at(w, distance):
            if distance == 0:
                across(w, z)
                return

            @pl.when(z >= distance)
            def _():
                across(w, z - distance)

            @pl.when(z + distance < DEPTH)
            def _():
                across(w, z + distance)

        def finish():
            keep().wait()
            to_beside().wait_send()

            def each(number, _):
                w, z_from = number // DEPTH, number % DEPTH
                spot = region(w, z_from, 0, c)

                @pl.when((z < DEPTH - 1) & (z_from <= z))
                def _():
                    to_up(w, z_from, spot).wait_send()

                @pl.when((z > 0) & (z_from >= z))
                def _():
                    to_down(w, z_from, spot).wait_send()

                to_far(w, z_from, spot).wait_send()
                for u in range(2):
                    to_mate(w, z_from, u, spot).wait_send()
                    arrive_mate(w, z_from, u)
                return 0

            lax.fori_loop(0, 2 * DEPTH, each, 0)

        return first, second, along, across_at, finish

    streams = [stream(index) for index in range(4)]
    for first, _, _, _, _ in streams:
        first()
    for _, second, _, _, _ in streams:
        second()
    for distance in range(1, DEPTH + 1):
        for w in range(2):
            for _, _, along, across_at, _ in streams:
                if distance < DEPTH:
                    along(w, distance)
                across_at(w, distance - 1)
    for streamed in streams:
        streamed[4]()


def gather_near(att, exp, con):
    dp = lax.axis_size("dp")
    rows, half, wide = att.shape[1], att.shape[2], exp.shape[1]
    vmem = pl.BlockSpec(memory_space=pltpu.VMEM)
    anywhere = pl.BlockSpec(memory_space=pl.ANY)
    dma = pltpu.SemaphoreType.DMA
    return pl.pallas_call(
        gather_kernel,
        in_specs=[vmem] * 3,
        out_specs=[anywhere] * 3,
        out_shape=[
            jax.ShapeDtypeStruct((att.shape[0], dp, rows, 2 * half), bf16),
            jax.ShapeDtypeStruct((dp, rows, 2 * wide), bf16),
            jax.ShapeDtypeStruct((dp, rows, 2 * wide), bf16),
        ],
        scratch_shapes=[
            dma((4,)),
            dma((4,)),
            dma((4, 2, DEPTH)),
            dma((4, 2, DEPTH)),
            dma((4, 2, DEPTH)),
            dma((4, 2, DEPTH, 2)),
            dma((4, 2, DEPTH, 2)),
            dma((4, 2, DEPTH, 2)),
        ],
        compiler_params=pltpu.CompilerParams(collective_id=0, has_side_effects=True),
    )(att, exp, con)


def gather_weights(att, exp, con):
    count, width = att.shape[0], D
    if lax.axis_size("dp") == 4 * DEPTH:
        att, exp, con = gather_near(att, exp, con)
        att = att.reshape(count, width, -1)
        exp, con = exp.reshape(width, -1), con.reshape(width, -1)
    else:
        chunks = exp.shape[1] // att.shape[2]
        narrow = [g[:, j * att.shape[2] : (j + 1) * att.shape[2]] for g in (exp, con) for j in range(chunks)]
        sides = lax.all_gather(att, ("mp", "dp"), axis=1, tiled=True).reshape(count, 2, width, -1)
        att = sides.transpose(0, 2, 1, 3).reshape(count, width, -1)
        sides = lax.all_gather(jnp.stack(narrow), ("mp", "dp"), axis=1, tiled=True).reshape(2, chunks, 2, width, -1)
        exp, con = sides.transpose(0, 3, 2, 1, 4).reshape(2, width, -1)
    project_self = jnp.concatenate([att[0], att[1], att[2]], axis=1)
    project_patch = jnp.concatenate([att[5], att[6]], axis=1)
    return project_self, att[3], att[4], project_patch, att[7], exp, con


PIECES = 16
SIDE_LAG = 2
NORM_STEP = 2


def scatter_kernel(exp, con, own, mix_own, ask, source, mix, norms, out, norm_out, acc, other, side, low, high, last, total, norm_buf, norm_line, *sems):
    local_sem, mate_send, mate_recv, side_send, side_recv, line_send, low_recv, high_recv, last_send, last_recv, norm_send, norm_recv = sems
    z, x, c, y = place()
    half = out.shape[2]
    mine = z * 4 + x * 2 + c
    mate = (z * 4 + x * 2 + 1 - c, y)
    greet(z, x, c, y)

    def copy(src, dst, send, receive, device):
        return pltpu.make_async_remote_copy(src_ref=src, dst_ref=dst, send_sem=send, recv_sem=receive, device_id=device, device_id_type=MESH)

    early = [(ref, ref.shape[4] // 2, j * half) for ref in (exp, con) for j in range(4)]
    late = [(own, half, 0), (own, half, 2 * half), (own, half, 4 * half), (mix_own, half, 0), (ask, half, 0)]
    late += [(source, half, 0), (source, half, 2 * half), (mix, half, 0)]
    pieces = [piece for pair in zip(early, late) for piece in pair]

    for p, (ref, stride, offset) in enumerate(pieces):
        for k in range(2):
            columns = pl.ds(k * stride + offset, half)
            spot = (p, slice(None), slice(None), k) if p % 2 == 0 else (p, slice(None), k)
            copy(ref.at[:, :, 1 - c, :, columns], other.at[spot], mate_send.at[p, k], mate_recv.at[p, k], mate).start()
            pltpu.make_async_copy(ref.at[:, :, c, :, columns], acc.at[spot], local_sem.at[p, k]).start()

    def kind(p):
        odd = p % 2
        u = x * (1 - odd) + y * odd
        w = y * (1 - odd) + x * odd
        over_x = (z * 4 + (1 - x) * 2 + c, y)
        over_y = (mine, 1 - y)
        first = tuple(one * (1 - odd) + two * odd for one, two in zip(over_x, over_y))
        second = tuple(two * (1 - odd) + one * odd for one, two in zip(over_x, over_y))
        return u, w, first, second

    def to_mate(p, k):
        return copy(other.at[p, :, k], other.at[p, :, k], mate_send.at[p, k], mate_recv.at[p, k], mate)

    def to_side(p):
        u, w, first, second = kind(p)
        return copy(acc.at[p, :, 1 - u], side.at[p], side_send.at[p], side_recv.at[p], first)

    def to_low(p, unit):
        u, w, first, second = kind(p)
        return copy(acc.at[p, unit, u], low.at[p, unit], line_send.at[p, unit], low_recv.at[p, unit], (mine - 4, y))

    def to_high(p, unit):
        u, w, first, second = kind(p)
        return copy(acc.at[p, unit, u], high.at[p, unit], line_send.at[p, unit], high_recv.at[p, unit], (mine + 4, y))

    def to_last(p):
        u, w, first, second = kind(p)
        return copy(acc.at[p, z, u, 1 - w], last.at[p], last_send.at[p], last_recv.at[p], second)

    def open_piece(p):
        for k in range(2):
            pltpu.make_async_copy(other.at[p, :, k], acc.at[p, :, k], local_sem.at[p, k]).wait()
        for k in range(2):
            to_mate(p, k).wait_recv()

        def add(unit, _):
            acc[p, unit] = (acc[p, unit].astype(f32) + other[p, unit].astype(f32)).astype(bf16)
            return 0

        lax.fori_loop(0, DEPTH, add, 0)
        to_side(p).start()

    def add_side(p):
        u, w, first, second = kind(p)
        to_side(p).wait_recv()

        def add(unit, _):
            acc[p, unit, u] = (acc[p, unit, u].astype(f32) + side[p, unit].astype(f32)).astype(bf16)
            return 0

        lax.fori_loop(0, DEPTH, add, 0)

    def pass_line(p, buffer, inner, has_source, beyond, send):
        u, w, first, second = kind(p)

        def each(unit, _):
            @pl.when(has_source & (beyond(unit) | (unit == z)))
            def _():
                inner(p, unit).wait_recv()

            @pl.when(has_source & beyond(unit))
            def _():
                acc[p, unit, u] = (acc[p, unit, u].astype(f32) + buffer[p, unit].astype(f32)).astype(bf16)

            @pl.when(beyond(unit))
            def _():
                send(p, unit).start()

            return 0

        lax.fori_loop(0, DEPTH, each, 0)

    def close_line(p):
        u, w, first, second = kind(p)
        total[...] = acc[p, z, u].astype(f32)

        @pl.when(z < DEPTH - 1)
        def _():
            total[...] += low[p, z].astype(f32)

        @pl.when(z > 0)
        def _():
            total[...] += high[p, z].astype(f32)

        acc[p, z, u, 1 - w] = total[1 - w].astype(bf16)
        to_last(p).start()
        out[p] = total[w]

    def close_piece(p):
        to_last(p).wait_recv()
        out[p] += last[p].astype(f32)

    def norm_pair(step):
        device = (mate, (z * 4 + (1 - x) * 2 + c, y), (mine, 1 - y))[step]
        return copy(norm_buf.at[step], norm_buf.at[3 + step], norm_send.at[step], norm_recv.at[step], device)

    def norm_up(unit):
        return copy(norm_line.at[unit], norm_line.at[unit], norm_send.at[3 + unit], norm_recv.at[3 + unit], (mine + 4, y))

    def norm_down(unit):
        return copy(norm_line.at[unit], norm_line.at[unit], norm_send.at[3 + DEPTH + unit], norm_recv.at[3 + unit], (mine - 4, y))

    def norm_steps(t):
        @pl.when(t == 0)
        def _():
            norm_buf[0] = norms[...]
            norm_pair(0).start()

        for step in range(1, 4):

            @pl.when(t == step * NORM_STEP)
            def _():
                norm_pair(step - 1).wait_recv()
                summed = norm_buf[step - 1] + norm_buf[2 + step]
                if step < 3:
                    norm_buf[step] = summed
                    norm_pair(step).start()
                else:
                    norm_line[z] = summed

                    @pl.when(z < DEPTH - 1)
                    def _():
                        norm_up(z).start()

                    @pl.when(z > 0)
                    def _():
                        norm_down(z).start()

        for distance in range(1, DEPTH):

            @pl.when((t == (3 + distance) * NORM_STEP) & (z >= distance))
            def _():
                norm_up(z - distance).wait_recv()

                @pl.when(z < DEPTH - 1)
                def _():
                    norm_up(z - distance).start()

            @pl.when((t == (3 + distance) * NORM_STEP) & (z + distance < DEPTH))
            def _():
                norm_down(z + distance).wait_recv()

                @pl.when(z > 0)
                def _():
                    norm_down(z + distance).start()

    def at(p, work):
        @pl.when((p >= 0) & (p < PIECES))
        def _():
            work(p)

    def step(t, _):
        at(t, open_piece)
        at(t - SIDE_LAG, add_side)
        at(
            t - SIDE_LAG - (DEPTH - 1 - z),
            lambda p: pass_line(p, low, to_low, z < DEPTH - 1, lambda unit: unit < z, to_low),
        )
        at(t - SIDE_LAG - z, lambda p: pass_line(p, high, to_high, z > 0, lambda unit: unit > z, to_high))
        norm_steps(t)
        at(t - SIDE_LAG - DEPTH, close_line)
        at(t - SIDE_LAG - DEPTH - 2, close_piece)
        return 0

    lax.fori_loop(0, PIECES + SIDE_LAG + DEPTH + 2, step, 0)
    norm_out[...] = norm_line[0] + norm_line[1] + norm_line[2] + norm_line[3]

    def drain(p, _):
        for k in range(2):
            to_mate(p, k).wait_send()
        to_side(p).wait_send()

        def each(unit, _):
            @pl.when(unit != z)
            def _():
                to_low(p, unit).wait_send()

            return 0

        lax.fori_loop(0, DEPTH, each, 0)
        to_last(p).wait_send()
        return 0

    lax.fori_loop(0, PIECES, drain, 0)
    for index in range(3):
        norm_pair(index).wait_send()
    for unit in range(DEPTH):

        @pl.when((z < DEPTH - 1) & (unit <= z))
        def _():
            norm_up(unit).wait_send()

        @pl.when((z > 0) & (unit >= z))
        def _():
            norm_down(unit).wait_send()


def scatter_near(exp, con, own, mix_own, ask, source, mix, norms):
    rows, half = D // (4 * DEPTH), D // 2
    grads = [g.reshape(DEPTH, 2, 2, rows, g.shape[1]) for g in (exp, con, own, mix_own, ask, source, mix)]
    vmem = pl.BlockSpec(memory_space=pltpu.VMEM)
    anywhere = pl.BlockSpec(memory_space=pl.ANY)
    dma = pltpu.SemaphoreType.DMA
    return pl.pallas_call(
        scatter_kernel,
        in_specs=[anywhere] * 7 + [vmem],
        out_specs=[vmem] * 2,
        out_shape=[jax.ShapeDtypeStruct((PIECES, rows, half), f32), jax.ShapeDtypeStruct(norms.shape, f32)],
        scratch_shapes=[
            pltpu.VMEM((PIECES, DEPTH, 2, 2, rows, half), bf16),
            pltpu.VMEM((PIECES, DEPTH, 2, 2, rows, half), bf16),
            pltpu.VMEM((PIECES, DEPTH, 2, rows, half), bf16),
            pltpu.VMEM((PIECES, DEPTH, 2, rows, half), bf16),
            pltpu.VMEM((PIECES, DEPTH, 2, rows, half), bf16),
            pltpu.VMEM((PIECES, rows, half), bf16),
            pltpu.VMEM((2, rows, half), f32),
            pltpu.VMEM((6, *norms.shape), f32),
            pltpu.VMEM((DEPTH, *norms.shape), f32),
            dma((PIECES, 2)),
            dma((PIECES, 2)),
            dma((PIECES, 2)),
            dma((PIECES,)),
            dma((PIECES,)),
            dma((PIECES, DEPTH)),
            dma((PIECES, DEPTH)),
            dma((PIECES, DEPTH)),
            dma((PIECES,)),
            dma((PIECES,)),
            dma((3 + 2 * DEPTH,)),
            dma((3 + DEPTH,)),
        ],
        cost_estimate=pl.CostEstimate(flops=0, bytes_accessed=PIECES * D * D * 16, transcendentals=0),
        compiler_params=pltpu.CompilerParams(collective_id=1, has_side_effects=True, vmem_limit_bytes=60 * 2**20),
    )(*grads, norms)


def scatter_grads(grads, norms):
    exp, con, own, mix_own, ask, source, mix = grads
    if lax.axis_size("dp") == 4 * DEPTH:
        parts, norm_sums = scatter_near(*grads, jnp.pad(norms, ((0, 8 - norms.shape[0]), (0, 0))))
        late = [parts[2 * i + 1] for i in range(8)]
        exp, con = (jnp.concatenate([parts[2 * i] for i in part], axis=1) for part in (range(4), range(4, 8)))
        return [*late, exp, con], norm_sums
    sides = []
    for g in (own, mix_own, ask, source, mix):
        sides.append(g.reshape(D, g.shape[1] // D, 2, D // 2).transpose(1, 2, 0, 3))
    for g in (exp, con):
        sides.append(g.reshape(D, 2, g.shape[1] // D, D // 2).transpose(2, 1, 0, 3))
    stacked = jnp.concatenate(sides).reshape(-1, 2 * D, D // 2)
    parts = lax.psum_scatter(stacked, ("mp", "dp"), scatter_dimension=1, tiled=True).astype(f32)
    chunks = (parts.shape[0] - 8) // 2
    exp, con = (jnp.concatenate(list(parts[start : start + chunks]), axis=1) for start in (8, 8 + chunks))
    return [*(parts[i] for i in range(8)), exp, con], lax.psum(norms, BOTH)


def body(text_tokens, image_tokens, resolution, *rest):
    shards, norms, cotangent = rest[:10], rest[10:16], rest[16]
    side = lax.axis_index("mp")
    half = text_tokens.shape[0] // 2
    width = text_tokens.shape[2]
    flat = [shard.T if turned else shard for shard, turned in zip(shards, TURNED)]
    weights = gather_weights(jnp.stack(flat[:8]), flat[8], flat[9])
    text = to_captions(text_tokens, side)
    grad_out = to_captions(cotangent, side)
    patches = lax.dynamic_slice_in_dim(image_tokens, side * half, half, 0)
    flags = lax.dynamic_slice_in_dim(resolution, side * half, half, 0)
    layer_out, text_grad, patch_grad, grads, norm_grads = layer(
        weights, norms, text.reshape(-1, width), grad_out.reshape(-1, width), patches.reshape(-1, width), flags
    )
    weight_grads, norm_outs = scatter_grads(grads, norm_grads)
    weight_outs = [g.T if turned else g for g, turned in zip(weight_grads, TURNED)]
    return (
        to_positions(layer_out.reshape(half, LEN, width), side),
        to_positions(text_grad.reshape(half, LEN, width), side).astype(f32),
        to_positions(patch_grad.reshape(half, PATCH, width), side).astype(f32),
        *weight_outs,
        *(norm_outs[i] for i in range(6)),
    )


def solution(mesh):
    tokens = P("dp", "mp", None)
    rows, columns = P("dp", "mp"), P("mp", "dp")
    kinds = (rows, rows, rows, columns, rows, rows, rows, columns, rows, columns)
    in_specs = (tokens, P("dp", None, None), P("dp"), *kinds, *([P()] * 6), tokens)
    out_specs = (tokens, tokens, tokens, *kinds, *([P()] * 6))
    return jax.shard_map(body, mesh=mesh, in_specs=in_specs, out_specs=out_specs, check_vma=False)
```

```python
import functools

import jax
import jax.numpy as jnp
from jax import lax
from jax.experimental import pallas as pl
from jax.experimental.pallas import tpu as pltpu
from jax.sharding import PartitionSpec as P

HD = 64
D = 768
GROUP = 256
ROWS = 1152
LEN = 64
PATCH = 576
SMALLP = 196
BOTH = ("dp", "mp")

epsilon = 1e-05
masked_score = -1000000000.0
bf16 = jnp.bfloat16
f32 = jnp.float32


def dot(left, right, left_dim, right_dim):
    return lax.dot_general(left, right, (((left_dim,), (right_dim,)), ((), ())), preferred_element_type=f32)


def matmul(left, right):
    return dot(left, right, 1, 0)


def matmul_t(left, right):
    return dot(left, right, 1, 1)


def weight_grad(left, right):
    return dot(left, right, 0, 0)


def norm_stats(value):
    average = jnp.mean(value, axis=-1, keepdims=True)
    centred = value - average
    spread = jnp.mean(centred * centred, axis=-1, keepdims=True)
    inverse = lax.rsqrt(spread + epsilon)
    return centred * inverse, inverse


def norm_back(normal, inverse, gain, grad):
    scaled = grad * gain
    mean_one = jnp.mean(scaled, axis=-1, keepdims=True)
    mean_two = jnp.mean(scaled * normal, axis=-1, keepdims=True)
    grad_value = (scaled - mean_one - normal * mean_two) * inverse
    return grad_value, jnp.sum(grad * normal, axis=0), jnp.sum(grad, axis=0)


def spread(rows):
    head = lax.broadcasted_iota(jnp.int32, rows.shape, 1) // HD
    zero = jnp.zeros_like(rows)
    return jnp.concatenate([jnp.where(head == h, rows, zero) for h in range(rows.shape[1] // HD)], axis=0)


def collect(blocks):
    count = blocks.shape[1] // HD
    length = blocks.shape[0] // count
    head = lax.broadcasted_iota(jnp.int32, (length, blocks.shape[1]), 1) // HD
    total = blocks[:length]
    for h in range(1, count):
        total = jnp.where(head == h, blocks[h * length : (h + 1) * length], total)
    return total


def groups(width):
    return [slice(start, start + GROUP) for start in range(0, width, GROUP)]


def attend_kernel(causal, batch, flag_ref, query_ref, key_ref, value_ref, mix_ref, prob_ref):
    keys = key_ref.shape[0] // batch
    shape = (keys, GROUP // HD * LEN)
    row = lax.broadcasted_iota(jnp.int32, shape, 0)
    for n in range(batch):
        ask, see = slice(n * LEN, (n + 1) * LEN), slice(n * keys, (n + 1) * keys)
        if causal:
            allowed = row <= lax.broadcasted_iota(jnp.int32, shape, 1) % LEN
        else:
            allowed = row < SMALLP + (PATCH - SMALLP) * flag_ref[pl.program_id(0) * batch + n]
        for part in groups(query_ref.shape[1]):
            queries = spread(query_ref[ask, part]) * jnp.asarray(HD ** (-0.5), bf16)
            scores = jnp.where(allowed, dot(key_ref[see, part], queries, 1, 1), masked_score)
            exponent = jnp.exp(scores - jnp.max(scores, axis=0, keepdims=True))
            probs = (exponent * (1.0 / jnp.sum(exponent, axis=0, keepdims=True))).astype(bf16)
            prob_ref[see, part] = probs
            mix_ref[ask, part] = collect(dot(probs, value_ref[see, part], 0, 0)).astype(bf16)


def attend_back_kernel(batch, query_ref, key_ref, value_ref, prob_ref, grad_ref, *outs):
    width = query_ref.shape[1]
    keys = key_ref.shape[0] // batch
    joined = outs[-1]
    query_out, shift = (outs[0], 0) if len(outs) == 2 else (joined, width)
    for n in range(batch):
        ask, see = slice(n * LEN, (n + 1) * LEN), slice(n * keys, (n + 1) * keys)
        for part in groups(width):
            queries = spread(query_ref[ask, part]) * jnp.asarray(HD ** (-0.5), bf16)
            grads = spread(grad_ref[ask, part])
            probs_low = prob_ref[see, part]
            probs = probs_low.astype(f32)
            grad_prob = dot(value_ref[see, part], grads, 1, 1)
            inner = jnp.sum(probs * grad_prob, axis=0, keepdims=True)
            grad_score = (probs * (grad_prob - inner)).astype(bf16)
            key_part = slice(shift + part.start, shift + part.stop)
            value_part = slice(shift + width + part.start, shift + width + part.stop)
            joined[see, value_part] = dot(probs_low, grads, 1, 0).astype(bf16)
            joined[see, key_part] = dot(grad_score, queries, 1, 0).astype(bf16)
            query_out[ask, part] = (collect(dot(grad_score, key_ref[see, part], 0, 0)) * HD ** (-0.5)).astype(bf16)


def column(rows, width, index):
    return pl.BlockSpec((rows, width), lambda i, *_: (i, index))


def attend_cost(queries, count, keys, products):
    if keys == LEN and products == 4:
        return pl.CostEstimate(flops=2**20, bytes_accessed=2**20, transcendentals=0)
    flops = 2 * products * count * LEN * keys * D * GROUP // HD
    return pl.CostEstimate(flops=flops, bytes_accessed=products * 2 * count * keys * D, transcendentals=0)


def batch_of(count, keys):
    for batch in (8, 4, 2):
        if count % batch == 0 and batch * keys <= ROWS:
            return batch
    return 1


def attend(queries, query_at, sources, key_at, value_at, flags, count, causal):
    keys = sources.shape[0] // count
    batch = batch_of(count, keys)
    ask, see, width = batch * LEN, batch * keys, D
    grid_spec = pltpu.PrefetchScalarGridSpec(
        num_scalar_prefetch=1,
        grid=(count // batch,),
        in_specs=[column(ask, width, query_at), column(see, width, key_at), column(see, width, value_at)],
        out_specs=[column(ask, width, 0), column(see, width, 0)],
    )
    return pl.pallas_call(
        functools.partial(attend_kernel, causal, batch),
        grid_spec=grid_spec,
        out_shape=(
            jax.ShapeDtypeStruct((count * LEN, width), bf16),
            jax.ShapeDtypeStruct((count * keys, width), bf16),
        ),
        cost_estimate=attend_cost(queries, count, keys, 2),
    )(flags, queries, sources, sources)


def attend_back(queries, query_at, sources, key_at, value_at, probs, grad_mix, count, whole):
    keys = sources.shape[0] // count
    batch = batch_of(count, keys)
    ask, see, width = batch * LEN, batch * keys, D
    widths = [(keys, 3 * width)] if whole else [(LEN, width), (keys, 2 * width)]
    return pl.pallas_call(
        functools.partial(attend_back_kernel, batch),
        grid=(count // batch,),
        in_specs=[
            column(ask, width, query_at),
            column(see, width, key_at),
            column(see, width, value_at),
            column(see, width, 0),
            column(ask, width, 0),
        ],
        out_specs=[column(batch * rows, wide, 0) for rows, wide in widths],
        out_shape=[jax.ShapeDtypeStruct((count * rows, wide), bf16) for rows, wide in widths],
        cost_estimate=attend_cost(queries, count, keys, 4),
    )(queries, sources, sources, probs, grad_mix)


def swap(rows):
    return lax.ppermute(rows, "mp", [(0, 1), (1, 0)])


def patch_kernel(side_ref, grad_ref, weight_ref, out_ref):
    for n in range(grad_ref.shape[0]):
        out_ref[n] = dot(grad_ref[n], weight_ref[...], 1, 0).astype(out_ref.dtype)


def patch_product(grads, weights, first, last, half, place_at, total, kind):
    batch = 2 - (last - first) % 2
    rows = PATCH // 2
    depth, width = weights.shape
    grid_spec = pltpu.PrefetchScalarGridSpec(
        num_scalar_prefetch=1,
        grid=((last - first) // batch,),
        in_specs=[
            pl.BlockSpec((batch, rows, depth), lambda i, at: (i + first // batch, at[0], 0)),
            pl.BlockSpec((depth, width), lambda i, at: (0, 0)),
        ],
        out_specs=pl.BlockSpec((batch, rows, width), lambda i, at: (i + at[1] // batch, 0, 0)),
    )
    flops = 2**20
    return pl.pallas_call(
        patch_kernel,
        grid_spec=grid_spec,
        out_shape=jax.ShapeDtypeStruct((total, rows, width), kind),
        cost_estimate=pl.CostEstimate(flops=flops, bytes_accessed=flops // width, transcendentals=0),
    )(jnp.stack([half, place_at]), grads.reshape(-1, PATCH, depth), weights)


def widen_kernel(side_ref, early_ref, late_ref, whole_ref, out_ref):
    early = pl.program_id(0) * 2 < pl.num_programs(0)

    @pl.when(early)
    def _():
        out_ref[...] = early_ref[...].astype(f32)

    @pl.when(jnp.logical_not(early))
    def _():
        out_ref[...] = late_ref[...].astype(f32)


def widen(early, late, whole, place_at):
    count, height, width = early.shape
    grid_spec = pltpu.PrefetchScalarGridSpec(
        num_scalar_prefetch=1,
        grid=(2 * count,),
        in_specs=[
            pl.BlockSpec((1, height, width), lambda i, at: (jnp.minimum(i, count - 1), 0, 0)),
            pl.BlockSpec((1, height, width), lambda i, at: (jnp.maximum(i - count, 0), 0, 0)),
            pl.BlockSpec(memory_space=pl.ANY),
        ],
        out_specs=pl.BlockSpec((1, height, width), lambda i, at: (i + at[0], 0, 0)),
    )
    return pl.pallas_call(
        widen_kernel,
        grid_spec=grid_spec,
        out_shape=jax.ShapeDtypeStruct(whole.shape, f32),
        input_output_aliases={3: 0},
    )(place_at[None], early, late, whole)


def gelu_parts(value):
    inner = 0.7978845608028654 * (value + 0.044715 * value * value * value)
    bent = jnp.tanh(inner)
    hidden = 0.5 * value * (1.0 + bent)
    slope = 0.5 * (1.0 + bent) + 0.5 * value * (1.0 - bent * bent) * 0.7978845608028654 * (1.0 + 3 * 0.044715 * value * value)
    return hidden, slope


def layer(weights, norms, text, cotangent, patches, resolution):
    count = text.shape[0] // LEN
    project_self, mix_self, query_cross, project_patch, mix_cross, expand, contract = weights
    first_gain, first_shift, second_gain, second_shift, third_gain, third_shift = norms
    stream = text.astype(f32)
    normal_one, inverse_one = norm_stats(stream)
    normed_one = (normal_one * first_gain + first_shift).astype(bf16)
    rows_one = matmul(normed_one, project_self).astype(bf16)
    mixed_one, probs_one = attend(rows_one, 0, rows_one, 1, 2, resolution, count, True)
    stream_one = stream + matmul_t(mixed_one, mix_self)
    normal_two, inverse_two = norm_stats(stream_one)
    normed_two = (normal_two * second_gain + second_shift).astype(bf16)
    queries_two = matmul(normed_two, query_cross).astype(bf16)
    rows_two = matmul(patches, project_patch).astype(bf16)
    mixed_two, probs_two = attend(queries_two, 0, rows_two, 0, 1, resolution, count, False)
    stream_two = stream_one + matmul_t(mixed_two, mix_cross)
    normal_three, inverse_three = norm_stats(stream_two)
    normed_three = (normal_three * third_gain + third_shift).astype(bf16)
    hidden, slope = gelu_parts(matmul(normed_three, expand))
    hidden = hidden.astype(bf16)
    layer_out = stream_two + matmul_t(hidden, contract)
    grad_pre = (slope * matmul(cotangent, contract)).astype(bf16)
    grad_expand = weight_grad(normed_three, grad_pre)
    grad_contract = weight_grad(cotangent, hidden)
    grad_normed = matmul_t(grad_pre, expand)
    grad_input, gain_three, shift_three = norm_back(normal_three, inverse_three, third_gain, grad_normed)
    grad_stream = cotangent.astype(f32) + grad_input
    grad_rows = grad_stream.astype(bf16)
    grad_mix_cross = weight_grad(grad_rows, mixed_two).astype(bf16)
    grad_expand, grad_contract = grad_expand.astype(bf16), grad_contract.astype(bf16)
    grad_rows, grad_expand, grad_contract, grad_mix_cross = lax.optimization_barrier(
        (grad_rows, grad_expand, grad_contract, grad_mix_cross)
    )
    grad_mixed = matmul(grad_rows, mix_cross).astype(bf16)
    grad_queries, grad_sources = attend_back(queries_two, 0, rows_two, 0, 1, probs_two, grad_mixed, count, False)
    side = lax.axis_index("mp")
    grad_query_cross = weight_grad(normed_two, grad_queries).astype(bf16)
    grad_patch = weight_grad(patches, grad_sources).astype(bf16)
    grad_patch, grad_sources, grad_query_cross = lax.optimization_barrier((grad_patch, grad_sources, grad_query_cross))
    turned_patch = jnp.concatenate([project_patch[:, :D].T, project_patch[:, D:].T])
    early = patch_product(grad_sources, turned_patch, 0, count // 2, 1 - side, 0 * side, count // 2, bf16)
    early, grad_queries = lax.optimization_barrier((early, grad_queries))
    early = swap(early)
    late = patch_product(grad_sources, turned_patch, count // 2, count, 1 - side, 0 * side, count // 2, bf16)
    patch_grad = patch_product(grad_sources, turned_patch, 0, count, side, side * count, 2 * count, f32)
    grad_normed = matmul_t(grad_queries, query_cross)
    grad_input, gain_two, shift_two = norm_back(normal_two, inverse_two, second_gain, grad_normed)
    grad_stream = grad_stream + grad_input
    grad_rows = grad_stream.astype(bf16)
    grad_mix_self = weight_grad(grad_rows, mixed_one)
    grad_mixed = matmul(grad_rows, mix_self).astype(bf16)
    (grad_one,) = attend_back(rows_one, 0, rows_one, 1, 2, probs_one, grad_mixed, count, True)
    grad_self = weight_grad(normed_one, grad_one)
    grad_normed = matmul_t(grad_one, project_self)
    grad_input, gain_one, shift_one = norm_back(normal_one, inverse_one, first_gain, grad_normed)
    text_grad = (grad_stream + grad_input).astype(bf16)
    norm_grads = jnp.stack([gain_one, shift_one, gain_two, shift_two, gain_three, shift_three])
    grads = [grad_expand, grad_contract, grad_self, grad_mix_self, grad_query_cross, grad_patch, grad_mix_cross]
    early, norm_grads = lax.optimization_barrier((early, norm_grads))
    weight_grads, norm_sums, late = scatter_grads([g.astype(bf16) for g in grads], norm_grads, late)
    patch_grad = widen(early, late, patch_grad, (1 - side) * count)
    return layer_out.astype(bf16), text_grad, patch_grad, weight_grads, norm_sums


def to_captions(rows, side):
    half = rows.shape[0] // 2
    mine = lax.dynamic_slice_in_dim(rows, side * half, half, 0)
    other = swap(lax.dynamic_slice_in_dim(rows, (1 - side) * half, half, 0))
    low = jnp.where(side == 0, mine, other)
    high = jnp.where(side == 0, other, mine)
    return jnp.concatenate([low, high], axis=1)


def to_positions(rows, side):
    count, length, width = rows.shape[0], rows.shape[1] // 2, rows.shape[2]
    mine = lax.dynamic_slice_in_dim(rows, side * length, length, 1)
    other = swap(lax.dynamic_slice_in_dim(rows, (1 - side) * length, length, 1))
    first = (jnp.arange(2) == side).reshape(2, 1, 1, 1)
    return jnp.where(first, mine[None], other[None]).reshape(2 * count, length, width)


TURNED = (False, False, False, True, False, False, False, True, False, True)


MESH = pl.DeviceIdType.MESH
DEPTH = 4
BUNDLE = 4


def place():
    index = lax.axis_index("dp")
    return index // 4, index // 2 % 2, index % 2, lax.axis_index("mp")


def greet(z, x, c, y):
    barrier = pltpu.get_barrier_semaphore()

    def hello(z_to, x_to, c_to, y_to):
        pl.semaphore_signal(barrier, inc=1, device_id=(z_to * 4 + x_to * 2 + c_to, y_to), device_id_type=MESH)

    hello(z, 1 - x, c, y)
    hello(z, x, 1 - c, y)
    hello(z, x, c, 1 - y)

    @pl.when(z > 0)
    def _():
        hello(z - 1, x, c, y)

    @pl.when(z < DEPTH - 1)
    def _():
        hello(z + 1, x, c, y)

    pl.semaphore_wait(barrier, 3 + jnp.where(z > 0, 1, 0) + jnp.where(z < DEPTH - 1, 1, 0))


def gather_kernel(att_in, exp_in, con_in, att, exp, con, own_sem, side_send, up_send, down_send, far_send, mate_send, recv, mate_recv):
    z, x, c, y = place()
    half, wide = att_in.shape[2], exp_in.shape[1]
    greet(z, x, c, y)

    def stream(index):
        early = index % 2 == 0
        part = index // 2
        line_first = index == 2

        def own():
            if early:
                return att_in.at[pl.ds(part * BUNDLE, BUNDLE)]
            return (exp_in, con_in)[part].at[...]

        def region(w, z_from, u, core):
            x_from = (x + (w if early else u)) % 2
            y_from = (y + (u if early else w)) % 2
            row = z_from * 4 + x_from * 2 + core
            if early:
                return att.at[pl.ds(part * BUNDLE, BUNDLE), row, :, pl.ds(pl.multiple_of(y_from * half, 128), half)]
            return (exp, con)[part].at[row, :, pl.ds(pl.multiple_of(y_from * wide, 128), wide)]

        if early:
            beside, far = (z * 4 + (1 - x) * 2 + c, y), (z * 4 + x * 2 + c, 1 - y)
        else:
            beside, far = (z * 4 + x * 2 + c, 1 - y), (z * 4 + (1 - x) * 2 + c, y)

        def copy(src, dst, send, receive, device):
            return pltpu.make_async_remote_copy(
                src_ref=src, dst_ref=dst, send_sem=send, recv_sem=receive, device_id=device, device_id_type=MESH
            )

        mine = z * 4 + x * 2 + c

        def to_beside(z_from, src):
            return copy(src, region(0, z_from, 0, c), side_send.at[index, z_from], recv.at[index, 1, z_from, 0], beside)

        def to_up(w, z_from, src):
            return copy(src, region(w, z_from, 0, c), up_send.at[index, w, z_from], recv.at[index, w, z_from, 0], (mine + 4, y))

        def to_down(w, z_from, src):
            return copy(src, region(w, z_from, 0, c), down_send.at[index, w, z_from], recv.at[index, w, z_from, 0], (mine - 4, y))

        def to_far(w, z_from, src):
            return copy(src, region(w, z_from, 0, c), far_send.at[index, w, z_from], recv.at[index, w, z_from, 1], far)

        def to_mate(w, z_from, u, src):
            return copy(
                src,
                region(w, z_from, u, c),
                mate_send.at[index, w, z_from, u],
                mate_recv.at[index, w, z_from, u],
                (z * 4 + x * 2 + 1 - c, y),
            )

        def keep():
            return pltpu.make_async_copy(own(), region(0, z, 0, c), own_sem.at[index])

        def arrive(w, z_from, u):
            spot = region(w, z_from, u, c)
            copy(spot, spot, far_send.at[index, w, z_from], recv.at[index, w, z_from, u], far).wait_recv()

        def arrive_mate(w, z_from, u):
            spot = region(w, z_from, u, 1 - c)
            copy(spot, spot, far_send.at[index, w, z_from], mate_recv.at[index, w, z_from, u], far).wait_recv()

        def pass_on(w, z_from, src, up, down):
            if w == 0 or not line_first:

                @pl.when(up)
                def _():
                    to_up(w, z_from, src).start()

                @pl.when(down)
                def _():
                    to_down(w, z_from, src).start()

            if w == 0 and line_first:
                to_beside(z_from, src).start()
            to_far(w, z_from, src).start()
            to_mate(w, z_from, 0, src).start()

        def first():
            if not line_first:
                to_beside(z, own()).start()
            pass_on(0, z, own(), z < DEPTH - 1, z > 0)
            keep().start()

        def second():
            arrive(1, z, 0)
            pass_on(1, z, region(1, z, 0, c), z < DEPTH - 1, z > 0)

        def along(w, distance):
            @pl.when(z >= distance)
            def _():
                z_from = z - distance
                arrive(w, z_from, 0)
                pass_on(w, z_from, region(w, z_from, 0, c), z < DEPTH - 1, z < 0)

            @pl.when(z + distance < DEPTH)
            def _():
                z_from = z + distance
                arrive(w, z_from, 0)
                pass_on(w, z_from, region(w, z_from, 0, c), z < 0, z > 0)

        def across(w, z_from):
            arrive(w, z_from, 1)
            to_mate(w, z_from, 1, region(w, z_from, 1, c)).start()

        def across_at(w, distance):
            if distance == 0:
                across(w, z)
                return

            @pl.when(z >= distance)
            def _():
                across(w, z - distance)

            @pl.when(z + distance < DEPTH)
            def _():
                across(w, z + distance)

        def finish():
            keep().wait()
            if not line_first:
                to_beside(z, own()).wait_send()

            def each(number, _):
                w, z_from = number // DEPTH, number % DEPTH
                spot = region(w, z_from, 0, c)
                in_line = (w == 0) if line_first else (w >= 0)

                @pl.when(in_line & (z < DEPTH - 1) & (z_from <= z))
                def _():
                    to_up(w, z_from, spot).wait_send()

                @pl.when(in_line & (z > 0) & (z_from >= z))
                def _():
                    to_down(w, z_from, spot).wait_send()

                if line_first:

                    @pl.when(w == 0)
                    def _():
                        to_beside(z_from, spot).wait_send()

                to_far(w, z_from, spot).wait_send()
                for u in range(2):
                    to_mate(w, z_from, u, spot).wait_send()
                    arrive_mate(w, z_from, u)
                return 0

            lax.fori_loop(0, 2 * DEPTH, each, 0)

        return first, second, along, across_at, finish

    streams = [stream(index) for index in range(4)]
    for first, _, _, _, _ in streams:
        first()
    for _, second, _, _, _ in streams:
        second()
    for distance in range(1, DEPTH + 1):
        for w in range(2):
            for _, _, along, across_at, _ in streams:
                if distance < DEPTH:
                    along(w, distance)
                across_at(w, distance - 1)
    for streamed in streams:
        streamed[4]()


def gather_near(att, exp, con):
    dp = lax.axis_size("dp")
    rows, half, wide = att.shape[1], att.shape[2], exp.shape[1]
    vmem = pl.BlockSpec(memory_space=pltpu.VMEM)
    anywhere = pl.BlockSpec(memory_space=pl.ANY)
    dma = pltpu.SemaphoreType.DMA
    return pl.pallas_call(
        gather_kernel,
        in_specs=[vmem] * 3,
        out_specs=[anywhere] * 3,
        out_shape=[
            jax.ShapeDtypeStruct((att.shape[0], dp, rows, 2 * half), bf16),
            jax.ShapeDtypeStruct((dp, rows, 2 * wide), bf16),
            jax.ShapeDtypeStruct((dp, rows, 2 * wide), bf16),
        ],
        scratch_shapes=[
            dma((4,)),
            dma((4, DEPTH)),
            dma((4, 2, DEPTH)),
            dma((4, 2, DEPTH)),
            dma((4, 2, DEPTH)),
            dma((4, 2, DEPTH, 2)),
            dma((4, 2, DEPTH, 2)),
            dma((4, 2, DEPTH, 2)),
        ],
        compiler_params=pltpu.CompilerParams(collective_id=0, has_side_effects=True),
    )(att, exp, con)


def gather_weights(att, exp, con):
    count, width = att.shape[0], D
    if lax.axis_size("dp") == 4 * DEPTH:
        att, exp, con = gather_near(att, exp, con)
        att = att.reshape(count, width, -1)
        exp, con = exp.reshape(width, -1), con.reshape(width, -1)
    else:
        chunks = exp.shape[1] // att.shape[2]
        narrow = [g[:, j * att.shape[2] : (j + 1) * att.shape[2]] for g in (exp, con) for j in range(chunks)]
        sides = lax.all_gather(att, ("mp", "dp"), axis=1, tiled=True).reshape(count, 2, width, -1)
        att = sides.transpose(0, 2, 1, 3).reshape(count, width, -1)
        sides = lax.all_gather(jnp.stack(narrow), ("mp", "dp"), axis=1, tiled=True).reshape(2, chunks, 2, width, -1)
        exp, con = sides.transpose(0, 3, 2, 1, 4).reshape(2, width, -1)
    project_self = jnp.concatenate([att[0], att[1], att[2]], axis=1)
    project_patch = jnp.concatenate([att[5], att[6]], axis=1)
    return project_self, att[3], att[4], project_patch, att[7], exp, con


PIECES = 16
SCATTER_COST = 2**20
SIDE_LAG = 1
NORM_STEP = 2


def scatter_kernel(exp, con, own, mix_own, ask, source, mix, norms, away, out, norm_out, back, acc, other, side, low, high, last, total, norm_buf, norm_line, *sems):
    local_sem, mate_send, mate_recv, side_send, side_recv, line_send, low_recv, high_recv, last_send, last_recv, norm_send, norm_recv, away_send, back_recv = sems
    z, x, c, y = place()
    half = out.shape[2]
    mine = z * 4 + x * 2 + c
    mate = (z * 4 + x * 2 + 1 - c, y)
    greet(z, x, c, y)

    def copy(src, dst, send, receive, device):
        return pltpu.make_async_remote_copy(src_ref=src, dst_ref=dst, send_sem=send, recv_sem=receive, device_id=device, device_id_type=MESH)

    pieces = [(ref, ref.shape[4] // 2, j * half) for ref in (exp, con) for j in range(4)]
    pieces += [(own, half, 0), (own, half, 2 * half), (own, half, 4 * half), (mix_own, half, 0), (ask, half, 0)]
    pieces += [(source, half, 0), (source, half, 2 * half), (mix, half, 0)]

    over_x, over_y = pieces[: PIECES * 2 // 3 + 1], pieces[PIECES * 2 // 3 + 1 :]
    for p in range(PIECES):
        ref, stride, offset = over_y[p // 3] if p % 3 == 2 else over_x[p // 3 * 2 + p % 3]
        for k in range(2):
            columns = pl.ds(k * stride + offset, half)
            spot = (p, slice(None), k) if p % 3 == 2 else (p, slice(None), slice(None), k)
            copy(ref.at[:, :, 1 - c, :, columns], other.at[spot], mate_send.at[p, k], mate_recv.at[p, k], mate).start()
            pltpu.make_async_copy(ref.at[:, :, c, :, columns], acc.at[spot], local_sem.at[p, k]).start()

    def part(j):
        rows = away.shape[1] // 2
        spot = (j // 2, pl.ds(j % 2 * rows, rows))
        return copy(away.at[spot], back.at[spot], away_send.at[j], back_recv.at[j], (mine, 1 - y))

    def kind(p):
        odd = jnp.where(p % 3 == 2, 1, 0)
        u = x * (1 - odd) + y * odd
        w = y * (1 - odd) + x * odd
        over_x = (z * 4 + (1 - x) * 2 + c, y)
        over_y = (mine, 1 - y)
        first = tuple(one * (1 - odd) + two * odd for one, two in zip(over_x, over_y))
        second = tuple(two * (1 - odd) + one * odd for one, two in zip(over_x, over_y))
        return u, w, first, second

    def to_mate(p, k):
        return copy(other.at[p, :, k], other.at[p, :, k], mate_send.at[p, k], mate_recv.at[p, k], mate)

    def to_side(p):
        u, w, first, second = kind(p)
        return copy(acc.at[p, :, 1 - u], side.at[p], side_send.at[p], side_recv.at[p], first)

    def to_low(p, unit):
        u, w, first, second = kind(p)
        return copy(acc.at[p, unit, u], low.at[p, unit], line_send.at[p, unit], low_recv.at[p, unit], (mine - 4, y))

    def to_high(p, unit):
        u, w, first, second = kind(p)
        return copy(acc.at[p, unit, u], high.at[p, unit], line_send.at[p, unit], high_recv.at[p, unit], (mine + 4, y))

    def to_last(p):
        u, w, first, second = kind(p)
        return copy(acc.at[p, z, u, 1 - w], last.at[p], last_send.at[p], last_recv.at[p], second)

    def open_piece(p):
        for k in range(2):
            pltpu.make_async_copy(other.at[p, :, k], acc.at[p, :, k], local_sem.at[p, k]).wait()
        for k in range(2):
            to_mate(p, k).wait_recv()

        def add(unit, _):
            acc[p, unit] = (acc[p, unit].astype(f32) + other[p, unit].astype(f32)).astype(bf16)
            return 0

        lax.fori_loop(0, DEPTH, add, 0)
        to_side(p).start()

    def add_side(p):
        u, w, first, second = kind(p)
        to_side(p).wait_recv()

        def add(unit, _):
            acc[p, unit, u] = (acc[p, unit, u].astype(f32) + side[p, unit].astype(f32)).astype(bf16)
            return 0

        lax.fori_loop(0, DEPTH, add, 0)

    def pass_line(p, buffer, inner, has_source, beyond, send):
        u, w, first, second = kind(p)

        def each(unit, _):
            @pl.when(has_source & (beyond(unit) | (unit == z)))
            def _():
                inner(p, unit).wait_recv()

            @pl.when(has_source & beyond(unit))
            def _():
                acc[p, unit, u] = (acc[p, unit, u].astype(f32) + buffer[p, unit].astype(f32)).astype(bf16)

            @pl.when(beyond(unit))
            def _():
                send(p, unit).start()

            return 0

        lax.fori_loop(0, DEPTH, each, 0)

    def close_line(p):
        u, w, first, second = kind(p)
        total[...] = acc[p, z, u].astype(f32)

        @pl.when(z < DEPTH - 1)
        def _():
            total[...] += low[p, z].astype(f32)

        @pl.when(z > 0)
        def _():
            total[...] += high[p, z].astype(f32)

        acc[p, z, u, 1 - w] = total[1 - w].astype(bf16)
        to_last(p).start()
        out[p] = total[w]

    def close_piece(p):
        to_last(p).wait_recv()
        out[p] += last[p].astype(f32)

    def norm_pair(step):
        device = (mate, (z * 4 + (1 - x) * 2 + c, y), (mine, 1 - y))[step]
        return copy(norm_buf.at[step], norm_buf.at[3 + step], norm_send.at[step], norm_recv.at[step], device)

    def norm_up(unit):
        return copy(norm_line.at[unit], norm_line.at[unit], norm_send.at[3 + unit], norm_recv.at[3 + unit], (mine + 4, y))

    def norm_down(unit):
        return copy(norm_line.at[unit], norm_line.at[unit], norm_send.at[3 + DEPTH + unit], norm_recv.at[3 + unit], (mine - 4, y))

    def norm_steps(t):
        @pl.when(t == 0)
        def _():
            norm_buf[0] = norms[...]
            norm_pair(0).start()

        for step in range(1, 4):

            @pl.when(t == step * NORM_STEP)
            def _():
                norm_pair(step - 1).wait_recv()
                summed = norm_buf[step - 1] + norm_buf[2 + step]
                if step < 3:
                    norm_buf[step] = summed
                    norm_pair(step).start()
                else:
                    norm_line[z] = summed

                    @pl.when(z < DEPTH - 1)
                    def _():
                        norm_up(z).start()

                    @pl.when(z > 0)
                    def _():
                        norm_down(z).start()

        for distance in range(1, DEPTH):

            @pl.when((t == (3 + distance) * NORM_STEP) & (z >= distance))
            def _():
                norm_up(z - distance).wait_recv()

                @pl.when(z < DEPTH - 1)
                def _():
                    norm_up(z - distance).start()

            @pl.when((t == (3 + distance) * NORM_STEP) & (z + distance < DEPTH))
            def _():
                norm_down(z + distance).wait_recv()

                @pl.when(z > 0)
                def _():
                    norm_down(z + distance).start()

    def at(p, work):
        @pl.when((p >= 0) & (p < PIECES))
        def _():
            work(p)

    def step(t, _):
        at(2 * t, open_piece)
        at(2 * t + 1, open_piece)
        for j in range(2 * away.shape[0]):

            @pl.when(t == 1 + PIECES * j // (2 * away.shape[0]))
            def _():
                part(j).start()

        at(t - SIDE_LAG, add_side)
        at(
            t - SIDE_LAG - (DEPTH - 1 - z),
            lambda p: pass_line(p, low, to_low, z < DEPTH - 1, lambda unit: unit < z, to_low),
        )
        at(t - SIDE_LAG - z, lambda p: pass_line(p, high, to_high, z > 0, lambda unit: unit > z, to_high))
        norm_steps(t)
        at(t - SIDE_LAG - DEPTH, close_line)
        return 0

    def close(p, _):
        close_piece(p)
        return 0

    lax.fori_loop(0, PIECES + SIDE_LAG + DEPTH, step, 0)
    lax.fori_loop(0, PIECES, close, 0)
    for j in range(2 * away.shape[0]):
        part(j).wait()
    norm_out[...] = norm_line[0] + norm_line[1] + norm_line[2] + norm_line[3]

    def drain(p, _):
        for k in range(2):
            to_mate(p, k).wait_send()
        to_side(p).wait_send()

        def each(unit, _):
            @pl.when(unit != z)
            def _():
                to_low(p, unit).wait_send()

            return 0

        lax.fori_loop(0, DEPTH, each, 0)
        to_last(p).wait_send()
        return 0

    lax.fori_loop(0, PIECES, drain, 0)
    for index in range(3):
        norm_pair(index).wait_send()
    for unit in range(DEPTH):

        @pl.when((z < DEPTH - 1) & (unit <= z))
        def _():
            norm_up(unit).wait_send()

        @pl.when((z > 0) & (unit >= z))
        def _():
            norm_down(unit).wait_send()


def scatter_near(exp, con, own, mix_own, ask, source, mix, norms, away):
    rows, half = D // (4 * DEPTH), D // 2
    grads = [g.reshape(DEPTH, 2, 2, rows, g.shape[1]) for g in (exp, con, own, mix_own, ask, source, mix)]
    vmem = pl.BlockSpec(memory_space=pltpu.VMEM)
    anywhere = pl.BlockSpec(memory_space=pl.ANY)
    dma = pltpu.SemaphoreType.DMA
    return pl.pallas_call(
        scatter_kernel,
        in_specs=[anywhere] * 7 + [vmem, anywhere],
        out_specs=[vmem, vmem, anywhere],
        out_shape=[
            jax.ShapeDtypeStruct((PIECES, rows, half), f32),
            jax.ShapeDtypeStruct(norms.shape, f32),
            jax.ShapeDtypeStruct(away.shape, away.dtype),
        ],
        scratch_shapes=[
            pltpu.VMEM((PIECES, DEPTH, 2, 2, rows, half), bf16),
            pltpu.VMEM((PIECES, DEPTH, 2, 2, rows, half), bf16),
            pltpu.VMEM((PIECES, DEPTH, 2, rows, half), bf16),
            pltpu.VMEM((PIECES, DEPTH, 2, rows, half), bf16),
            pltpu.VMEM((PIECES, DEPTH, 2, rows, half), bf16),
            pltpu.VMEM((PIECES, rows, half), bf16),
            pltpu.VMEM((2, rows, half), f32),
            pltpu.VMEM((6, *norms.shape), f32),
            pltpu.VMEM((DEPTH, *norms.shape), f32),
            dma((PIECES, 2)),
            dma((PIECES, 2)),
            dma((PIECES, 2)),
            dma((PIECES,)),
            dma((PIECES,)),
            dma((PIECES, DEPTH)),
            dma((PIECES, DEPTH)),
            dma((PIECES, DEPTH)),
            dma((PIECES,)),
            dma((PIECES,)),
            dma((3 + 2 * DEPTH,)),
            dma((3 + DEPTH,)),
            dma((2 * away.shape[0],)),
            dma((2 * away.shape[0],)),
        ],
        cost_estimate=pl.CostEstimate(flops=0, bytes_accessed=SCATTER_COST, transcendentals=0),
        compiler_params=pltpu.CompilerParams(collective_id=1, has_side_effects=True, vmem_limit_bytes=60 * 2**20),
    )(*grads, norms, away)


def scatter_grads(grads, norms, away):
    exp, con, own, mix_own, ask, source, mix = grads
    if lax.axis_size("dp") == 4 * DEPTH:
        parts, norm_sums, back = scatter_near(*grads, jnp.pad(norms, ((0, 8 - norms.shape[0]), (0, 0))), away)
        ordered = [parts[p] for p in range(PIECES) if p % 3 != 2] + [parts[p] for p in range(PIECES) if p % 3 == 2]
        exp, con = (jnp.concatenate(part, axis=1) for part in (ordered[:4], ordered[4:8]))
        return [*ordered[8:], exp, con], norm_sums, back
    sides = []
    for g in (own, mix_own, ask, source, mix):
        sides.append(g.reshape(D, g.shape[1] // D, 2, D // 2).transpose(1, 2, 0, 3))
    for g in (exp, con):
        sides.append(g.reshape(D, 2, g.shape[1] // D, D // 2).transpose(2, 1, 0, 3))
    stacked = jnp.concatenate(sides).reshape(-1, 2 * D, D // 2)
    parts = lax.psum_scatter(stacked, ("mp", "dp"), scatter_dimension=1, tiled=True).astype(f32)
    chunks = (parts.shape[0] - 8) // 2
    exp, con = (jnp.concatenate(list(parts[start : start + chunks]), axis=1) for start in (8, 8 + chunks))
    return [*(parts[i] for i in range(8)), exp, con], lax.psum(norms, BOTH), swap(away)


def body(text_tokens, image_tokens, resolution, *rest):
    shards, norms, cotangent = rest[:10], rest[10:16], rest[16]
    side = lax.axis_index("mp")
    half = text_tokens.shape[0] // 2
    width = text_tokens.shape[2]
    flat = [shard.T if turned else shard for shard, turned in zip(shards, TURNED)]
    weights = gather_weights(jnp.stack(flat[:8]), flat[8], flat[9])
    text = to_captions(text_tokens, side)
    grad_out = to_captions(cotangent, side)
    patches = lax.dynamic_slice_in_dim(image_tokens, side * half, half, 0)
    flags = lax.dynamic_slice_in_dim(resolution, side * half, half, 0)
    layer_out, text_grad, patch_grad, weight_grads, norm_outs = layer(
        weights, norms, text.reshape(-1, width), grad_out.reshape(-1, width), patches.reshape(-1, width), flags
    )
    weight_outs = [g.T if turned else g for g, turned in zip(weight_grads, TURNED)]
    return (
        to_positions(layer_out.reshape(half, LEN, width), side),
        to_positions(text_grad.reshape(half, LEN, width), side).astype(f32),
        patch_grad,
        *weight_outs,
        *(norm_outs[i] for i in range(6)),
    )


def solution(mesh):
    tokens = P("dp", "mp", None)
    rows, columns = P("dp", "mp"), P("mp", "dp")
    kinds = (rows, rows, rows, columns, rows, rows, rows, columns, rows, columns)
    in_specs = (tokens, P("dp", None, None), P("dp"), *kinds, *([P()] * 6), tokens)
    out_specs = (tokens, tokens, tokens, *kinds, *([P()] * 6))
    return jax.shard_map(body, mesh=mesh, in_specs=in_specs, out_specs=out_specs, check_vma=False)
```

```python
import functools

import jax
import jax.numpy as jnp
from jax import lax
from jax.experimental import pallas as pl
from jax.experimental.pallas import tpu as pltpu
from jax.sharding import PartitionSpec as P

HD = 64
D = 768
GROUP = 256
ROWS = 1152
LEN = 64
PATCH = 576
SMALLP = 196
BOTH = ("dp", "mp")

epsilon = 1e-05
masked_score = -1000000000.0
bf16 = jnp.bfloat16
f32 = jnp.float32


def dot(left, right, left_dim, right_dim):
    return lax.dot_general(left, right, (((left_dim,), (right_dim,)), ((), ())), preferred_element_type=f32)


def matmul(left, right):
    return dot(left, right, 1, 0)


def matmul_t(left, right):
    return dot(left, right, 1, 1)


def weight_grad(left, right):
    return dot(left, right, 0, 0)


def norm_stats(value):
    average = jnp.mean(value, axis=-1, keepdims=True)
    centred = value - average
    spread = jnp.mean(centred * centred, axis=-1, keepdims=True)
    inverse = lax.rsqrt(spread + epsilon)
    return centred * inverse, inverse


def norm_back(normal, inverse, gain, grad):
    scaled = grad * gain
    mean_one = jnp.mean(scaled, axis=-1, keepdims=True)
    mean_two = jnp.mean(scaled * normal, axis=-1, keepdims=True)
    grad_value = (scaled - mean_one - normal * mean_two) * inverse
    return grad_value, jnp.sum(grad * normal, axis=0, keepdims=True), jnp.sum(grad, axis=0, keepdims=True)


def spread(rows):
    head = lax.broadcasted_iota(jnp.int32, rows.shape, 1) // HD
    zero = jnp.zeros_like(rows)
    return jnp.concatenate([jnp.where(head == h, rows, zero) for h in range(rows.shape[1] // HD)], axis=0)


def collect(blocks):
    count = blocks.shape[1] // HD
    length = blocks.shape[0] // count
    head = lax.broadcasted_iota(jnp.int32, (length, blocks.shape[1]), 1) // HD
    total = blocks[:length]
    for h in range(1, count):
        total = jnp.where(head == h, blocks[h * length : (h + 1) * length], total)
    return total


def groups(width):
    return [slice(start, start + GROUP) for start in range(0, width, GROUP)]


def attend_kernel(causal, batch, flag_ref, query_ref, key_ref, value_ref, mix_ref, prob_ref):
    keys = key_ref.shape[0] // batch
    shape = (keys, GROUP // HD * LEN)
    row = lax.broadcasted_iota(jnp.int32, shape, 0)
    for n in range(batch):
        ask, see = slice(n * LEN, (n + 1) * LEN), slice(n * keys, (n + 1) * keys)
        if causal:
            allowed = row <= lax.broadcasted_iota(jnp.int32, shape, 1) % LEN
        else:
            allowed = row < SMALLP + (PATCH - SMALLP) * flag_ref[pl.program_id(0) * batch + n]
        for part in groups(query_ref.shape[1]):
            queries = spread(query_ref[ask, part]) * jnp.asarray(HD ** (-0.5), bf16)
            scores = jnp.where(allowed, dot(key_ref[see, part], queries, 1, 1), masked_score)
            exponent = jnp.exp(scores - jnp.max(scores, axis=0, keepdims=True))
            probs = (exponent * (1.0 / jnp.sum(exponent, axis=0, keepdims=True))).astype(bf16)
            prob_ref[see, part] = probs
            mix_ref[ask, part] = collect(dot(probs, value_ref[see, part], 0, 0)).astype(bf16)


def attend_back_kernel(batch, query_ref, key_ref, value_ref, prob_ref, grad_ref, *outs):
    width = query_ref.shape[1]
    keys = key_ref.shape[0] // batch
    joined = outs[-1]
    query_out, shift = (outs[0], 0) if len(outs) == 2 else (joined, width)
    for n in range(batch):
        ask, see = slice(n * LEN, (n + 1) * LEN), slice(n * keys, (n + 1) * keys)
        for part in groups(width):
            queries = spread(query_ref[ask, part]) * jnp.asarray(HD ** (-0.5), bf16)
            grads = spread(grad_ref[ask, part])
            probs_low = prob_ref[see, part]
            probs = probs_low.astype(f32)
            grad_prob = dot(value_ref[see, part], grads, 1, 1)
            inner = jnp.sum(probs * grad_prob, axis=0, keepdims=True)
            grad_score = (probs * (grad_prob - inner)).astype(bf16)
            key_part = slice(shift + part.start, shift + part.stop)
            value_part = slice(shift + width + part.start, shift + width + part.stop)
            joined[see, value_part] = dot(probs_low, grads, 1, 0).astype(bf16)
            joined[see, key_part] = dot(grad_score, queries, 1, 0).astype(bf16)
            query_out[ask, part] = (collect(dot(grad_score, key_ref[see, part], 0, 0)) * HD ** (-0.5)).astype(bf16)


def column(rows, width):
    return pl.BlockSpec((rows, width), lambda i, *_: (i, 0))


def attend_cost(queries, count, keys, products):
    if keys == LEN and products == 4:
        return pl.CostEstimate(flops=2**20, bytes_accessed=2**20, transcendentals=0)
    flops = 2 * products * count * LEN * keys * D * GROUP // HD
    return pl.CostEstimate(flops=flops, bytes_accessed=products * 2 * count * keys * D, transcendentals=0)


def batch_of(count, keys):
    for batch in (8, 4, 2):
        if count % batch == 0 and batch * keys <= ROWS:
            return batch
    return 1


def attend(queries, sources, values, flags, count, causal):
    keys = sources.shape[0] // count
    batch = batch_of(count, keys)
    ask, see, width = batch * LEN, batch * keys, D
    grid_spec = pltpu.PrefetchScalarGridSpec(
        num_scalar_prefetch=1,
        grid=(count // batch,),
        in_specs=[column(ask, width), column(see, width), column(see, width)],
        out_specs=[column(ask, width), column(see, width)],
    )
    return pl.pallas_call(
        functools.partial(attend_kernel, causal, batch),
        grid_spec=grid_spec,
        out_shape=(
            jax.ShapeDtypeStruct((count * LEN, width), bf16),
            jax.ShapeDtypeStruct((count * keys, width), bf16),
        ),
        cost_estimate=attend_cost(queries, count, keys, 2),
    )(flags, queries, sources, values)


def attend_back(queries, sources, values, probs, grad_mix, count, whole):
    keys = sources.shape[0] // count
    batch = batch_of(count, keys)
    ask, see, width = batch * LEN, batch * keys, D
    widths = [(keys, 3 * width)] if whole else [(LEN, width), (keys, 2 * width)]
    return pl.pallas_call(
        functools.partial(attend_back_kernel, batch),
        grid=(count // batch,),
        in_specs=[
            column(ask, width),
            column(see, width),
            column(see, width),
            column(see, width),
            column(ask, width),
        ],
        out_specs=[column(batch * rows, wide) for rows, wide in widths],
        out_shape=[jax.ShapeDtypeStruct((count * rows, wide), bf16) for rows, wide in widths],
        cost_estimate=attend_cost(queries, count, keys, 4),
    )(queries, sources, values, probs, grad_mix)


def swap(rows):
    return lax.ppermute(rows, "mp", [(0, 1), (1, 0)])


def patch_kernel(side_ref, grad_ref, key_ref, value_ref, out_ref):
    width = key_ref.shape[1]
    for n in range(grad_ref.shape[0]):
        product = dot(grad_ref[n, :, :width], key_ref[...], 1, 1) + dot(grad_ref[n, :, width:], value_ref[...], 1, 1)
        out_ref[n] = product.astype(out_ref.dtype)


def patch_product(grads, key_w, value_w, first, last, half, place_at, total, kind):
    batch = 2 - (last - first) % 2
    rows = PATCH // 2
    width, depth = key_w.shape[0], 2 * key_w.shape[1]
    grid_spec = pltpu.PrefetchScalarGridSpec(
        num_scalar_prefetch=1,
        grid=((last - first) // batch,),
        in_specs=[
            pl.BlockSpec((batch, rows, depth), lambda i, at: (i + first // batch, at[0], 0)),
            pl.BlockSpec(key_w.shape, lambda i, at: (0, 0)),
            pl.BlockSpec(value_w.shape, lambda i, at: (0, 0)),
        ],
        out_specs=pl.BlockSpec((batch, rows, width), lambda i, at: (i + at[1] // batch, 0, 0)),
    )
    flops = 2**20
    return pl.pallas_call(
        patch_kernel,
        grid_spec=grid_spec,
        out_shape=jax.ShapeDtypeStruct((total, rows, width), kind),
        cost_estimate=pl.CostEstimate(flops=flops, bytes_accessed=flops // width, transcendentals=0),
    )(jnp.stack([half, place_at]), grads.reshape(-1, PATCH, depth), key_w, value_w)


def widen_kernel(first, side_ref, early_ref, late_ref, whole_ref, out_ref):
    early = pl.program_id(0) < first

    @pl.when(early)
    def _():
        out_ref[...] = early_ref[...].astype(f32)

    @pl.when(jnp.logical_not(early))
    def _():
        out_ref[...] = late_ref[...].astype(f32)


def widen(early, late, whole, place_at):
    count, height, width = early.shape
    grid_spec = pltpu.PrefetchScalarGridSpec(
        num_scalar_prefetch=1,
        grid=(count + late.shape[0],),
        in_specs=[
            pl.BlockSpec((1, height, width), lambda i, at: (jnp.minimum(i, count - 1), 0, 0)),
            pl.BlockSpec((1, height, width), lambda i, at: (jnp.maximum(i - count, 0), 0, 0)),
            pl.BlockSpec(memory_space=pl.ANY),
        ],
        out_specs=pl.BlockSpec((1, height, width), lambda i, at: (i + at[0], 0, 0)),
    )
    return pl.pallas_call(
        functools.partial(widen_kernel, count),
        grid_spec=grid_spec,
        out_shape=jax.ShapeDtypeStruct(whole.shape, f32),
        input_output_aliases={3: 0},
    )(place_at[None], early, late, whole)


def gelu_parts(value):
    inner = 0.7978845608028654 * (value + 0.044715 * value * value * value)
    bent = jnp.tanh(inner)
    hidden = 0.5 * value * (1.0 + bent)
    slope = 0.5 * (1.0 + bent) + 0.5 * value * (1.0 - bent * bent) * 0.7978845608028654 * (1.0 + 3 * 0.044715 * value * value)
    return hidden, slope


def layer(weights, norms, text, cotangent, patches, resolution):
    count = text.shape[0] // LEN
    query_self, key_self, value_self, mix_self, query_cross, key_cross, value_cross, mix_cross, expand, contract = weights
    first_gain, first_shift, second_gain, second_shift, third_gain, third_shift = norms
    stream = text.astype(f32)
    normal_one, inverse_one = norm_stats(stream)
    normed_one = (normal_one * first_gain + first_shift).astype(bf16)
    queries_one, keys_one, values_one = (matmul(normed_one, w).astype(bf16) for w in (query_self, key_self, value_self))
    mixed_one, probs_one = attend(queries_one, keys_one, values_one, resolution, count, True)
    stream_one = stream + matmul_t(mixed_one, mix_self)
    normal_two, inverse_two = norm_stats(stream_one)
    normed_two = (normal_two * second_gain + second_shift).astype(bf16)
    queries_two = matmul(normed_two, query_cross).astype(bf16)
    keys_two, values_two = (matmul(patches, w).astype(bf16) for w in (key_cross, value_cross))
    mixed_two, probs_two = attend(queries_two, keys_two, values_two, resolution, count, False)
    stream_two = stream_one + matmul_t(mixed_two, mix_cross)
    normal_three, inverse_three = norm_stats(stream_two)
    normed_three = (normal_three * third_gain + third_shift).astype(bf16)
    hidden, slope = gelu_parts(matmul(normed_three, expand))
    hidden = hidden.astype(bf16)
    layer_out = stream_two + matmul_t(hidden, contract)
    grad_pre = (slope * matmul(cotangent, contract)).astype(bf16)
    grad_expand = weight_grad(normed_three, grad_pre)
    grad_contract = weight_grad(cotangent, hidden)
    grad_normed = matmul_t(grad_pre, expand)
    grad_input, gain_three, shift_three = norm_back(normal_three, inverse_three, third_gain, grad_normed)
    grad_stream = cotangent.astype(f32) + grad_input
    grad_rows = grad_stream.astype(bf16)
    grad_mix_cross = weight_grad(grad_rows, mixed_two).astype(bf16)
    grad_expand, grad_contract = grad_expand.astype(bf16), grad_contract.astype(bf16)
    layer_out = layer_out.astype(bf16)
    grad_rows, grad_expand, grad_contract, grad_mix_cross, layer_out = lax.optimization_barrier(
        (grad_rows, grad_expand, grad_contract, grad_mix_cross, layer_out)
    )
    grad_mixed = matmul(grad_rows, mix_cross).astype(bf16)
    grad_queries, grad_sources = attend_back(queries_two, keys_two, values_two, probs_two, grad_mixed, count, False)
    side = lax.axis_index("mp")
    grad_query_cross = weight_grad(normed_two, grad_queries).astype(bf16)
    grad_patch = weight_grad(patches, grad_sources).astype(bf16)
    grad_patch, grad_sources, grad_query_cross = lax.optimization_barrier((grad_patch, grad_sources, grad_query_cross))
    first = count * 5 // 8
    near, far = (0, first), (first, count)
    early = patch_product(grad_sources, key_cross, value_cross, *near, 1 - side, 0 * side, first, bf16)
    early, grad_queries = lax.optimization_barrier((early, grad_queries))
    early = swap(early)
    late = patch_product(grad_sources, key_cross, value_cross, *far, 1 - side, 0 * side, count - first, bf16)
    grad_normed = matmul_t(grad_queries, query_cross)
    grad_input, gain_two, shift_two = norm_back(normal_two, inverse_two, second_gain, grad_normed)
    grad_stream = grad_stream + grad_input
    grad_rows = grad_stream.astype(bf16)
    grad_mix_self = weight_grad(grad_rows, mixed_one)
    grad_mixed = matmul(grad_rows, mix_self).astype(bf16)
    (grad_one,) = attend_back(queries_one, keys_one, values_one, probs_one, grad_mixed, count, True)
    grad_self = weight_grad(normed_one, grad_one)
    grad_normed = sum(matmul_t(grad_one[:, i * D : (i + 1) * D], w) for i, w in enumerate((query_self, key_self, value_self)))
    grad_input, gain_one, shift_one = norm_back(normal_one, inverse_one, first_gain, grad_normed)
    text_grad = (grad_stream + grad_input).astype(bf16)
    norm_grads = [gain_one, shift_one, gain_two, shift_two, gain_three, shift_three]
    grads = [grad_expand, grad_contract, grad_self, grad_mix_self, grad_query_cross, grad_patch, grad_mix_cross]
    early, norm_grads[0] = lax.optimization_barrier((early, norm_grads[0]))
    grads = [g.astype(bf16) for g in grads]
    layer_mine, layer_away = split_positions(layer_out.reshape(count, LEN, D), side)
    text_mine, text_away = split_positions(text_grad.reshape(count, LEN, D), side)
    weight_grads, norm_sums, patch_grad, text_back, layer_back = scatter_grads(
        grads, norm_grads, grad_sources, early, late, key_cross, value_cross, text_away, layer_away
    )
    layer_out = join_positions(layer_mine, layer_back, side)
    text_grad = join_positions(text_mine, text_back, side).astype(f32)
    return layer_out, text_grad, patch_grad, weight_grads, norm_sums


def split_captions(rows, side):
    half = rows.shape[0] // 2
    return tuple(lax.dynamic_slice_in_dim(rows, at * half, half, 0) for at in (side, 1 - side))


def join_captions(mine, other, side):
    low = jnp.where(side == 0, mine, other)
    high = jnp.where(side == 0, other, mine)
    return jnp.concatenate([low, high], axis=1)


def split_positions(rows, side):
    half = rows.shape[1] // 2
    return tuple(lax.dynamic_slice_in_dim(rows, at * half, half, 1) for at in (side, 1 - side))


def join_positions(mine, other, side):
    first = (jnp.arange(2) == side).reshape(2, 1, 1, 1)
    return jnp.where(first, mine[None], other[None]).reshape(2 * mine.shape[0], *mine.shape[1:])


TURNED = (False, False, False, True, False, False, False, True, False, True)


MESH = pl.DeviceIdType.MESH
DEPTH = 4
BUNDLE = 4


def place():
    index = lax.axis_index("dp")
    return index // 4, index // 2 % 2, index % 2, lax.axis_index("mp")


def greet(z, x, c, y):
    barrier = pltpu.get_barrier_semaphore()

    def hello(z_to, x_to, c_to, y_to):
        pl.semaphore_signal(barrier, inc=1, device_id=(z_to * 4 + x_to * 2 + c_to, y_to), device_id_type=MESH)

    hello(z, 1 - x, c, y)
    hello(z, x, 1 - c, y)
    hello(z, x, c, 1 - y)

    @pl.when(z > 0)
    def _():
        hello(z - 1, x, c, y)

    @pl.when(z < DEPTH - 1)
    def _():
        hello(z + 1, x, c, y)

    pl.semaphore_wait(barrier, 3 + jnp.where(z > 0, 1, 0) + jnp.where(z < DEPTH - 1, 1, 0))


class Bundle:
    def __init__(self, copies, total):
        self.copies, self.total = copies, total

    def start(self):
        for one in self.copies:
            one.start()

    def wait(self):
        self.total.wait()

    def wait_send(self):
        self.total.wait_send()

    def wait_recv(self):
        self.total.wait_recv()


def gather_kernel(att_in, exp_in, con_in, text_in, grad_in, image, *refs):
    att, refs = refs[: att_in.shape[0]], refs[att_in.shape[0] :]
    exp, con, text_out, grad_out, patches, image_buf, own_sem, side_send, up_send, down_send = refs[:10]
    far_send, mate_send, recv, mate_recv, trade_send, trade_recv, load_sem, store_sem = refs[10:]
    z, x, c, y = place()
    half, wide = att_in.shape[2], exp_in.shape[1]
    greet(z, x, c, y)

    def stream(index):
        early = index % 2 == 0
        part = index // 2
        line_first = index == 2

        bundle = range(part * BUNDLE, (part + 1) * BUNDLE)
        whole = att_in.at[pl.ds(part * BUNDLE, BUNDLE)] if early else (exp_in, con_in)[part].at[...]

        def own():
            return [att_in.at[i] for i in bundle] if early else [whole]

        def region(w, z_from, u, core):
            x_from = (x + (w if early else u)) % 2
            y_from = (y + (u if early else w)) % 2
            row = z_from * 4 + x_from * 2 + core
            if early:
                return [att[i].at[row, :, pl.ds(pl.multiple_of(y_from * half, 128), half)] for i in bundle]
            return [(exp, con)[part].at[row, :, pl.ds(pl.multiple_of(y_from * wide, 128), wide)]]

        if early:
            beside, far = (z * 4 + (1 - x) * 2 + c, y), (z * 4 + x * 2 + c, 1 - y)
        else:
            beside, far = (z * 4 + x * 2 + c, 1 - y), (z * 4 + (1 - x) * 2 + c, y)

        def copy(src, dst, send, receive, device):
            def make(one, two):
                return pltpu.make_async_remote_copy(
                    src_ref=one, dst_ref=two, send_sem=send, recv_sem=receive, device_id=device, device_id_type=MESH
                )

            return Bundle([make(one, two) for one, two in zip(src, dst)], make(whole, whole))

        mine = z * 4 + x * 2 + c

        def to_beside(z_from, src):
            return copy(src, region(0, z_from, 0, c), side_send.at[index, z_from], recv.at[index, 1, z_from, 0], beside)

        def to_up(w, z_from, src):
            return copy(src, region(w, z_from, 0, c), up_send.at[index, w, z_from], recv.at[index, w, z_from, 0], (mine + 4, y))

        def to_down(w, z_from, src):
            return copy(src, region(w, z_from, 0, c), down_send.at[index, w, z_from], recv.at[index, w, z_from, 0], (mine - 4, y))

        def to_far(w, z_from, src):
            return copy(src, region(w, z_from, 0, c), far_send.at[index, w, z_from], recv.at[index, w, z_from, 1], far)

        def to_mate(w, z_from, u, src):
            return copy(
                src,
                region(w, z_from, u, c),
                mate_send.at[index, w, z_from, u],
                mate_recv.at[index, w, z_from, u],
                (z * 4 + x * 2 + 1 - c, y),
            )

        def keep():
            def make(one, two):
                return pltpu.make_async_copy(one, two, own_sem.at[index])

            return Bundle([make(one, two) for one, two in zip(own(), region(0, z, 0, c))], make(whole, whole))

        def arrive(w, z_from, u):
            spot = region(w, z_from, u, c)
            copy(spot, spot, far_send.at[index, w, z_from], recv.at[index, w, z_from, u], far).wait_recv()

        def arrive_mate(w, z_from, u):
            spot = region(w, z_from, u, 1 - c)
            copy(spot, spot, far_send.at[index, w, z_from], mate_recv.at[index, w, z_from, u], far).wait_recv()

        def pass_on(w, z_from, src, up, down):
            if w == 0 or not line_first:

                @pl.when(up)
                def _():
                    to_up(w, z_from, src).start()

                @pl.when(down)
                def _():
                    to_down(w, z_from, src).start()

            if w == 0 and line_first:
                to_beside(z_from, src).start()
            to_far(w, z_from, src).start()
            to_mate(w, z_from, 0, src).start()

        def first():
            if not line_first:
                to_beside(z, own()).start()
            pass_on(0, z, own(), z < DEPTH - 1, z > 0)
            keep().start()

        def second():
            arrive(1, z, 0)
            pass_on(1, z, region(1, z, 0, c), z < DEPTH - 1, z > 0)

        def along(w, distance):
            @pl.when(z >= distance)
            def _():
                z_from = z - distance
                arrive(w, z_from, 0)
                pass_on(w, z_from, region(w, z_from, 0, c), z < DEPTH - 1, z < 0)

            @pl.when(z + distance < DEPTH)
            def _():
                z_from = z + distance
                arrive(w, z_from, 0)
                pass_on(w, z_from, region(w, z_from, 0, c), z < 0, z > 0)

        def across(w, z_from):
            arrive(w, z_from, 1)
            to_mate(w, z_from, 1, region(w, z_from, 1, c)).start()

        def across_at(w, distance):
            if distance == 0:
                across(w, z)
                return

            @pl.when(z >= distance)
            def _():
                across(w, z - distance)

            @pl.when(z + distance < DEPTH)
            def _():
                across(w, z + distance)

        def finish():
            keep().wait()
            if not line_first:
                to_beside(z, own()).wait_send()

            def each(number, _):
                w, z_from = number // DEPTH, number % DEPTH
                spot = region(w, z_from, 0, c)
                in_line = (w == 0) if line_first else (w >= 0)

                @pl.when(in_line & (z < DEPTH - 1) & (z_from <= z))
                def _():
                    to_up(w, z_from, spot).wait_send()

                @pl.when(in_line & (z > 0) & (z_from >= z))
                def _():
                    to_down(w, z_from, spot).wait_send()

                if line_first:

                    @pl.when(w == 0)
                    def _():
                        to_beside(z_from, spot).wait_send()

                to_far(w, z_from, spot).wait_send()
                for u in range(2):
                    to_mate(w, z_from, u, spot).wait_send()
                    arrive_mate(w, z_from, u)
                return 0

            lax.fori_loop(0, 2 * DEPTH, each, 0)

        return first, second, along, across_at, finish

    def trade(k):
        src, dst = ((text_in, text_out), (grad_in, grad_out))[k]
        return pltpu.make_async_remote_copy(
            src_ref=src,
            dst_ref=dst,
            send_sem=trade_send.at[k],
            recv_sem=trade_recv.at[k],
            device_id=(z * 4 + x * 2 + c, 1 - y),
            device_id_type=MESH,
        )

    count = patches.shape[0]

    def load(n):
        return pltpu.make_async_copy(image.at[y * count + n], image_buf.at[n], load_sem.at[n])

    def store(n):
        return pltpu.make_async_copy(image_buf.at[n], patches.at[n], store_sem.at[n])

    streams = [stream(index) for index in range(4)]
    for first, _, _, _, _ in streams:
        first()
    for n in range(count):
        load(n).start()
    for _, second, _, _, _ in streams:
        second()
    for k in range(2):
        trade(k).start()
    for n in range(count):
        load(n).wait()
        store(n).start()
    for distance in range(1, DEPTH + 1):
        for w in range(2):
            for _, _, along, across_at, _ in streams:
                if distance < DEPTH:
                    along(w, distance)
                across_at(w, distance - 1)
    for streamed in streams:
        streamed[4]()
    for k in range(2):
        trade(k).wait()
    for n in range(count):
        store(n).wait()


def gather_near(att, exp, con, text, grad, image):
    dp = lax.axis_size("dp")
    count = image.shape[0] // 2
    rows, half, wide = att.shape[1], att.shape[2], exp.shape[1]
    vmem = pl.BlockSpec(memory_space=pltpu.VMEM)
    anywhere = pl.BlockSpec(memory_space=pl.ANY)
    dma = pltpu.SemaphoreType.DMA
    return pl.pallas_call(
        gather_kernel,
        in_specs=[vmem] * 3 + [anywhere] * 3,
        out_specs=[anywhere] * (att.shape[0] + 5),
        out_shape=[jax.ShapeDtypeStruct((dp, rows, 2 * half), bf16)] * att.shape[0]
        + [
            jax.ShapeDtypeStruct((dp, rows, 2 * wide), bf16),
            jax.ShapeDtypeStruct((dp, rows, 2 * wide), bf16),
            jax.ShapeDtypeStruct(text.shape, bf16),
            jax.ShapeDtypeStruct(grad.shape, bf16),
            jax.ShapeDtypeStruct((count, *image.shape[1:]), bf16),
        ],
        scratch_shapes=[
            pltpu.VMEM((count, *image.shape[1:]), bf16),
            dma((4,)),
            dma((4, DEPTH)),
            dma((4, 2, DEPTH)),
            dma((4, 2, DEPTH)),
            dma((4, 2, DEPTH)),
            dma((4, 2, DEPTH, 2)),
            dma((4, 2, DEPTH, 2)),
            dma((4, 2, DEPTH, 2)),
            dma((2,)),
            dma((2,)),
            dma((count,)),
            dma((count,)),
        ],
        compiler_params=pltpu.CompilerParams(collective_id=0, has_side_effects=True),
    )(att, exp, con, text, grad, image)


def gather_weights(att, exp, con, text, grad, image):
    count, width = att.shape[0], D
    if lax.axis_size("dp") == 4 * DEPTH:
        *att, exp, con, text, grad, patches = gather_near(att, exp, con, text, grad, image)
        att = [w.reshape(width, -1) for w in att]
        exp, con = exp.reshape(width, -1), con.reshape(width, -1)
    else:
        chunks = exp.shape[1] // att.shape[2]
        narrow = [g[:, j * att.shape[2] : (j + 1) * att.shape[2]] for g in (exp, con) for j in range(chunks)]
        sides = lax.all_gather(att, ("mp", "dp"), axis=1, tiled=True).reshape(count, 2, width, -1)
        att = sides.transpose(0, 2, 1, 3).reshape(count, width, -1)
        sides = lax.all_gather(jnp.stack(narrow), ("mp", "dp"), axis=1, tiled=True).reshape(2, chunks, 2, width, -1)
        exp, con = sides.transpose(0, 3, 2, 1, 4).reshape(2, width, -1)
        text, grad = swap(text), swap(grad)
        patches, _ = split_captions(image, lax.axis_index("mp"))
    return [*(att[i] for i in range(8)), exp, con], text, grad, patches


PIECES = 16
SCATTER_COST = 2**20
SIDE_LAG = 1
NORM_STEP = 2
NORMS = 6


def scatter_kernel(exp, con, own, mix_own, ask, source, mix, *rest):
    norms, rest = rest[:NORMS], rest[NORMS:]
    scatter_body(exp, con, own, mix_own, ask, source, mix, norms, *rest)


def scatter_body(exp, con, own, mix_own, ask, source, mix, norms, away, early, kept, key_w, value_w, text, result, out, norm_out, whole, text_back, result_back, acc, other, side, low, high, last, total, norm_buf, norm_line, back, early_buf, kept_buf, weight_buf, wide, *sems):
    local_sem, mate_send, mate_recv, side_send, side_recv, line_send, low_recv, high_recv, last_send, last_recv, norm_send, norm_recv, away_send, back_recv, load_sem, wide_sem, trade_send, trade_recv = sems
    z, x, c, y = place()
    half = out.shape[2]
    mine = z * 4 + x * 2 + c
    mate = (z * 4 + x * 2 + 1 - c, y)
    greet(z, x, c, y)

    def copy(src, dst, send, receive, device):
        return pltpu.make_async_remote_copy(src_ref=src, dst_ref=dst, send_sem=send, recv_sem=receive, device_id=device, device_id_type=MESH)

    pieces = [(ref, ref.shape[4] // 2, j * half) for ref in (exp, con) for j in range(4)]
    pieces += [(own, half, 0), (own, half, 2 * half), (own, half, 4 * half), (mix_own, half, 0), (ask, half, 0)]
    pieces += [(source, half, 0), (source, half, 2 * half), (mix, half, 0)]

    over_x, over_y = pieces[: PIECES * 2 // 3 + 1], pieces[PIECES * 2 // 3 + 1 :]
    for p in range(PIECES):
        ref, stride, offset = over_y[p // 3] if p % 3 == 2 else over_x[p // 3 * 2 + p % 3]
        for k in range(2):
            columns = pl.ds(k * stride + offset, half)
            spot = (p, slice(None), k) if p % 3 == 2 else (p, slice(None), slice(None), k)
            copy(ref.at[:, :, 1 - c, :, columns], other.at[spot], mate_send.at[p, k], mate_recv.at[p, k], mate).start()
            pltpu.make_async_copy(ref.at[:, :, c, :, columns], acc.at[spot], local_sem.at[p, k]).start()

    count, given = kept.shape[0], away.shape[0]

    def load(n):
        return pltpu.make_async_copy(kept.at[n, y], kept_buf.at[n], load_sem.at[n])

    def load_early():
        return pltpu.make_async_copy(early, early_buf, load_sem.at[count])

    def load_weight(k):
        return pltpu.make_async_copy((key_w, value_w)[k], weight_buf.at[k], load_sem.at[count + 1 + k])

    for k in range(2):
        load_weight(k).start()
    for n in range(count):
        load(n).start()
    load_early().start()

    def put(item):
        place_at = jnp.where(item < count, y * count + item, (1 - y) * count + item - count)
        return pltpu.make_async_copy(wide.at[item % 2], whole.at[place_at], wide_sem.at[item % 2])

    def room(item):
        @pl.when(item >= 2)
        def _():
            put(item - 2).wait()

    def keep(item):
        @pl.when(item == 0)
        def _():
            for k in range(2):
                load_weight(k).wait()

        load(item).wait()
        room(item)
        rows, width = kept_buf.at[item], weight_buf.shape[1]
        product = dot(rows[:, :width], weight_buf[0], 1, 1) + dot(rows[:, width:], weight_buf[1], 1, 1)
        wide[item % 2] = product.astype(bf16)
        put(item).start()

    def widen_early(item):
        @pl.when(item == count)
        def _():
            load_early().wait()

        room(item)
        wide[item % 2] = early_buf[item - count]
        put(item).start()

    def widen_late(item):
        n = item - 2 * count + given
        for k in range(2):
            part(2 * n + k).wait_recv()
        room(item)
        wide[item % 2] = back[n]
        put(item).start()

    def trade(k):
        src, dst = ((text, text_back), (result, result_back))[k]
        return copy(src, dst, trade_send.at[k], trade_recv.at[k], (mine, 1 - y))

    def part(j):
        rows = away.shape[1] // 2
        spot = (j // 2, pl.ds(pl.multiple_of(j % 2 * rows, 16), rows))
        return copy(away.at[spot], back.at[spot], away_send.at[j], back_recv.at[j], (mine, 1 - y))

    def kind(p):
        odd = jnp.where(p % 3 == 2, 1, 0)
        u = x * (1 - odd) + y * odd
        w = y * (1 - odd) + x * odd
        over_x = (z * 4 + (1 - x) * 2 + c, y)
        over_y = (mine, 1 - y)
        first = tuple(one * (1 - odd) + two * odd for one, two in zip(over_x, over_y))
        second = tuple(two * (1 - odd) + one * odd for one, two in zip(over_x, over_y))
        return u, w, first, second

    def to_mate(p, k):
        return copy(other.at[p, :, k], other.at[p, :, k], mate_send.at[p, k], mate_recv.at[p, k], mate)

    def to_side(p):
        u, w, first, second = kind(p)
        return copy(acc.at[p, :, 1 - u], side.at[p], side_send.at[p], side_recv.at[p], first)

    def to_low(p, unit):
        u, w, first, second = kind(p)
        return copy(acc.at[p, unit, u], low.at[p, unit], line_send.at[p, unit], low_recv.at[p, unit], (mine - 4, y))

    def to_high(p, unit):
        u, w, first, second = kind(p)
        return copy(acc.at[p, unit, u], high.at[p, unit], line_send.at[p, unit], high_recv.at[p, unit], (mine + 4, y))

    def to_last(p):
        u, w, first, second = kind(p)
        return copy(acc.at[p, z, u, 1 - w], last.at[p], last_send.at[p], last_recv.at[p], second)

    def open_piece(p):
        for k in range(2):
            pltpu.make_async_copy(other.at[p, :, k], acc.at[p, :, k], local_sem.at[p, k]).wait()
        for k in range(2):
            to_mate(p, k).wait_recv()

        def add(unit, _):
            acc[p, unit] = (acc[p, unit].astype(f32) + other[p, unit].astype(f32)).astype(bf16)
            return 0

        lax.fori_loop(0, DEPTH, add, 0)
        to_side(p).start()

    def add_side(p):
        u, w, first, second = kind(p)
        to_side(p).wait_recv()

        def add(unit, _):
            acc[p, unit, u] = (acc[p, unit, u].astype(f32) + side[p, unit].astype(f32)).astype(bf16)
            return 0

        lax.fori_loop(0, DEPTH, add, 0)

    def pass_line(p, buffer, inner, has_source, beyond, send):
        u, w, first, second = kind(p)

        def each(unit, _):
            @pl.when(has_source & (beyond(unit) | (unit == z)))
            def _():
                inner(p, unit).wait_recv()

            @pl.when(has_source & beyond(unit))
            def _():
                acc[p, unit, u] = (acc[p, unit, u].astype(f32) + buffer[p, unit].astype(f32)).astype(bf16)

            @pl.when(beyond(unit))
            def _():
                send(p, unit).start()

            return 0

        lax.fori_loop(0, DEPTH, each, 0)

    def close_line(p):
        u, w, first, second = kind(p)
        total[...] = acc[p, z, u].astype(f32)

        @pl.when(z < DEPTH - 1)
        def _():
            total[...] += low[p, z].astype(f32)

        @pl.when(z > 0)
        def _():
            total[...] += high[p, z].astype(f32)

        acc[p, z, u, 1 - w] = total[1 - w].astype(bf16)
        to_last(p).start()
        out[p] = total[w]

    def close_piece(p):
        to_last(p).wait_recv()
        out[p] += last[p].astype(f32)

    def norm_pair(step):
        device = (mate, (z * 4 + (1 - x) * 2 + c, y), (mine, 1 - y))[step]
        return copy(norm_buf.at[step], norm_buf.at[3 + step], norm_send.at[step], norm_recv.at[step], device)

    def norm_up(unit):
        return copy(norm_line.at[unit], norm_line.at[unit], norm_send.at[3 + unit], norm_recv.at[3 + unit], (mine + 4, y))

    def norm_down(unit):
        return copy(norm_line.at[unit], norm_line.at[unit], norm_send.at[3 + DEPTH + unit], norm_recv.at[3 + unit], (mine - 4, y))

    def norm_steps(t):
        @pl.when(t == 0)
        def _():
            norm_buf[0] = jnp.zeros(norm_buf.shape[1:], f32)
            for i, row in enumerate(norms):
                norm_buf[0, i : i + 1] = row[...]
            norm_pair(0).start()

        for step in range(1, 4):

            @pl.when(t == step * NORM_STEP)
            def _():
                norm_pair(step - 1).wait_recv()
                summed = norm_buf[step - 1] + norm_buf[2 + step]
                if step < 3:
                    norm_buf[step] = summed
                    norm_pair(step).start()
                else:
                    norm_line[z] = summed

                    @pl.when(z < DEPTH - 1)
                    def _():
                        norm_up(z).start()

                    @pl.when(z > 0)
                    def _():
                        norm_down(z).start()

        for distance in range(1, DEPTH):

            @pl.when((t == (3 + distance) * NORM_STEP) & (z >= distance))
            def _():
                norm_up(z - distance).wait_recv()

                @pl.when(z < DEPTH - 1)
                def _():
                    norm_up(z - distance).start()

            @pl.when((t == (3 + distance) * NORM_STEP) & (z + distance < DEPTH))
            def _():
                norm_down(z + distance).wait_recv()

                @pl.when(z > 0)
                def _():
                    norm_down(z + distance).start()

    def at(p, work):
        @pl.when((p >= 0) & (p < PIECES))
        def _():
            work(p)

    def step(t, _):
        at(2 * t, open_piece)
        at(2 * t + 1, open_piece)
        for j in range(2 * away.shape[0]):

            @pl.when(t == 1 + PIECES * j // (2 * away.shape[0]))
            def _():
                part(j).start()

        for k in range(2):

            @pl.when(t == 3 + 4 * k)
            def _():
                trade(k).start()

        at(t - SIDE_LAG, add_side)
        at(
            t - SIDE_LAG - (DEPTH - 1 - z),
            lambda p: pass_line(p, low, to_low, z < DEPTH - 1, lambda unit: unit < z, to_low),
        )
        at(t - SIDE_LAG - z, lambda p: pass_line(p, high, to_high, z > 0, lambda unit: unit > z, to_high))
        norm_steps(t)
        at(t - SIDE_LAG - DEPTH, close_line)
        item = t - 2

        @pl.when((item >= 0) & (item < count))
        def _():
            keep(item)

        @pl.when((item >= count) & (item < 2 * count - given))
        def _():
            widen_early(item)

        @pl.when((item >= 2 * count - given) & (item < 2 * count))
        def _():
            widen_late(item)

        return 0

    def close(p, _):
        close_piece(p)
        return 0

    lax.fori_loop(0, PIECES + SIDE_LAG + DEPTH, step, 0)
    lax.fori_loop(0, PIECES, close, 0)
    for k in range(2):
        trade(k).wait()
    for j in range(2 * given):
        part(j).wait_send()
    for item in (2 * count - 2, 2 * count - 1):
        put(item).wait()
    norm_out[...] = norm_line[0] + norm_line[1] + norm_line[2] + norm_line[3]

    def drain(p, _):
        for k in range(2):
            to_mate(p, k).wait_send()
        to_side(p).wait_send()

        def each(unit, _):
            @pl.when(unit != z)
            def _():
                to_low(p, unit).wait_send()

            return 0

        lax.fori_loop(0, DEPTH, each, 0)
        to_last(p).wait_send()
        return 0

    lax.fori_loop(0, PIECES, drain, 0)
    for index in range(3):
        norm_pair(index).wait_send()
    for unit in range(DEPTH):

        @pl.when((z < DEPTH - 1) & (unit <= z))
        def _():
            norm_up(unit).wait_send()

        @pl.when((z > 0) & (unit >= z))
        def _():
            norm_down(unit).wait_send()


def scatter_near(exp, con, own, mix_own, ask, source, mix, norms, away, early, kept, key_w, value_w, text, result):
    rows, half = D // (4 * DEPTH), D // 2
    count, height = kept.shape[0], kept.shape[2]
    grads = [g.reshape(DEPTH, 2, 2, rows, g.shape[1]) for g in (exp, con, own, mix_own, ask, source, mix)]
    vmem = pl.BlockSpec(memory_space=pltpu.VMEM)
    anywhere = pl.BlockSpec(memory_space=pl.ANY)
    dma = pltpu.SemaphoreType.DMA
    return pl.pallas_call(
        scatter_kernel,
        in_specs=[anywhere] * 7 + [vmem] * NORMS + [anywhere] * 7,
        out_specs=[vmem, vmem, anywhere, anywhere, anywhere],
        out_shape=[
            jax.ShapeDtypeStruct((PIECES, rows, half), f32),
            jax.ShapeDtypeStruct((8, D), f32),
            jax.ShapeDtypeStruct((2 * count, height, D), bf16),
            jax.ShapeDtypeStruct(text.shape, bf16),
            jax.ShapeDtypeStruct(result.shape, bf16),
        ],
        scratch_shapes=[
            pltpu.VMEM((PIECES, DEPTH, 2, 2, rows, half), bf16),
            pltpu.VMEM((PIECES, DEPTH, 2, 2, rows, half), bf16),
            pltpu.VMEM((PIECES, DEPTH, 2, rows, half), bf16),
            pltpu.VMEM((PIECES, DEPTH, 2, rows, half), bf16),
            pltpu.VMEM((PIECES, DEPTH, 2, rows, half), bf16),
            pltpu.VMEM((PIECES, rows, half), bf16),
            pltpu.VMEM((2, rows, half), f32),
            pltpu.VMEM((6, 8, D), f32),
            pltpu.VMEM((DEPTH, 8, D), f32),
            pltpu.VMEM(away.shape, bf16),
            pltpu.VMEM(early.shape, bf16),
            pltpu.VMEM((count, height, 2 * D), bf16),
            pltpu.VMEM((2, D, D), bf16),
            pltpu.VMEM((2, height, D), bf16),
            dma((PIECES, 2)),
            dma((PIECES, 2)),
            dma((PIECES, 2)),
            dma((PIECES,)),
            dma((PIECES,)),
            dma((PIECES, DEPTH)),
            dma((PIECES, DEPTH)),
            dma((PIECES, DEPTH)),
            dma((PIECES,)),
            dma((PIECES,)),
            dma((3 + 2 * DEPTH,)),
            dma((3 + DEPTH,)),
            dma((2 * away.shape[0],)),
            dma((2 * away.shape[0],)),
            dma((count + 3,)),
            dma((2,)),
            dma((2,)),
            dma((2,)),
        ],
        cost_estimate=pl.CostEstimate(flops=0, bytes_accessed=SCATTER_COST, transcendentals=0),
        compiler_params=pltpu.CompilerParams(collective_id=1, has_side_effects=True, vmem_limit_bytes=60 * 2**20),
    )(*grads, *norms, away, early, kept, key_w, value_w, text, result)


def scatter_grads(grads, norms, sources, early, late, key_w, value_w, text, result):
    exp, con, own, mix_own, ask, source, mix = grads
    count = sources.shape[0] // PATCH
    if lax.axis_size("dp") == 4 * DEPTH:
        kept = sources.reshape(count, 2, PATCH // 2, -1)
        parts, norm_sums, whole, text, result = scatter_near(*grads, norms, late, early, kept, key_w, value_w, text, result)
        ordered = [parts[p] for p in range(PIECES) if p % 3 != 2] + [parts[p] for p in range(PIECES) if p % 3 == 2]
        exp, con = (jnp.concatenate(part, axis=1) for part in (ordered[:4], ordered[4:8]))
        return [*ordered[8:], exp, con], norm_sums, whole.astype(f32), text, result
    side = lax.axis_index("mp")
    whole = patch_product(sources, key_w, value_w, 0, count, side, side * count, 2 * count, f32)
    whole = widen(early, swap(late), whole, (1 - side) * count)
    sides = []
    for g in (own, mix_own, ask, source, mix):
        sides.append(g.reshape(D, g.shape[1] // D, 2, D // 2).transpose(1, 2, 0, 3))
    for g in (exp, con):
        sides.append(g.reshape(D, 2, g.shape[1] // D, D // 2).transpose(2, 1, 0, 3))
    stacked = jnp.concatenate(sides).reshape(-1, 2 * D, D // 2)
    parts = lax.psum_scatter(stacked, ("mp", "dp"), scatter_dimension=1, tiled=True).astype(f32)
    chunks = (parts.shape[0] - 8) // 2
    exp, con = (jnp.concatenate(list(parts[start : start + chunks]), axis=1) for start in (8, 8 + chunks))
    return [*(parts[i] for i in range(8)), exp, con], lax.psum(jnp.concatenate(norms), BOTH), whole, swap(text), swap(result)


def body(text_tokens, image_tokens, resolution, *rest):
    shards, norms, cotangent = rest[:10], rest[10:16], rest[16]
    side = lax.axis_index("mp")
    half = text_tokens.shape[0] // 2
    width = text_tokens.shape[2]
    flat = [shard.T if turned else shard for shard, turned in zip(shards, TURNED)]
    text_mine, text_away = split_captions(text_tokens, side)
    grad_mine, grad_away = split_captions(cotangent, side)
    weights, text_back, grad_back, patches = gather_weights(
        jnp.stack(flat[:8]), flat[8], flat[9], text_away, grad_away, image_tokens
    )
    text = join_captions(text_mine, text_back, side)
    grad_out = join_captions(grad_mine, grad_back, side)
    flags = lax.dynamic_slice_in_dim(resolution, side * half, half, 0)
    layer_out, text_grad, patch_grad, weight_grads, norm_outs = layer(
        weights, norms, text.reshape(-1, width), grad_out.reshape(-1, width), patches.reshape(-1, width), flags
    )
    weight_outs = [g.T if turned else g for g, turned in zip(weight_grads, TURNED)]
    return (
        layer_out,
        text_grad,
        patch_grad,
        *weight_outs,
        *(norm_outs[i] for i in range(6)),
    )


def solution(mesh):
    tokens = P("dp", "mp", None)
    rows, columns = P("dp", "mp"), P("mp", "dp")
    kinds = (rows, rows, rows, columns, rows, rows, rows, columns, rows, columns)
    in_specs = (tokens, P("dp", None, None), P("dp"), *kinds, *([P()] * 6), tokens)
    out_specs = (tokens, tokens, tokens, *kinds, *([P()] * 6))
    return jax.shard_map(body, mesh=mesh, in_specs=in_specs, out_specs=out_specs, check_vma=False)
```

```python
import functools

import jax
import jax.numpy as jnp
from jax import lax
from jax.experimental import pallas as pl
from jax.experimental.pallas import tpu as pltpu
from jax.sharding import PartitionSpec as P

HD = 64
D = 768
GROUP = 256
ROWS = 1152
LEN = 64
PATCH = 576
SMALLP = 196
BOTH = ("dp", "mp")

epsilon = 1e-05
masked_score = -1000000000.0
bf16 = jnp.bfloat16
f32 = jnp.float32


def dot(left, right, left_dim, right_dim):
    return lax.dot_general(left, right, (((left_dim,), (right_dim,)), ((), ())), preferred_element_type=f32)


def matmul(left, right):
    return dot(left, right, 1, 0)


def matmul_t(left, right):
    return dot(left, right, 1, 1)


def weight_grad(left, right):
    return dot(left, right, 0, 0)


def norm_stats(value):
    average = jnp.mean(value, axis=-1, keepdims=True)
    centred = value - average
    spread = jnp.mean(centred * centred, axis=-1, keepdims=True)
    inverse = lax.rsqrt(spread + epsilon)
    return centred * inverse, inverse


def norm_back(normal, inverse, gain, grad):
    scaled = grad * gain
    mean_one = jnp.mean(scaled, axis=-1, keepdims=True)
    mean_two = jnp.mean(scaled * normal, axis=-1, keepdims=True)
    grad_value = (scaled - mean_one - normal * mean_two) * inverse
    return grad_value, jnp.sum(grad * normal, axis=0, keepdims=True), jnp.sum(grad, axis=0, keepdims=True)


def spread(rows):
    head = lax.broadcasted_iota(jnp.int32, rows.shape, 1) // HD
    zero = jnp.zeros_like(rows)
    return jnp.concatenate([jnp.where(head == h, rows, zero) for h in range(rows.shape[1] // HD)], axis=0)


def collect(blocks):
    count = blocks.shape[1] // HD
    length = blocks.shape[0] // count
    head = lax.broadcasted_iota(jnp.int32, (length, blocks.shape[1]), 1) // HD
    total = blocks[:length]
    for h in range(1, count):
        total = jnp.where(head == h, blocks[h * length : (h + 1) * length], total)
    return total


def groups(width):
    return [slice(start, start + GROUP) for start in range(0, width, GROUP)]


def attend_kernel(causal, batch, flag_ref, query_ref, key_ref, value_ref, mix_ref, prob_ref):
    keys = key_ref.shape[0] // batch
    shape = (keys, GROUP // HD * LEN)
    row = lax.broadcasted_iota(jnp.int32, shape, 0)
    for n in range(batch):
        ask, see = slice(n * LEN, (n + 1) * LEN), slice(n * keys, (n + 1) * keys)
        if causal:
            allowed = row <= lax.broadcasted_iota(jnp.int32, shape, 1) % LEN
        else:
            allowed = row < SMALLP + (PATCH - SMALLP) * flag_ref[pl.program_id(0) * batch + n]
        for part in groups(query_ref.shape[1]):
            queries = spread(query_ref[ask, part]) * jnp.asarray(HD ** (-0.5), bf16)
            scores = jnp.where(allowed, dot(key_ref[see, part], queries, 1, 1), masked_score)
            exponent = jnp.exp(scores - jnp.max(scores, axis=0, keepdims=True))
            probs = (exponent * (1.0 / jnp.sum(exponent, axis=0, keepdims=True))).astype(bf16)
            prob_ref[see, part] = probs
            mix_ref[ask, part] = collect(dot(probs, value_ref[see, part], 0, 0)).astype(bf16)


def attend_back_kernel(batch, query_ref, key_ref, value_ref, prob_ref, grad_ref, *outs):
    width = query_ref.shape[1]
    keys = key_ref.shape[0] // batch
    joined = outs[-1]
    query_out, shift = (outs[0], 0) if len(outs) == 2 else (joined, width)
    for n in range(batch):
        ask, see = slice(n * LEN, (n + 1) * LEN), slice(n * keys, (n + 1) * keys)
        for part in groups(width):
            queries = spread(query_ref[ask, part]) * jnp.asarray(HD ** (-0.5), bf16)
            grads = spread(grad_ref[ask, part])
            probs_low = prob_ref[see, part]
            probs = probs_low.astype(f32)
            grad_prob = dot(value_ref[see, part], grads, 1, 1)
            inner = jnp.sum(probs * grad_prob, axis=0, keepdims=True)
            grad_score = (probs * (grad_prob - inner)).astype(bf16)
            key_part = slice(shift + part.start, shift + part.stop)
            value_part = slice(shift + width + part.start, shift + width + part.stop)
            joined[see, value_part] = dot(probs_low, grads, 1, 0).astype(bf16)
            joined[see, key_part] = dot(grad_score, queries, 1, 0).astype(bf16)
            query_out[ask, part] = (collect(dot(grad_score, key_ref[see, part], 0, 0)) * HD ** (-0.5)).astype(bf16)


def column(rows, width):
    return pl.BlockSpec((rows, width), lambda i, *_: (i, 0))


def attend_cost(queries, count, keys, products):
    if keys == LEN and products == 4:
        return pl.CostEstimate(flops=2**20, bytes_accessed=2**20, transcendentals=0)
    flops = 2 * products * count * LEN * keys * D * GROUP // HD
    return pl.CostEstimate(flops=flops, bytes_accessed=products * 2 * count * keys * D, transcendentals=0)


def batch_of(count, keys):
    for batch in (8, 4, 2):
        if count % batch == 0 and batch * keys <= ROWS:
            return batch
    return 1


def attend(queries, sources, values, flags, count, causal):
    keys = sources.shape[0] // count
    batch = batch_of(count, keys)
    ask, see, width = batch * LEN, batch * keys, D
    grid_spec = pltpu.PrefetchScalarGridSpec(
        num_scalar_prefetch=1,
        grid=(count // batch,),
        in_specs=[column(ask, width), column(see, width), column(see, width)],
        out_specs=[column(ask, width), column(see, width)],
    )
    return pl.pallas_call(
        functools.partial(attend_kernel, causal, batch),
        grid_spec=grid_spec,
        out_shape=(
            jax.ShapeDtypeStruct((count * LEN, width), bf16),
            jax.ShapeDtypeStruct((count * keys, width), bf16),
        ),
        cost_estimate=attend_cost(queries, count, keys, 2),
    )(flags, queries, sources, values)


def attend_back(queries, sources, values, probs, grad_mix, count, whole):
    keys = sources.shape[0] // count
    batch = batch_of(count, keys)
    ask, see, width = batch * LEN, batch * keys, D
    widths = [(keys, 3 * width)] if whole else [(LEN, width), (keys, 2 * width)]
    return pl.pallas_call(
        functools.partial(attend_back_kernel, batch),
        grid=(count // batch,),
        in_specs=[
            column(ask, width),
            column(see, width),
            column(see, width),
            column(see, width),
            column(ask, width),
        ],
        out_specs=[column(batch * rows, wide) for rows, wide in widths],
        out_shape=[jax.ShapeDtypeStruct((count * rows, wide), bf16) for rows, wide in widths],
        cost_estimate=attend_cost(queries, count, keys, 4),
    )(queries, sources, values, probs, grad_mix)


def swap(rows):
    return lax.ppermute(rows, "mp", [(0, 1), (1, 0)])


def patch_kernel(side_ref, grad_ref, key_ref, value_ref, out_ref):
    width = key_ref.shape[1]
    for n in range(grad_ref.shape[0]):
        product = dot(grad_ref[n, :, :width], key_ref[...], 1, 1) + dot(grad_ref[n, :, width:], value_ref[...], 1, 1)
        out_ref[n] = product.astype(out_ref.dtype)


def patch_product(grads, key_w, value_w, first, last, half, place_at, total, kind):
    batch = 2 - (last - first) % 2
    rows = PATCH // 2
    width, depth = key_w.shape[0], 2 * key_w.shape[1]
    grid_spec = pltpu.PrefetchScalarGridSpec(
        num_scalar_prefetch=1,
        grid=((last - first) // batch,),
        in_specs=[
            pl.BlockSpec((batch, rows, depth), lambda i, at: (i + first // batch, at[0], 0)),
            pl.BlockSpec(key_w.shape, lambda i, at: (0, 0)),
            pl.BlockSpec(value_w.shape, lambda i, at: (0, 0)),
        ],
        out_specs=pl.BlockSpec((batch, rows, width), lambda i, at: (i + at[1] // batch, 0, 0)),
    )
    flops = 2**20
    return pl.pallas_call(
        patch_kernel,
        grid_spec=grid_spec,
        out_shape=jax.ShapeDtypeStruct((total, rows, width), kind),
        cost_estimate=pl.CostEstimate(flops=flops, bytes_accessed=flops // width, transcendentals=0),
    )(jnp.stack([half, place_at]), grads.reshape(-1, PATCH, depth), key_w, value_w)


def widen_kernel(first, side_ref, early_ref, late_ref, whole_ref, out_ref):
    early = pl.program_id(0) < first

    @pl.when(early)
    def _():
        out_ref[...] = early_ref[...].astype(f32)

    @pl.when(jnp.logical_not(early))
    def _():
        out_ref[...] = late_ref[...].astype(f32)


def widen(early, late, whole, place_at):
    count, height, width = early.shape
    grid_spec = pltpu.PrefetchScalarGridSpec(
        num_scalar_prefetch=1,
        grid=(count + late.shape[0],),
        in_specs=[
            pl.BlockSpec((1, height, width), lambda i, at: (jnp.minimum(i, count - 1), 0, 0)),
            pl.BlockSpec((1, height, width), lambda i, at: (jnp.maximum(i - count, 0), 0, 0)),
            pl.BlockSpec(memory_space=pl.ANY),
        ],
        out_specs=pl.BlockSpec((1, height, width), lambda i, at: (i + at[0], 0, 0)),
    )
    return pl.pallas_call(
        functools.partial(widen_kernel, count),
        grid_spec=grid_spec,
        out_shape=jax.ShapeDtypeStruct(whole.shape, f32),
        input_output_aliases={3: 0},
    )(place_at[None], early, late, whole)


def gelu_parts(value):
    inner = 0.7978845608028654 * (value + 0.044715 * value * value * value)
    bent = jnp.tanh(inner)
    hidden = 0.5 * value * (1.0 + bent)
    slope = 0.5 * (1.0 + bent) + 0.5 * value * (1.0 - bent * bent) * 0.7978845608028654 * (1.0 + 3 * 0.044715 * value * value)
    return hidden, slope


def layer(weights, norms, text, cotangent, patches, resolution):
    count = text.shape[0] // LEN
    query_self, key_self, value_self, mix_self, query_cross, key_cross, value_cross, mix_cross, expand, contract = weights
    first_gain, first_shift, second_gain, second_shift, third_gain, third_shift = norms
    stream = text.astype(f32)
    normal_one, inverse_one = norm_stats(stream)
    normed_one = (normal_one * first_gain + first_shift).astype(bf16)
    queries_one, keys_one, values_one = (matmul(normed_one, w).astype(bf16) for w in (query_self, key_self, value_self))
    mixed_one, probs_one = attend(queries_one, keys_one, values_one, resolution, count, True)
    stream_one = stream + matmul_t(mixed_one, mix_self)
    normal_two, inverse_two = norm_stats(stream_one)
    normed_two = (normal_two * second_gain + second_shift).astype(bf16)
    queries_two = matmul(normed_two, query_cross).astype(bf16)
    keys_two, values_two = (matmul(patches, w).astype(bf16) for w in (key_cross, value_cross))
    mixed_two, probs_two = attend(queries_two, keys_two, values_two, resolution, count, False)
    stream_two = stream_one + matmul_t(mixed_two, mix_cross)
    normal_three, inverse_three = norm_stats(stream_two)
    normed_three = (normal_three * third_gain + third_shift).astype(bf16)
    hidden, slope = gelu_parts(matmul(normed_three, expand))
    hidden = hidden.astype(bf16)
    layer_out = stream_two + matmul_t(hidden, contract)
    grad_pre = (slope * matmul(cotangent, contract)).astype(bf16)
    grad_expand = weight_grad(normed_three, grad_pre)
    grad_contract = weight_grad(cotangent, hidden)
    grad_normed = matmul_t(grad_pre, expand)
    grad_input, gain_three, shift_three = norm_back(normal_three, inverse_three, third_gain, grad_normed)
    grad_stream = cotangent.astype(f32) + grad_input
    grad_rows = grad_stream.astype(bf16)
    grad_mix_cross = weight_grad(grad_rows, mixed_two).astype(bf16)
    grad_expand, grad_contract = grad_expand.astype(bf16), grad_contract.astype(bf16)
    layer_out = layer_out.astype(bf16)
    grad_rows, grad_expand, grad_contract, grad_mix_cross, layer_out = lax.optimization_barrier(
        (grad_rows, grad_expand, grad_contract, grad_mix_cross, layer_out)
    )
    grad_mixed = matmul(grad_rows, mix_cross).astype(bf16)
    grad_queries, grad_sources = attend_back(queries_two, keys_two, values_two, probs_two, grad_mixed, count, False)
    side = lax.axis_index("mp")
    grad_query_cross = weight_grad(normed_two, grad_queries).astype(bf16)
    grad_patch = weight_grad(patches, grad_sources).astype(bf16)
    grad_patch, grad_sources, grad_query_cross = lax.optimization_barrier((grad_patch, grad_sources, grad_query_cross))
    first = count // 2
    early = patch_product(grad_sources, key_cross, value_cross, 0, first, 1 - side, 0 * side, first, bf16)
    early, grad_queries = lax.optimization_barrier((early, grad_queries))
    early = swap(early)
    grad_normed = matmul_t(grad_queries, query_cross)
    grad_input, gain_two, shift_two = norm_back(normal_two, inverse_two, second_gain, grad_normed)
    grad_stream = grad_stream + grad_input
    grad_rows = grad_stream.astype(bf16)
    grad_mix_self = weight_grad(grad_rows, mixed_one)
    grad_mixed = matmul(grad_rows, mix_self).astype(bf16)
    (grad_one,) = attend_back(queries_one, keys_one, values_one, probs_one, grad_mixed, count, True)
    grad_self = weight_grad(normed_one, grad_one)
    grad_normed = sum(matmul_t(grad_one[:, i * D : (i + 1) * D], w) for i, w in enumerate((query_self, key_self, value_self)))
    grad_input, gain_one, shift_one = norm_back(normal_one, inverse_one, first_gain, grad_normed)
    text_grad = (grad_stream + grad_input).astype(bf16)
    norm_grads = [gain_one, shift_one, gain_two, shift_two, gain_three, shift_three]
    grads = [grad_expand, grad_contract, grad_self, grad_mix_self, grad_query_cross, grad_patch, grad_mix_cross]
    early, norm_grads[0] = lax.optimization_barrier((early, norm_grads[0]))
    grads = [g.astype(bf16) for g in grads]
    layer_mine, layer_away = split_positions(layer_out.reshape(count, LEN, D), side)
    text_mine, text_away = split_positions(text_grad.reshape(count, LEN, D), side)
    weight_grads, norm_sums, patch_grad, text_back, layer_back = scatter_grads(
        grads, norm_grads, grad_sources, early, key_cross, value_cross, text_away, layer_away
    )
    layer_out = join_positions(layer_mine, layer_back, side)
    text_grad = join_positions(text_mine, text_back, side).astype(f32)
    return layer_out, text_grad, patch_grad, weight_grads, norm_sums


def split_captions(rows, side):
    half = rows.shape[0] // 2
    return tuple(lax.dynamic_slice_in_dim(rows, at * half, half, 0) for at in (side, 1 - side))


def join_captions(mine, other, side):
    low = jnp.where(side == 0, mine, other)
    high = jnp.where(side == 0, other, mine)
    return jnp.concatenate([low, high], axis=1)


def split_positions(rows, side):
    half = rows.shape[1] // 2
    return tuple(lax.dynamic_slice_in_dim(rows, at * half, half, 1) for at in (side, 1 - side))


def join_positions(mine, other, side):
    first = (jnp.arange(2) == side).reshape(2, 1, 1, 1)
    return jnp.where(first, mine[None], other[None]).reshape(2 * mine.shape[0], *mine.shape[1:])


TURNED = (False, False, False, True, False, False, False, True, False, True)


MESH = pl.DeviceIdType.MESH
DEPTH = 4
BUNDLE = 4


def place():
    index = lax.axis_index("dp")
    return index // 4, index // 2 % 2, index % 2, lax.axis_index("mp")


def greet(z, x, c, y):
    barrier = pltpu.get_barrier_semaphore()

    def hello(z_to, x_to, c_to, y_to):
        pl.semaphore_signal(barrier, inc=1, device_id=(z_to * 4 + x_to * 2 + c_to, y_to), device_id_type=MESH)

    hello(z, 1 - x, c, y)
    hello(z, x, 1 - c, y)
    hello(z, x, c, 1 - y)

    @pl.when(z > 0)
    def _():
        hello(z - 1, x, c, y)

    @pl.when(z < DEPTH - 1)
    def _():
        hello(z + 1, x, c, y)

    pl.semaphore_wait(barrier, 3 + jnp.where(z > 0, 1, 0) + jnp.where(z < DEPTH - 1, 1, 0))


class Bundle:
    def __init__(self, copies, total):
        self.copies, self.total = copies, total

    def start(self):
        for one in self.copies:
            one.start()

    def wait(self):
        self.total.wait()

    def wait_send(self):
        self.total.wait_send()

    def wait_recv(self):
        self.total.wait_recv()


def gather_kernel(att_in, exp_in, con_in, text_in, grad_in, image, *refs):
    att, refs = refs[: att_in.shape[0]], refs[att_in.shape[0] :]
    exp, con, text_out, grad_out, patches, image_buf, own_sem, side_send, up_send, down_send = refs[:10]
    far_send, mate_send, recv, mate_recv, trade_send, trade_recv, load_sem, store_sem = refs[10:]
    z, x, c, y = place()
    half, wide = att_in.shape[2], exp_in.shape[1]
    greet(z, x, c, y)

    def stream(index):
        early = index % 2 == 0
        part = index // 2
        line_first = index == 2

        bundle = range(part * BUNDLE, (part + 1) * BUNDLE)
        whole = att_in.at[pl.ds(part * BUNDLE, BUNDLE)] if early else (exp_in, con_in)[part].at[...]

        def own():
            return [att_in.at[i] for i in bundle] if early else [whole]

        def region(w, z_from, u, core):
            x_from = (x + (w if early else u)) % 2
            y_from = (y + (u if early else w)) % 2
            row = z_from * 4 + x_from * 2 + core
            if early:
                return [att[i].at[row, :, pl.ds(pl.multiple_of(y_from * half, 128), half)] for i in bundle]
            return [(exp, con)[part].at[row, :, pl.ds(pl.multiple_of(y_from * wide, 128), wide)]]

        if early:
            beside, far = (z * 4 + (1 - x) * 2 + c, y), (z * 4 + x * 2 + c, 1 - y)
        else:
            beside, far = (z * 4 + x * 2 + c, 1 - y), (z * 4 + (1 - x) * 2 + c, y)

        def copy(src, dst, send, receive, device):
            def make(one, two):
                return pltpu.make_async_remote_copy(
                    src_ref=one, dst_ref=two, send_sem=send, recv_sem=receive, device_id=device, device_id_type=MESH
                )

            return Bundle([make(one, two) for one, two in zip(src, dst)], make(whole, whole))

        mine = z * 4 + x * 2 + c

        def to_beside(z_from, src):
            return copy(src, region(0, z_from, 0, c), side_send.at[index, z_from], recv.at[index, 1, z_from, 0], beside)

        def to_up(w, z_from, src):
            return copy(src, region(w, z_from, 0, c), up_send.at[index, w, z_from], recv.at[index, w, z_from, 0], (mine + 4, y))

        def to_down(w, z_from, src):
            return copy(src, region(w, z_from, 0, c), down_send.at[index, w, z_from], recv.at[index, w, z_from, 0], (mine - 4, y))

        def to_far(w, z_from, src):
            return copy(src, region(w, z_from, 0, c), far_send.at[index, w, z_from], recv.at[index, w, z_from, 1], far)

        def to_mate(w, z_from, u, src):
            return copy(
                src,
                region(w, z_from, u, c),
                mate_send.at[index, w, z_from, u],
                mate_recv.at[index, w, z_from, u],
                (z * 4 + x * 2 + 1 - c, y),
            )

        def keep():
            def make(one, two):
                return pltpu.make_async_copy(one, two, own_sem.at[index])

            return Bundle([make(one, two) for one, two in zip(own(), region(0, z, 0, c))], make(whole, whole))

        def arrive(w, z_from, u):
            spot = region(w, z_from, u, c)
            copy(spot, spot, far_send.at[index, w, z_from], recv.at[index, w, z_from, u], far).wait_recv()

        def arrive_mate(w, z_from, u):
            spot = region(w, z_from, u, 1 - c)
            copy(spot, spot, far_send.at[index, w, z_from], mate_recv.at[index, w, z_from, u], far).wait_recv()

        def pass_on(w, z_from, src, up, down):
            if w == 0 or not line_first:

                @pl.when(up)
                def _():
                    to_up(w, z_from, src).start()

                @pl.when(down)
                def _():
                    to_down(w, z_from, src).start()

            if w == 0 and line_first:
                to_beside(z_from, src).start()
            to_far(w, z_from, src).start()
            to_mate(w, z_from, 0, src).start()

        def first():
            if not line_first:
                to_beside(z, own()).start()
            pass_on(0, z, own(), z < DEPTH - 1, z > 0)
            keep().start()

        def second():
            arrive(1, z, 0)
            pass_on(1, z, region(1, z, 0, c), z < DEPTH - 1, z > 0)

        def along(w, distance):
            @pl.when(z >= distance)
            def _():
                z_from = z - distance
                arrive(w, z_from, 0)
                pass_on(w, z_from, region(w, z_from, 0, c), z < DEPTH - 1, z < 0)

            @pl.when(z + distance < DEPTH)
            def _():
                z_from = z + distance
                arrive(w, z_from, 0)
                pass_on(w, z_from, region(w, z_from, 0, c), z < 0, z > 0)

        def across(w, z_from):
            arrive(w, z_from, 1)
            to_mate(w, z_from, 1, region(w, z_from, 1, c)).start()

        def across_at(w, distance):
            if distance == 0:
                across(w, z)
                return

            @pl.when(z >= distance)
            def _():
                across(w, z - distance)

            @pl.when(z + distance < DEPTH)
            def _():
                across(w, z + distance)

        def finish():
            keep().wait()
            if not line_first:
                to_beside(z, own()).wait_send()

            def each(number, _):
                w, z_from = number // DEPTH, number % DEPTH
                spot = region(w, z_from, 0, c)
                in_line = (w == 0) if line_first else (w >= 0)

                @pl.when(in_line & (z < DEPTH - 1) & (z_from <= z))
                def _():
                    to_up(w, z_from, spot).wait_send()

                @pl.when(in_line & (z > 0) & (z_from >= z))
                def _():
                    to_down(w, z_from, spot).wait_send()

                if line_first:

                    @pl.when(w == 0)
                    def _():
                        to_beside(z_from, spot).wait_send()

                to_far(w, z_from, spot).wait_send()
                for u in range(2):
                    to_mate(w, z_from, u, spot).wait_send()
                    arrive_mate(w, z_from, u)
                return 0

            lax.fori_loop(0, 2 * DEPTH, each, 0)

        return first, second, along, across_at, finish

    def trade(k):
        src, dst = ((text_in, text_out), (grad_in, grad_out))[k]
        return pltpu.make_async_remote_copy(
            src_ref=src,
            dst_ref=dst,
            send_sem=trade_send.at[k],
            recv_sem=trade_recv.at[k],
            device_id=(z * 4 + x * 2 + c, 1 - y),
            device_id_type=MESH,
        )

    count = patches.shape[0]

    def load(n):
        return pltpu.make_async_copy(image.at[y * count + n], image_buf.at[n], load_sem.at[n])

    def store(n):
        return pltpu.make_async_copy(image_buf.at[n], patches.at[n], store_sem.at[n])

    streams = [stream(index) for index in range(4)]
    for first, _, _, _, _ in streams:
        first()
    for n in range(count):
        load(n).start()
    for _, second, _, _, _ in streams:
        second()
    for k in range(2):
        trade(k).start()
    for n in range(count):
        load(n).wait()
        store(n).start()
    for distance in range(1, DEPTH + 1):
        for w in range(2):
            for _, _, along, across_at, _ in streams:
                if distance < DEPTH:
                    along(w, distance)
                across_at(w, distance - 1)
    for streamed in streams:
        streamed[4]()
    for k in range(2):
        trade(k).wait()
    for n in range(count):
        store(n).wait()


def gather_near(att, exp, con, text, grad, image):
    dp = lax.axis_size("dp")
    count = image.shape[0] // 2
    rows, half, wide = att.shape[1], att.shape[2], exp.shape[1]
    vmem = pl.BlockSpec(memory_space=pltpu.VMEM)
    anywhere = pl.BlockSpec(memory_space=pl.ANY)
    dma = pltpu.SemaphoreType.DMA
    return pl.pallas_call(
        gather_kernel,
        in_specs=[vmem] * 3 + [anywhere] * 3,
        out_specs=[anywhere] * (att.shape[0] + 5),
        out_shape=[jax.ShapeDtypeStruct((dp, rows, 2 * half), bf16)] * att.shape[0]
        + [
            jax.ShapeDtypeStruct((dp, rows, 2 * wide), bf16),
            jax.ShapeDtypeStruct((dp, rows, 2 * wide), bf16),
            jax.ShapeDtypeStruct(text.shape, bf16),
            jax.ShapeDtypeStruct(grad.shape, bf16),
            jax.ShapeDtypeStruct((count, *image.shape[1:]), bf16),
        ],
        scratch_shapes=[
            pltpu.VMEM((count, *image.shape[1:]), bf16),
            dma((4,)),
            dma((4, DEPTH)),
            dma((4, 2, DEPTH)),
            dma((4, 2, DEPTH)),
            dma((4, 2, DEPTH)),
            dma((4, 2, DEPTH, 2)),
            dma((4, 2, DEPTH, 2)),
            dma((4, 2, DEPTH, 2)),
            dma((2,)),
            dma((2,)),
            dma((count,)),
            dma((count,)),
        ],
        compiler_params=pltpu.CompilerParams(collective_id=0, has_side_effects=True),
    )(att, exp, con, text, grad, image)


def gather_weights(att, exp, con, text, grad, image):
    count, width = att.shape[0], D
    if lax.axis_size("dp") == 4 * DEPTH:
        *att, exp, con, text, grad, patches = gather_near(att, exp, con, text, grad, image)
        att = [w.reshape(width, -1) for w in att]
        exp, con = exp.reshape(width, -1), con.reshape(width, -1)
    else:
        chunks = exp.shape[1] // att.shape[2]
        narrow = [g[:, j * att.shape[2] : (j + 1) * att.shape[2]] for g in (exp, con) for j in range(chunks)]
        sides = lax.all_gather(att, ("mp", "dp"), axis=1, tiled=True).reshape(count, 2, width, -1)
        att = sides.transpose(0, 2, 1, 3).reshape(count, width, -1)
        sides = lax.all_gather(jnp.stack(narrow), ("mp", "dp"), axis=1, tiled=True).reshape(2, chunks, 2, width, -1)
        exp, con = sides.transpose(0, 3, 2, 1, 4).reshape(2, width, -1)
        text, grad = swap(text), swap(grad)
        patches, _ = split_captions(image, lax.axis_index("mp"))
    return [*(att[i] for i in range(8)), exp, con], text, grad, patches


PIECES = 16
PERIOD = 4
SCATTER_COST = 2**20
SIDE_LAG = 1
NORM_STEP = 2
NORMS = 6


def scatter_kernel(exp, con, own, mix_own, ask, source, mix, *rest):
    norms, rest = rest[:NORMS], rest[NORMS:]
    scatter_body(exp, con, own, mix_own, ask, source, mix, norms, *rest)


def scatter_body(exp, con, own, mix_own, ask, source, mix, norms, early, kept, key_w, value_w, text, result, out, norm_out, whole, text_back, result_back, acc, other, side, low, high, last, total, norm_buf, norm_line, back, sent, sent_in, early_buf, kept_buf, weight_buf, wide, *sems):
    local_sem, mate_send, mate_recv, side_send, side_recv, line_send, low_recv, high_recv, last_send, last_recv, norm_send, norm_recv, away_send, back_recv, load_sem, wide_sem, trade_send, trade_recv = sems
    z, x, c, y = place()
    half = out.shape[2]
    mine = z * 4 + x * 2 + c
    mate = (z * 4 + x * 2 + 1 - c, y)
    greet(z, x, c, y)

    def copy(src, dst, send, receive, device):
        return pltpu.make_async_remote_copy(src_ref=src, dst_ref=dst, send_sem=send, recv_sem=receive, device_id=device, device_id_type=MESH)

    pieces = [(ref, ref.shape[4] // 2, j * half) for ref in (exp, con) for j in range(4)]
    pieces += [(own, half, 0), (own, half, 2 * half), (own, half, 4 * half), (mix_own, half, 0), (ask, half, 0)]
    pieces += [(source, half, 0), (source, half, 2 * half), (mix, half, 0)]

    over_x, over_y = pieces[: PIECES - PIECES // PERIOD], pieces[PIECES - PIECES // PERIOD :]
    for p in range(PIECES):
        odd = p % PERIOD == PERIOD - 1
        ref, stride, offset = over_y[p // PERIOD] if odd else over_x[p // PERIOD * (PERIOD - 1) + p % PERIOD]
        for k in range(2):
            columns = pl.ds(k * stride + offset, half)
            spot = (p, slice(None), k) if odd else (p, slice(None), slice(None), k)
            copy(ref.at[:, :, 1 - c, :, columns], other.at[spot], mate_send.at[p, k], mate_recv.at[p, k], mate).start()
            pltpu.make_async_copy(ref.at[:, :, c, :, columns], acc.at[spot], local_sem.at[p, k]).start()

    count, given = kept.shape[0], back.shape[0]

    def load(n):
        return pltpu.make_async_copy(kept.at[n, y], kept_buf.at[n], load_sem.at[n])

    def load_sent(n):
        return pltpu.make_async_copy(kept.at[count - given + n, 1 - y], sent_in.at[n], load_sem.at[count + 3 + n])

    def load_early():
        return pltpu.make_async_copy(early, early_buf, load_sem.at[count])

    def load_weight(k):
        return pltpu.make_async_copy((key_w, value_w)[k], weight_buf.at[k], load_sem.at[count + 1 + k])

    for k in range(2):
        load_weight(k).start()
    for n in range(given):
        load_sent(n).start()
    for n in range(count):
        load(n).start()
    load_early().start()

    def put(item):
        place_at = jnp.where(item < count, y * count + item, (1 - y) * count + item - count)
        return pltpu.make_async_copy(wide.at[item % 2], whole.at[place_at], wide_sem.at[item % 2])

    def room(item):
        @pl.when(item >= 2)
        def _():
            put(item - 2).wait()

    def product(rows):
        width = weight_buf.shape[1]
        return (dot(rows[:, :width], weight_buf[0], 1, 1) + dot(rows[:, width:], weight_buf[1], 1, 1)).astype(bf16)

    def give(n):
        @pl.when(n == 0)
        def _():
            for k in range(2):
                load_weight(k).wait()

        load_sent(n).wait()
        sent[n] = product(sent_in.at[n])
        for k in range(2):
            part(2 * n + k).start()

    def keep(item):
        load(item).wait()
        room(item)
        wide[item % 2] = product(kept_buf.at[item])
        put(item).start()

    def widen_early(item):
        @pl.when(item == count)
        def _():
            load_early().wait()

        room(item)
        wide[item % 2] = early_buf[item - count]
        put(item).start()

    def widen_late(item):
        n = item - 2 * count + given
        for k in range(2):
            part(2 * n + k).wait_recv()
        room(item)
        wide[item % 2] = back[n]
        put(item).start()

    def trade(k):
        src, dst = ((text, text_back), (result, result_back))[k]
        return copy(src, dst, trade_send.at[k], trade_recv.at[k], (mine, 1 - y))

    def part(j):
        rows = sent.shape[1] // 2
        spot = (j // 2, pl.ds(pl.multiple_of(j % 2 * rows, 16), rows))
        return copy(sent.at[spot], back.at[spot], away_send.at[j], back_recv.at[j], (mine, 1 - y))

    def kind(p):
        odd = jnp.where(p % PERIOD == PERIOD - 1, 1, 0)
        u = x * (1 - odd) + y * odd
        w = y * (1 - odd) + x * odd
        over_x = (z * 4 + (1 - x) * 2 + c, y)
        over_y = (mine, 1 - y)
        first = tuple(one * (1 - odd) + two * odd for one, two in zip(over_x, over_y))
        second = tuple(two * (1 - odd) + one * odd for one, two in zip(over_x, over_y))
        return u, w, first, second

    def to_mate(p, k):
        return copy(other.at[p, :, k], other.at[p, :, k], mate_send.at[p, k], mate_recv.at[p, k], mate)

    def to_side(p):
        u, w, first, second = kind(p)
        return copy(acc.at[p, :, 1 - u], side.at[p], side_send.at[p], side_recv.at[p], first)

    def to_low(p, unit):
        u, w, first, second = kind(p)
        return copy(acc.at[p, unit, u], low.at[p, unit], line_send.at[p, unit], low_recv.at[p, unit], (mine - 4, y))

    def to_high(p, unit):
        u, w, first, second = kind(p)
        return copy(acc.at[p, unit, u], high.at[p, unit], line_send.at[p, unit], high_recv.at[p, unit], (mine + 4, y))

    def to_last(p):
        u, w, first, second = kind(p)
        return copy(acc.at[p, z, u, 1 - w], last.at[p], last_send.at[p], last_recv.at[p], second)

    def open_piece(p):
        for k in range(2):
            pltpu.make_async_copy(other.at[p, :, k], acc.at[p, :, k], local_sem.at[p, k]).wait()
        for k in range(2):
            to_mate(p, k).wait_recv()

        def add(unit, _):
            acc[p, unit] = (acc[p, unit].astype(f32) + other[p, unit].astype(f32)).astype(bf16)
            return 0

        lax.fori_loop(0, DEPTH, add, 0)
        to_side(p).start()

    def add_side(p):
        u, w, first, second = kind(p)
        to_side(p).wait_recv()

        def add(unit, _):
            acc[p, unit, u] = (acc[p, unit, u].astype(f32) + side[p, unit].astype(f32)).astype(bf16)
            return 0

        lax.fori_loop(0, DEPTH, add, 0)

    def pass_line(p, buffer, inner, has_source, beyond, send):
        u, w, first, second = kind(p)

        def each(unit, _):
            @pl.when(has_source & (beyond(unit) | (unit == z)))
            def _():
                inner(p, unit).wait_recv()

            @pl.when(has_source & beyond(unit))
            def _():
                acc[p, unit, u] = (acc[p, unit, u].astype(f32) + buffer[p, unit].astype(f32)).astype(bf16)

            @pl.when(beyond(unit))
            def _():
                send(p, unit).start()

            return 0

        lax.fori_loop(0, DEPTH, each, 0)

    def close_line(p):
        u, w, first, second = kind(p)
        total[...] = acc[p, z, u].astype(f32)

        @pl.when(z < DEPTH - 1)
        def _():
            total[...] += low[p, z].astype(f32)

        @pl.when(z > 0)
        def _():
            total[...] += high[p, z].astype(f32)

        acc[p, z, u, 1 - w] = total[1 - w].astype(bf16)
        to_last(p).start()
        out[p] = total[w]

    def close_piece(p):
        to_last(p).wait_recv()
        out[p] += last[p].astype(f32)

    def norm_pair(step):
        device = (mate, (z * 4 + (1 - x) * 2 + c, y), (mine, 1 - y))[step]
        return copy(norm_buf.at[step], norm_buf.at[3 + step], norm_send.at[step], norm_recv.at[step], device)

    def norm_up(unit):
        return copy(norm_line.at[unit], norm_line.at[unit], norm_send.at[3 + unit], norm_recv.at[3 + unit], (mine + 4, y))

    def norm_down(unit):
        return copy(norm_line.at[unit], norm_line.at[unit], norm_send.at[3 + DEPTH + unit], norm_recv.at[3 + unit], (mine - 4, y))

    def norm_steps(t):
        @pl.when(t == 0)
        def _():
            norm_buf[0] = jnp.zeros(norm_buf.shape[1:], f32)
            for i, row in enumerate(norms):
                norm_buf[0, i : i + 1] = row[...]
            norm_pair(0).start()

        for step in range(1, 4):

            @pl.when(t == step * NORM_STEP)
            def _():
                norm_pair(step - 1).wait_recv()
                summed = norm_buf[step - 1] + norm_buf[2 + step]
                if step < 3:
                    norm_buf[step] = summed
                    norm_pair(step).start()
                else:
                    norm_line[z] = summed

                    @pl.when(z < DEPTH - 1)
                    def _():
                        norm_up(z).start()

                    @pl.when(z > 0)
                    def _():
                        norm_down(z).start()

        for distance in range(1, DEPTH):

            @pl.when((t == (3 + distance) * NORM_STEP) & (z >= distance))
            def _():
                norm_up(z - distance).wait_recv()

                @pl.when(z < DEPTH - 1)
                def _():
                    norm_up(z - distance).start()

            @pl.when((t == (3 + distance) * NORM_STEP) & (z + distance < DEPTH))
            def _():
                norm_down(z + distance).wait_recv()

                @pl.when(z > 0)
                def _():
                    norm_down(z + distance).start()

    def at(p, work):
        @pl.when((p >= 0) & (p < PIECES))
        def _():
            work(p)

    def step(t, _):
        at(2 * t, open_piece)
        at(2 * t + 1, open_piece)
        @pl.when((t % 3 == 1) & (t < 3 * given))
        def _():
            give(t // 3)

        for k in range(2):

            @pl.when(t == 3 + 4 * k)
            def _():
                trade(k).start()

        at(t - SIDE_LAG, add_side)
        at(
            t - SIDE_LAG - (DEPTH - 1 - z),
            lambda p: pass_line(p, low, to_low, z < DEPTH - 1, lambda unit: unit < z, to_low),
        )
        at(t - SIDE_LAG - z, lambda p: pass_line(p, high, to_high, z > 0, lambda unit: unit > z, to_high))
        norm_steps(t)
        at(t - SIDE_LAG - DEPTH, close_line)
        item = t - 2

        @pl.when((item >= 0) & (item < count))
        def _():
            keep(item)

        @pl.when((item >= count) & (item < 2 * count - given))
        def _():
            widen_early(item)

        @pl.when((item >= 2 * count - given) & (item < 2 * count))
        def _():
            widen_late(item)

        return 0

    def close(p, _):
        close_piece(p)
        return 0

    lax.fori_loop(0, PIECES + SIDE_LAG + DEPTH, step, 0)
    lax.fori_loop(0, PIECES, close, 0)
    for k in range(2):
        trade(k).wait()
    for j in range(2 * given):
        part(j).wait_send()
    for item in (2 * count - 2, 2 * count - 1):
        put(item).wait()
    norm_out[...] = norm_line[0] + norm_line[1] + norm_line[2] + norm_line[3]

    def drain(p, _):
        for k in range(2):
            to_mate(p, k).wait_send()
        to_side(p).wait_send()

        def each(unit, _):
            @pl.when(unit != z)
            def _():
                to_low(p, unit).wait_send()

            return 0

        lax.fori_loop(0, DEPTH, each, 0)
        to_last(p).wait_send()
        return 0

    lax.fori_loop(0, PIECES, drain, 0)
    for index in range(3):
        norm_pair(index).wait_send()
    for unit in range(DEPTH):

        @pl.when((z < DEPTH - 1) & (unit <= z))
        def _():
            norm_up(unit).wait_send()

        @pl.when((z > 0) & (unit >= z))
        def _():
            norm_down(unit).wait_send()


def scatter_near(exp, con, own, mix_own, ask, source, mix, norms, early, kept, key_w, value_w, text, result):
    rows, half = D // (4 * DEPTH), D // 2
    count, height = kept.shape[0], kept.shape[2]
    given = count - early.shape[0]
    grads = [g.reshape(DEPTH, 2, 2, rows, g.shape[1]) for g in (exp, con, own, mix_own, ask, source, mix)]
    vmem = pl.BlockSpec(memory_space=pltpu.VMEM)
    anywhere = pl.BlockSpec(memory_space=pl.ANY)
    dma = pltpu.SemaphoreType.DMA
    return pl.pallas_call(
        scatter_kernel,
        in_specs=[anywhere] * 7 + [vmem] * NORMS + [anywhere] * 6,
        out_specs=[vmem, vmem, anywhere, anywhere, anywhere],
        out_shape=[
            jax.ShapeDtypeStruct((PIECES, rows, half), f32),
            jax.ShapeDtypeStruct((8, D), f32),
            jax.ShapeDtypeStruct((2 * count, height, D), bf16),
            jax.ShapeDtypeStruct(text.shape, bf16),
            jax.ShapeDtypeStruct(result.shape, bf16),
        ],
        scratch_shapes=[
            pltpu.VMEM((PIECES, DEPTH, 2, 2, rows, half), bf16),
            pltpu.VMEM((PIECES, DEPTH, 2, 2, rows, half), bf16),
            pltpu.VMEM((PIECES, DEPTH, 2, rows, half), bf16),
            pltpu.VMEM((PIECES, DEPTH, 2, rows, half), bf16),
            pltpu.VMEM((PIECES, DEPTH, 2, rows, half), bf16),
            pltpu.VMEM((PIECES, rows, half), bf16),
            pltpu.VMEM((2, rows, half), f32),
            pltpu.VMEM((6, 8, D), f32),
            pltpu.VMEM((DEPTH, 8, D), f32),
            pltpu.VMEM((given, height, D), bf16),
            pltpu.VMEM((given, height, D), bf16),
            pltpu.VMEM((given, height, 2 * D), bf16),
            pltpu.VMEM(early.shape, bf16),
            pltpu.VMEM((count, height, 2 * D), bf16),
            pltpu.VMEM((2, D, D), bf16),
            pltpu.VMEM((2, height, D), bf16),
            dma((PIECES, 2)),
            dma((PIECES, 2)),
            dma((PIECES, 2)),
            dma((PIECES,)),
            dma((PIECES,)),
            dma((PIECES, DEPTH)),
            dma((PIECES, DEPTH)),
            dma((PIECES, DEPTH)),
            dma((PIECES,)),
            dma((PIECES,)),
            dma((3 + 2 * DEPTH,)),
            dma((3 + DEPTH,)),
            dma((2 * given,)),
            dma((2 * given,)),
            dma((count + 3 + given,)),
            dma((2,)),
            dma((2,)),
            dma((2,)),
        ],
        cost_estimate=pl.CostEstimate(flops=0, bytes_accessed=SCATTER_COST, transcendentals=0),
        compiler_params=pltpu.CompilerParams(collective_id=1, has_side_effects=True, vmem_limit_bytes=60 * 2**20),
    )(*grads, *norms, early, kept, key_w, value_w, text, result)


def scatter_grads(grads, norms, sources, early, key_w, value_w, text, result):
    exp, con, own, mix_own, ask, source, mix = grads
    count = sources.shape[0] // PATCH
    if lax.axis_size("dp") == 4 * DEPTH:
        kept = sources.reshape(count, 2, PATCH // 2, -1)
        parts, norm_sums, whole, text, result = scatter_near(*grads, norms, early, kept, key_w, value_w, text, result)
        odd = [p % PERIOD == PERIOD - 1 for p in range(PIECES)]
        ordered = [parts[p] for p in range(PIECES) if not odd[p]] + [parts[p] for p in range(PIECES) if odd[p]]
        exp, con = (jnp.concatenate(part, axis=1) for part in (ordered[:4], ordered[4:8]))
        return [*ordered[8:], exp, con], norm_sums, whole.astype(f32), text, result
    side = lax.axis_index("mp")
    whole = patch_product(sources, key_w, value_w, 0, count, side, side * count, 2 * count, f32)
    first = early.shape[0]
    late = patch_product(sources, key_w, value_w, first, count, 1 - side, 0 * side, count - first, bf16)
    whole = widen(early, swap(late), whole, (1 - side) * count)
    sides = []
    for g in (own, mix_own, ask, source, mix):
        sides.append(g.reshape(D, g.shape[1] // D, 2, D // 2).transpose(1, 2, 0, 3))
    for g in (exp, con):
        sides.append(g.reshape(D, 2, g.shape[1] // D, D // 2).transpose(2, 1, 0, 3))
    stacked = jnp.concatenate(sides).reshape(-1, 2 * D, D // 2)
    parts = lax.psum_scatter(stacked, ("mp", "dp"), scatter_dimension=1, tiled=True).astype(f32)
    chunks = (parts.shape[0] - 8) // 2
    exp, con = (jnp.concatenate(list(parts[start : start + chunks]), axis=1) for start in (8, 8 + chunks))
    return [*(parts[i] for i in range(8)), exp, con], lax.psum(jnp.concatenate(norms), BOTH), whole, swap(text), swap(result)


def body(text_tokens, image_tokens, resolution, *rest):
    shards, norms, cotangent = rest[:10], rest[10:16], rest[16]
    side = lax.axis_index("mp")
    half = text_tokens.shape[0] // 2
    width = text_tokens.shape[2]
    flat = [shard.T if turned else shard for shard, turned in zip(shards, TURNED)]
    text_mine, text_away = split_captions(text_tokens, side)
    grad_mine, grad_away = split_captions(cotangent, side)
    weights, text_back, grad_back, patches = gather_weights(
        jnp.stack(flat[:8]), flat[8], flat[9], text_away, grad_away, image_tokens
    )
    text = join_captions(text_mine, text_back, side)
    grad_out = join_captions(grad_mine, grad_back, side)
    flags = lax.dynamic_slice_in_dim(resolution, side * half, half, 0)
    layer_out, text_grad, patch_grad, weight_grads, norm_outs = layer(
        weights, norms, text.reshape(-1, width), grad_out.reshape(-1, width), patches.reshape(-1, width), flags
    )
    weight_outs = [g.T if turned else g for g, turned in zip(weight_grads, TURNED)]
    return (
        layer_out,
        text_grad,
        patch_grad,
        *weight_outs,
        *(norm_outs[i] for i in range(6)),
    )


def solution(mesh):
    tokens = P("dp", "mp", None)
    rows, columns = P("dp", "mp"), P("mp", "dp")
    kinds = (rows, rows, rows, columns, rows, rows, rows, columns, rows, columns)
    in_specs = (tokens, P("dp", None, None), P("dp"), *kinds, *([P()] * 6), tokens)
    out_specs = (tokens, tokens, tokens, *kinds, *([P()] * 6))
    return jax.shard_map(body, mesh=mesh, in_specs=in_specs, out_specs=out_specs, check_vma=False)
```

```python
import functools

import jax
import jax.numpy as jnp
from jax import lax
from jax.experimental import pallas as pl
from jax.experimental.pallas import tpu as pltpu
from jax.sharding import PartitionSpec as P

HD = 64
D = 768
GROUP = 256
ROWS = 1152
LEN = 64
PATCH = 576
SMALLP = 196
BOTH = ("dp", "mp")

epsilon = 1e-05
masked_score = -1000000000.0
bf16 = jnp.bfloat16
f32 = jnp.float32


def dot(left, right, left_dim, right_dim):
    return lax.dot_general(left, right, (((left_dim,), (right_dim,)), ((), ())), preferred_element_type=f32)


def matmul(left, right):
    return dot(left, right, 1, 0)


def matmul_t(left, right):
    return dot(left, right, 1, 1)


def weight_grad(left, right):
    return dot(left, right, 0, 0)


def norm_stats(value):
    average = jnp.mean(value, axis=-1, keepdims=True)
    centred = value - average
    spread = jnp.mean(centred * centred, axis=-1, keepdims=True)
    inverse = lax.rsqrt(spread + epsilon)
    return centred * inverse, inverse


def norm_back(normal, inverse, gain, grad):
    scaled = grad * gain
    mean_one = jnp.mean(scaled, axis=-1, keepdims=True)
    mean_two = jnp.mean(scaled * normal, axis=-1, keepdims=True)
    grad_value = (scaled - mean_one - normal * mean_two) * inverse
    return grad_value, jnp.sum(grad * normal, axis=0, keepdims=True), jnp.sum(grad, axis=0, keepdims=True)


def spread(rows):
    head = lax.broadcasted_iota(jnp.int32, rows.shape, 1) // HD
    zero = jnp.zeros_like(rows)
    return jnp.concatenate([jnp.where(head == h, rows, zero) for h in range(rows.shape[1] // HD)], axis=0)


def collect(blocks):
    count = blocks.shape[1] // HD
    length = blocks.shape[0] // count
    head = lax.broadcasted_iota(jnp.int32, (length, blocks.shape[1]), 1) // HD
    total = blocks[:length]
    for h in range(1, count):
        total = jnp.where(head == h, blocks[h * length : (h + 1) * length], total)
    return total


def groups(width):
    return [slice(start, start + GROUP) for start in range(0, width, GROUP)]


def attend_kernel(causal, batch, flag_ref, query_ref, key_ref, value_ref, mix_ref, prob_ref):
    keys = key_ref.shape[0] // batch
    shape = (keys, GROUP // HD * LEN)
    row = lax.broadcasted_iota(jnp.int32, shape, 0)
    for n in range(batch):
        ask, see = slice(n * LEN, (n + 1) * LEN), slice(n * keys, (n + 1) * keys)
        if causal:
            allowed = row <= lax.broadcasted_iota(jnp.int32, shape, 1) % LEN
        else:
            allowed = row < SMALLP + (PATCH - SMALLP) * flag_ref[pl.program_id(0) * batch + n]
        for part in groups(query_ref.shape[1]):
            queries = spread(query_ref[ask, part]) * jnp.asarray(HD ** (-0.5), bf16)
            scores = jnp.where(allowed, dot(key_ref[see, part], queries, 1, 1), masked_score)
            exponent = jnp.exp(scores - jnp.max(scores, axis=0, keepdims=True))
            probs = (exponent * (1.0 / jnp.sum(exponent, axis=0, keepdims=True))).astype(bf16)
            prob_ref[see, part] = probs
            mix_ref[ask, part] = collect(dot(probs, value_ref[see, part], 0, 0)).astype(bf16)


def attend_back_kernel(batch, query_ref, key_ref, value_ref, prob_ref, grad_ref, *outs):
    width = query_ref.shape[1]
    keys = key_ref.shape[0] // batch
    joined = outs[-1]
    query_out, shift = (outs[0], 0) if len(outs) == 2 else (joined, width)
    for n in range(batch):
        ask, see = slice(n * LEN, (n + 1) * LEN), slice(n * keys, (n + 1) * keys)
        for part in groups(width):
            queries = spread(query_ref[ask, part]) * jnp.asarray(HD ** (-0.5), bf16)
            grads = spread(grad_ref[ask, part])
            probs_low = prob_ref[see, part]
            probs = probs_low.astype(f32)
            grad_prob = dot(value_ref[see, part], grads, 1, 1)
            inner = jnp.sum(probs * grad_prob, axis=0, keepdims=True)
            grad_score = (probs * (grad_prob - inner)).astype(bf16)
            key_part = slice(shift + part.start, shift + part.stop)
            value_part = slice(shift + width + part.start, shift + width + part.stop)
            joined[see, value_part] = dot(probs_low, grads, 1, 0).astype(bf16)
            joined[see, key_part] = dot(grad_score, queries, 1, 0).astype(bf16)
            query_out[ask, part] = (collect(dot(grad_score, key_ref[see, part], 0, 0)) * HD ** (-0.5)).astype(bf16)


def column(rows, width):
    return pl.BlockSpec((rows, width), lambda i, *_: (i, 0))


def attend_cost(queries, count, keys, products):
    if keys == LEN and products == 4:
        return pl.CostEstimate(flops=2**20, bytes_accessed=2**20, transcendentals=0)
    flops = 2 * products * count * LEN * keys * D * GROUP // HD
    return pl.CostEstimate(flops=flops, bytes_accessed=products * 2 * count * keys * D, transcendentals=0)


def batch_of(count, keys):
    for batch in (8, 4, 2):
        if count % batch == 0 and batch * keys <= ROWS:
            return batch
    return 1


def attend(queries, sources, values, flags, count, causal):
    keys = sources.shape[0] // count
    batch = batch_of(count, keys)
    ask, see, width = batch * LEN, batch * keys, D
    grid_spec = pltpu.PrefetchScalarGridSpec(
        num_scalar_prefetch=1,
        grid=(count // batch,),
        in_specs=[column(ask, width), column(see, width), column(see, width)],
        out_specs=[column(ask, width), column(see, width)],
    )
    return pl.pallas_call(
        functools.partial(attend_kernel, causal, batch),
        grid_spec=grid_spec,
        out_shape=(
            jax.ShapeDtypeStruct((count * LEN, width), bf16),
            jax.ShapeDtypeStruct((count * keys, width), bf16),
        ),
        cost_estimate=attend_cost(queries, count, keys, 2),
    )(flags, queries, sources, values)


def attend_back(queries, sources, values, probs, grad_mix, count, whole):
    keys = sources.shape[0] // count
    batch = batch_of(count, keys)
    ask, see, width = batch * LEN, batch * keys, D
    widths = [(keys, 3 * width)] if whole else [(LEN, width), (keys, 2 * width)]
    return pl.pallas_call(
        functools.partial(attend_back_kernel, batch),
        grid=(count // batch,),
        in_specs=[
            column(ask, width),
            column(see, width),
            column(see, width),
            column(see, width),
            column(ask, width),
        ],
        out_specs=[column(batch * rows, wide) for rows, wide in widths],
        out_shape=[jax.ShapeDtypeStruct((count * rows, wide), bf16) for rows, wide in widths],
        cost_estimate=attend_cost(queries, count, keys, 4),
    )(queries, sources, values, probs, grad_mix)


def swap(rows):
    return lax.ppermute(rows, "mp", [(0, 1), (1, 0)])


def patch_kernel(side_ref, grad_ref, key_ref, value_ref, out_ref):
    width = key_ref.shape[1]
    rows = grad_ref[...].reshape(-1, 2 * width)
    product = dot(rows[:, :width], key_ref[...], 1, 1) + dot(rows[:, width:], value_ref[...], 1, 1)
    out_ref[...] = product.astype(out_ref.dtype).reshape(out_ref.shape)


def patch_product(grads, key_w, value_w, first, last, half, place_at, total, kind):
    batch = 2 - (last - first) % 2
    rows = PATCH // 2
    width, depth = key_w.shape[0], 2 * key_w.shape[1]
    grid_spec = pltpu.PrefetchScalarGridSpec(
        num_scalar_prefetch=1,
        grid=((last - first) // batch,),
        in_specs=[
            pl.BlockSpec((batch, rows, depth), lambda i, at: (i + first // batch, at[0], 0)),
            pl.BlockSpec(key_w.shape, lambda i, at: (0, 0)),
            pl.BlockSpec(value_w.shape, lambda i, at: (0, 0)),
        ],
        out_specs=pl.BlockSpec((batch, rows, width), lambda i, at: (i + at[1] // batch, 0, 0)),
    )
    flops = 2**20
    return pl.pallas_call(
        patch_kernel,
        grid_spec=grid_spec,
        out_shape=jax.ShapeDtypeStruct((total, rows, width), kind),
        cost_estimate=pl.CostEstimate(flops=flops, bytes_accessed=flops // width, transcendentals=0),
    )(jnp.stack([half, place_at]), grads.reshape(-1, PATCH, depth), key_w, value_w)


def widen_kernel(first, side_ref, early_ref, late_ref, whole_ref, out_ref):
    early = pl.program_id(0) < first

    @pl.when(early)
    def _():
        out_ref[...] = early_ref[...].astype(f32)

    @pl.when(jnp.logical_not(early))
    def _():
        out_ref[...] = late_ref[...].astype(f32)


def widen(early, late, whole, place_at):
    count, height, width = early.shape
    grid_spec = pltpu.PrefetchScalarGridSpec(
        num_scalar_prefetch=1,
        grid=(count + late.shape[0],),
        in_specs=[
            pl.BlockSpec((1, height, width), lambda i, at: (jnp.minimum(i, count - 1), 0, 0)),
            pl.BlockSpec((1, height, width), lambda i, at: (jnp.maximum(i - count, 0), 0, 0)),
            pl.BlockSpec(memory_space=pl.ANY),
        ],
        out_specs=pl.BlockSpec((1, height, width), lambda i, at: (i + at[0], 0, 0)),
    )
    return pl.pallas_call(
        functools.partial(widen_kernel, count),
        grid_spec=grid_spec,
        out_shape=jax.ShapeDtypeStruct(whole.shape, f32),
        input_output_aliases={3: 0},
    )(place_at[None], early, late, whole)


def gelu_parts(value):
    inner = 0.7978845608028654 * (value + 0.044715 * value * value * value)
    bent = jnp.tanh(inner)
    hidden = 0.5 * value * (1.0 + bent)
    slope = 0.5 * (1.0 + bent) + 0.5 * value * (1.0 - bent * bent) * 0.7978845608028654 * (1.0 + 3 * 0.044715 * value * value)
    return hidden, slope


def layer(weights, norms, text, cotangent, patches, resolution):
    count = text.shape[0] // LEN
    query_self, key_self, value_self, mix_self, query_cross, key_cross, value_cross, mix_cross, expand, contract = weights
    first_gain, first_shift, second_gain, second_shift, third_gain, third_shift = norms
    stream = text.astype(f32)
    normal_one, inverse_one = norm_stats(stream)
    normed_one = (normal_one * first_gain + first_shift).astype(bf16)
    queries_one, keys_one, values_one = (matmul(normed_one, w).astype(bf16) for w in (query_self, key_self, value_self))
    mixed_one, probs_one = attend(queries_one, keys_one, values_one, resolution, count, True)
    stream_one = stream + matmul_t(mixed_one, mix_self)
    normal_two, inverse_two = norm_stats(stream_one)
    normed_two = (normal_two * second_gain + second_shift).astype(bf16)
    queries_two = matmul(normed_two, query_cross).astype(bf16)
    keys_two, values_two = (matmul(patches, w).astype(bf16) for w in (key_cross, value_cross))
    mixed_two, probs_two = attend(queries_two, keys_two, values_two, resolution, count, False)
    stream_two = stream_one + matmul_t(mixed_two, mix_cross)
    normal_three, inverse_three = norm_stats(stream_two)
    normed_three = (normal_three * third_gain + third_shift).astype(bf16)
    hidden, slope = gelu_parts(matmul(normed_three, expand))
    hidden = hidden.astype(bf16)
    layer_out = stream_two + matmul_t(hidden, contract)
    grad_pre = (slope * matmul(cotangent, contract)).astype(bf16)
    grad_expand = weight_grad(normed_three, grad_pre)
    grad_contract = weight_grad(cotangent, hidden)
    grad_normed = matmul_t(grad_pre, expand)
    grad_input, gain_three, shift_three = norm_back(normal_three, inverse_three, third_gain, grad_normed)
    grad_stream = cotangent.astype(f32) + grad_input
    grad_rows = grad_stream.astype(bf16)
    grad_mix_cross = weight_grad(grad_rows, mixed_two).astype(bf16)
    grad_expand, grad_contract = grad_expand.astype(bf16), grad_contract.astype(bf16)
    layer_out = layer_out.astype(bf16)
    grad_rows, grad_expand, grad_contract, grad_mix_cross, layer_out = lax.optimization_barrier(
        (grad_rows, grad_expand, grad_contract, grad_mix_cross, layer_out)
    )
    grad_mixed = matmul(grad_rows, mix_cross).astype(bf16)
    grad_queries, grad_sources = attend_back(queries_two, keys_two, values_two, probs_two, grad_mixed, count, False)
    side = lax.axis_index("mp")
    grad_query_cross = weight_grad(normed_two, grad_queries).astype(bf16)
    grad_patch = weight_grad(patches, grad_sources).astype(bf16)
    grad_patch, grad_sources, grad_query_cross = lax.optimization_barrier((grad_patch, grad_sources, grad_query_cross))
    first = count // 2
    early = patch_product(grad_sources, key_cross, value_cross, 0, first, 1 - side, 0 * side, first, bf16)
    early, grad_queries = lax.optimization_barrier((early, grad_queries))
    early = swap(early)
    grad_normed = matmul_t(grad_queries, query_cross)
    grad_input, gain_two, shift_two = norm_back(normal_two, inverse_two, second_gain, grad_normed)
    grad_stream = grad_stream + grad_input
    grad_rows = grad_stream.astype(bf16)
    grad_mix_self = weight_grad(grad_rows, mixed_one)
    grad_mixed = matmul(grad_rows, mix_self).astype(bf16)
    (grad_one,) = attend_back(queries_one, keys_one, values_one, probs_one, grad_mixed, count, True)
    grad_self = weight_grad(normed_one, grad_one)
    grad_normed = sum(matmul_t(grad_one[:, i * D : (i + 1) * D], w) for i, w in enumerate((query_self, key_self, value_self)))
    grad_input, gain_one, shift_one = norm_back(normal_one, inverse_one, first_gain, grad_normed)
    text_grad = (grad_stream + grad_input).astype(bf16)
    norm_grads = [gain_one, shift_one, gain_two, shift_two, gain_three, shift_three]
    grads = [grad_expand, grad_contract, grad_self, grad_mix_self, grad_query_cross, grad_patch, grad_mix_cross]
    early, norm_grads[0] = lax.optimization_barrier((early, norm_grads[0]))
    grads = [g.astype(bf16) for g in grads]
    layer_out, text_grad = (rows.reshape(count, LEN, D) for rows in (layer_out, text_grad))
    layer_mine, _ = split_positions(layer_out, side)
    text_mine, _ = split_positions(text_grad, side)
    weight_grads, norm_sums, patch_grad, text_back, layer_back = scatter_grads(
        grads, norm_grads, grad_sources, early, key_cross, value_cross, text_grad, layer_out
    )
    layer_out = join_positions(layer_mine, layer_back, side)
    text_grad = join_positions(text_mine, text_back, side).astype(f32)
    return layer_out, text_grad, patch_grad, weight_grads, norm_sums


def split_captions(rows, side):
    half = rows.shape[0] // 2
    return tuple(lax.dynamic_slice_in_dim(rows, at * half, half, 0) for at in (side, 1 - side))


def join_captions(mine, other, side):
    low = jnp.where(side == 0, mine, other)
    high = jnp.where(side == 0, other, mine)
    return jnp.concatenate([low, high], axis=1)


def split_positions(rows, side):
    half = rows.shape[1] // 2
    return tuple(lax.dynamic_slice_in_dim(rows, at * half, half, 1) for at in (side, 1 - side))


def join_positions(mine, other, side):
    first = (jnp.arange(2) == side).reshape(2, 1, 1, 1)
    return jnp.where(first, mine[None], other[None]).reshape(2 * mine.shape[0], *mine.shape[1:])


TURNED = (False, False, False, True, False, False, False, True, False, True)


MESH = pl.DeviceIdType.MESH
DEPTH = 4
BUNDLE = 4


def place():
    index = lax.axis_index("dp")
    return index // 4, index // 2 % 2, index % 2, lax.axis_index("mp")


def greet(z, x, c, y):
    barrier = pltpu.get_barrier_semaphore()

    def hello(z_to, x_to, c_to, y_to):
        pl.semaphore_signal(barrier, inc=1, device_id=(z_to * 4 + x_to * 2 + c_to, y_to), device_id_type=MESH)

    hello(z, 1 - x, c, y)
    hello(z, x, 1 - c, y)
    hello(z, x, c, 1 - y)

    @pl.when(z > 0)
    def _():
        hello(z - 1, x, c, y)

    @pl.when(z < DEPTH - 1)
    def _():
        hello(z + 1, x, c, y)

    pl.semaphore_wait(barrier, 3 + jnp.where(z > 0, 1, 0) + jnp.where(z < DEPTH - 1, 1, 0))


class Bundle:
    def __init__(self, copies, total):
        self.copies, self.total = copies, total

    def start(self):
        for one in self.copies:
            one.start()

    def wait(self):
        self.total.wait()

    def wait_send(self):
        self.total.wait_send()

    def wait_recv(self):
        self.total.wait_recv()


def gather_kernel(att_in, exp_in, con_in, text_in, grad_in, image, *refs):
    att, refs = refs[: att_in.shape[0]], refs[att_in.shape[0] :]
    exp, con, text_out, grad_out, patches, image_buf, own_sem, side_send, up_send, down_send = refs[:10]
    far_send, mate_send, recv, mate_recv, trade_send, trade_recv, load_sem, store_sem = refs[10:]
    z, x, c, y = place()
    half, wide = att_in.shape[2], exp_in.shape[1]
    greet(z, x, c, y)

    def stream(index):
        early = index % 2 == 0
        part = index // 2
        line_first = index == 2

        bundle = range(part * BUNDLE, (part + 1) * BUNDLE)
        whole = att_in.at[pl.ds(part * BUNDLE, BUNDLE)] if early else (exp_in, con_in)[part].at[...]

        def own():
            return [att_in.at[i] for i in bundle] if early else [whole]

        def region(w, z_from, u, core):
            x_from = (x + (w if early else u)) % 2
            y_from = (y + (u if early else w)) % 2
            row = z_from * 4 + x_from * 2 + core
            if early:
                return [att[i].at[row, :, pl.ds(pl.multiple_of(y_from * half, 128), half)] for i in bundle]
            return [(exp, con)[part].at[row, :, pl.ds(pl.multiple_of(y_from * wide, 128), wide)]]

        if early:
            beside, far = (z * 4 + (1 - x) * 2 + c, y), (z * 4 + x * 2 + c, 1 - y)
        else:
            beside, far = (z * 4 + x * 2 + c, 1 - y), (z * 4 + (1 - x) * 2 + c, y)

        def copy(src, dst, send, receive, device):
            def make(one, two):
                return pltpu.make_async_remote_copy(
                    src_ref=one, dst_ref=two, send_sem=send, recv_sem=receive, device_id=device, device_id_type=MESH
                )

            return Bundle([make(one, two) for one, two in zip(src, dst)], make(whole, whole))

        mine = z * 4 + x * 2 + c

        def to_beside(z_from, src):
            return copy(src, region(0, z_from, 0, c), side_send.at[index, z_from], recv.at[index, 1, z_from, 0], beside)

        def to_up(w, z_from, src):
            return copy(src, region(w, z_from, 0, c), up_send.at[index, w, z_from], recv.at[index, w, z_from, 0], (mine + 4, y))

        def to_down(w, z_from, src):
            return copy(src, region(w, z_from, 0, c), down_send.at[index, w, z_from], recv.at[index, w, z_from, 0], (mine - 4, y))

        def to_far(w, z_from, src):
            return copy(src, region(w, z_from, 0, c), far_send.at[index, w, z_from], recv.at[index, w, z_from, 1], far)

        def to_mate(w, z_from, u, src):
            return copy(
                src,
                region(w, z_from, u, c),
                mate_send.at[index, w, z_from, u],
                mate_recv.at[index, w, z_from, u],
                (z * 4 + x * 2 + 1 - c, y),
            )

        def keep():
            def make(one, two):
                return pltpu.make_async_copy(one, two, own_sem.at[index])

            return Bundle([make(one, two) for one, two in zip(own(), region(0, z, 0, c))], make(whole, whole))

        def arrive(w, z_from, u):
            spot = region(w, z_from, u, c)
            copy(spot, spot, far_send.at[index, w, z_from], recv.at[index, w, z_from, u], far).wait_recv()

        def arrive_mate(w, z_from, u):
            spot = region(w, z_from, u, 1 - c)
            copy(spot, spot, far_send.at[index, w, z_from], mate_recv.at[index, w, z_from, u], far).wait_recv()

        def pass_on(w, z_from, src, up, down):
            if w == 0 or not line_first:

                @pl.when(up)
                def _():
                    to_up(w, z_from, src).start()

                @pl.when(down)
                def _():
                    to_down(w, z_from, src).start()

            if w == 0 and line_first:
                to_beside(z_from, src).start()
            to_far(w, z_from, src).start()
            to_mate(w, z_from, 0, src).start()

        def first():
            if not line_first:
                to_beside(z, own()).start()
            pass_on(0, z, own(), z < DEPTH - 1, z > 0)
            keep().start()

        def second():
            arrive(1, z, 0)
            pass_on(1, z, region(1, z, 0, c), z < DEPTH - 1, z > 0)

        def along(w, distance):
            @pl.when(z >= distance)
            def _():
                z_from = z - distance
                arrive(w, z_from, 0)
                pass_on(w, z_from, region(w, z_from, 0, c), z < DEPTH - 1, z < 0)

            @pl.when(z + distance < DEPTH)
            def _():
                z_from = z + distance
                arrive(w, z_from, 0)
                pass_on(w, z_from, region(w, z_from, 0, c), z < 0, z > 0)

        def across(w, z_from):
            arrive(w, z_from, 1)
            to_mate(w, z_from, 1, region(w, z_from, 1, c)).start()

        def across_at(w, distance):
            if distance == 0:
                across(w, z)
                return

            @pl.when(z >= distance)
            def _():
                across(w, z - distance)

            @pl.when(z + distance < DEPTH)
            def _():
                across(w, z + distance)

        def finish():
            keep().wait()
            if not line_first:
                to_beside(z, own()).wait_send()

            def each(number, _):
                w, z_from = number // DEPTH, number % DEPTH
                spot = region(w, z_from, 0, c)
                in_line = (w == 0) if line_first else (w >= 0)

                @pl.when(in_line & (z < DEPTH - 1) & (z_from <= z))
                def _():
                    to_up(w, z_from, spot).wait_send()

                @pl.when(in_line & (z > 0) & (z_from >= z))
                def _():
                    to_down(w, z_from, spot).wait_send()

                if line_first:

                    @pl.when(w == 0)
                    def _():
                        to_beside(z_from, spot).wait_send()

                to_far(w, z_from, spot).wait_send()
                for u in range(2):
                    to_mate(w, z_from, u, spot).wait_send()
                    arrive_mate(w, z_from, u)
                return 0

            lax.fori_loop(0, 2 * DEPTH, each, 0)

        return first, second, along, across_at, finish

    def trade(k):
        src, dst = ((text_in, text_out), (grad_in, grad_out))[k]
        return pltpu.make_async_remote_copy(
            src_ref=src.at[pl.ds((1 - y) * count, count)],
            dst_ref=dst,
            send_sem=trade_send.at[k],
            recv_sem=trade_recv.at[k],
            device_id=(z * 4 + x * 2 + c, 1 - y),
            device_id_type=MESH,
        )

    count = patches.shape[0]

    def load(n):
        return pltpu.make_async_copy(image.at[y * count + n], image_buf.at[n], load_sem.at[n])

    def store(n):
        return pltpu.make_async_copy(image_buf.at[n], patches.at[n], store_sem.at[n])

    streams = [stream(index) for index in range(4)]
    for first, _, _, _, _ in streams:
        first()
    for n in range(count):
        load(n).start()
    for _, second, _, _, _ in streams:
        second()
    for k in range(2):
        trade(k).start()
    for n in range(count):
        load(n).wait()
        store(n).start()
    for distance in range(1, DEPTH + 1):
        for w in range(2):
            for _, _, along, across_at, _ in streams:
                if distance < DEPTH:
                    along(w, distance)
                across_at(w, distance - 1)
    for streamed in streams:
        streamed[4]()
    for k in range(2):
        trade(k).wait()
    for n in range(count):
        store(n).wait()


def gather_near(att, exp, con, text, grad, image):
    dp = lax.axis_size("dp")
    count = image.shape[0] // 2
    rows, half, wide = att.shape[1], att.shape[2], exp.shape[1]
    vmem = pl.BlockSpec(memory_space=pltpu.VMEM)
    anywhere = pl.BlockSpec(memory_space=pl.ANY)
    dma = pltpu.SemaphoreType.DMA
    return pl.pallas_call(
        gather_kernel,
        in_specs=[vmem] * 3 + [anywhere] * 3,
        out_specs=[anywhere] * (att.shape[0] + 5),
        out_shape=[jax.ShapeDtypeStruct((dp, rows, 2 * half), bf16)] * att.shape[0]
        + [
            jax.ShapeDtypeStruct((dp, rows, 2 * wide), bf16),
            jax.ShapeDtypeStruct((dp, rows, 2 * wide), bf16),
            jax.ShapeDtypeStruct((count, *text.shape[1:]), bf16),
            jax.ShapeDtypeStruct((count, *grad.shape[1:]), bf16),
            jax.ShapeDtypeStruct((count, *image.shape[1:]), bf16),
        ],
        scratch_shapes=[
            pltpu.VMEM((count, *image.shape[1:]), bf16),
            dma((4,)),
            dma((4, DEPTH)),
            dma((4, 2, DEPTH)),
            dma((4, 2, DEPTH)),
            dma((4, 2, DEPTH)),
            dma((4, 2, DEPTH, 2)),
            dma((4, 2, DEPTH, 2)),
            dma((4, 2, DEPTH, 2)),
            dma((2,)),
            dma((2,)),
            dma((count,)),
            dma((count,)),
        ],
        compiler_params=pltpu.CompilerParams(collective_id=0, has_side_effects=True),
    )(att, exp, con, text, grad, image)


def gather_weights(att, exp, con, text, grad, image):
    count, width = att.shape[0], D
    if lax.axis_size("dp") == 4 * DEPTH:
        *att, exp, con, text, grad, patches = gather_near(att, exp, con, text, grad, image)
        att = [w.reshape(width, -1) for w in att]
        exp, con = exp.reshape(width, -1), con.reshape(width, -1)
    else:
        chunks = exp.shape[1] // att.shape[2]
        narrow = [g[:, j * att.shape[2] : (j + 1) * att.shape[2]] for g in (exp, con) for j in range(chunks)]
        sides = lax.all_gather(att, ("mp", "dp"), axis=1, tiled=True).reshape(count, 2, width, -1)
        att = sides.transpose(0, 2, 1, 3).reshape(count, width, -1)
        sides = lax.all_gather(jnp.stack(narrow), ("mp", "dp"), axis=1, tiled=True).reshape(2, chunks, 2, width, -1)
        exp, con = sides.transpose(0, 3, 2, 1, 4).reshape(2, width, -1)
        text, grad = (swap(split_captions(rows, lax.axis_index("mp"))[1]) for rows in (text, grad))
        patches, _ = split_captions(image, lax.axis_index("mp"))
    return [*(att[i] for i in range(8)), exp, con], text, grad, patches


PIECES = 16
PERIOD = 4
SCATTER_COST = 2**20
SIDE_LAG = 1
NORM_STEP = 2
NORMS = 6


def scatter_kernel(exp, con, own, mix_own, ask, source, mix, *rest):
    norms, rest = rest[:NORMS], rest[NORMS:]
    scatter_body(exp, con, own, mix_own, ask, source, mix, norms, *rest)


def scatter_body(exp, con, own, mix_own, ask, source, mix, norms, early, kept, key_w, value_w, text, result, out, norm_out, whole, text_back, result_back, acc, other, side, low, high, last, total, norm_buf, norm_line, back, sent, sent_in, early_buf, kept_buf, weight_buf, wide, *sems):
    local_sem, mate_send, mate_recv, side_send, side_recv, line_send, low_recv, high_recv, last_send, last_recv, norm_send, norm_recv, away_send, back_recv, load_sem, wide_sem, trade_send, trade_recv = sems
    z, x, c, y = place()
    half = out.shape[2]
    mine = z * 4 + x * 2 + c
    mate = (z * 4 + x * 2 + 1 - c, y)
    greet(z, x, c, y)

    def copy(src, dst, send, receive, device):
        return pltpu.make_async_remote_copy(src_ref=src, dst_ref=dst, send_sem=send, recv_sem=receive, device_id=device, device_id_type=MESH)

    pieces = [(ref, ref.shape[4] // 2, j * half) for ref in (exp, con) for j in range(4)]
    pieces += [(own, half, 0), (own, half, 2 * half), (own, half, 4 * half), (mix_own, half, 0), (ask, half, 0)]
    pieces += [(source, half, 0), (source, half, 2 * half), (mix, half, 0)]

    over_x, over_y = pieces[: PIECES - PIECES // PERIOD], pieces[PIECES - PIECES // PERIOD :]
    for p in range(PIECES):
        odd = p % PERIOD == PERIOD - 1
        ref, stride, offset = over_y[p // PERIOD] if odd else over_x[p // PERIOD * (PERIOD - 1) + p % PERIOD]
        for k in range(2):
            columns = pl.ds(k * stride + offset, half)
            spot = (p, slice(None), k) if odd else (p, slice(None), slice(None), k)
            copy(ref.at[:, :, 1 - c, :, columns], other.at[spot], mate_send.at[p, k], mate_recv.at[p, k], mate).start()
            pltpu.make_async_copy(ref.at[:, :, c, :, columns], acc.at[spot], local_sem.at[p, k]).start()

    count, given = kept.shape[0], back.shape[0]

    def load(n):
        return pltpu.make_async_copy(kept.at[n, y], kept_buf.at[n], load_sem.at[n])

    def load_sent(n):
        return pltpu.make_async_copy(kept.at[count - given + n, 1 - y], sent_in.at[n], load_sem.at[count + 3 + n])

    def load_early():
        return pltpu.make_async_copy(early, early_buf, load_sem.at[count])

    def load_weight(k):
        return pltpu.make_async_copy((key_w, value_w)[k], weight_buf.at[k], load_sem.at[count + 1 + k])

    for k in range(2):
        load_weight(k).start()
    for n in range(given):
        load_sent(n).start()
    for n in range(count):
        load(n).start()
    load_early().start()

    def put(item):
        place_at = jnp.where(item < count, y * count + item, (1 - y) * count + item - count)
        return pltpu.make_async_copy(wide.at[item % 2], whole.at[place_at], wide_sem.at[item % 2])

    def room(item):
        @pl.when(item >= 2)
        def _():
            put(item - 2).wait()

    def product(rows):
        width = weight_buf.shape[1]
        return (dot(rows[:, :width], weight_buf[0], 1, 1) + dot(rows[:, width:], weight_buf[1], 1, 1)).astype(bf16)

    def give(n):
        @pl.when(n == 0)
        def _():
            for k in range(2):
                load_weight(k).wait()

        load_sent(n).wait()
        sent[n] = product(sent_in.at[n])
        for k in range(2):
            part(2 * n + k).start()

    def keep(item):
        load(item).wait()
        room(item)
        wide[item % 2] = product(kept_buf.at[item])
        put(item).start()

    def widen_early(item):
        @pl.when(item == count)
        def _():
            load_early().wait()

        room(item)
        wide[item % 2] = early_buf[item - count]
        put(item).start()

    def widen_late(item):
        n = item - 2 * count + given
        for k in range(2):
            part(2 * n + k).wait_recv()
        room(item)
        wide[item % 2] = back[n]
        put(item).start()

    def trade(k):
        src, dst = ((text, text_back), (result, result_back))[k]
        rows = dst.shape[1]
        return copy(src.at[:, pl.ds(pl.multiple_of((1 - y) * rows, 16), rows)], dst, trade_send.at[k], trade_recv.at[k], (mine, 1 - y))

    def part(j):
        rows = sent.shape[1] // 2
        spot = (j // 2, pl.ds(pl.multiple_of(j % 2 * rows, 16), rows))
        return copy(sent.at[spot], back.at[spot], away_send.at[j], back_recv.at[j], (mine, 1 - y))

    def kind(p):
        odd = jnp.where(p % PERIOD == PERIOD - 1, 1, 0)
        u = x * (1 - odd) + y * odd
        w = y * (1 - odd) + x * odd
        over_x = (z * 4 + (1 - x) * 2 + c, y)
        over_y = (mine, 1 - y)
        first = tuple(one * (1 - odd) + two * odd for one, two in zip(over_x, over_y))
        second = tuple(two * (1 - odd) + one * odd for one, two in zip(over_x, over_y))
        return u, w, first, second

    def to_mate(p, k):
        return copy(other.at[p, :, k], other.at[p, :, k], mate_send.at[p, k], mate_recv.at[p, k], mate)

    def to_side(p):
        u, w, first, second = kind(p)
        return copy(acc.at[p, :, 1 - u], side.at[p], side_send.at[p], side_recv.at[p], first)

    def to_low(p, unit):
        u, w, first, second = kind(p)
        return copy(acc.at[p, unit, u], low.at[p, unit], line_send.at[p, unit], low_recv.at[p, unit], (mine - 4, y))

    def to_high(p, unit):
        u, w, first, second = kind(p)
        return copy(acc.at[p, unit, u], high.at[p, unit], line_send.at[p, unit], high_recv.at[p, unit], (mine + 4, y))

    def to_last(p):
        u, w, first, second = kind(p)
        return copy(acc.at[p, z, u, 1 - w], last.at[p], last_send.at[p], last_recv.at[p], second)

    def open_piece(p):
        for k in range(2):
            pltpu.make_async_copy(other.at[p, :, k], acc.at[p, :, k], local_sem.at[p, k]).wait()
        for k in range(2):
            to_mate(p, k).wait_recv()

        def add(unit, _):
            acc[p, unit] = (acc[p, unit].astype(f32) + other[p, unit].astype(f32)).astype(bf16)
            return 0

        lax.fori_loop(0, DEPTH, add, 0)
        to_side(p).start()

    def add_side(p):
        u, w, first, second = kind(p)
        to_side(p).wait_recv()

        def add(unit, _):
            acc[p, unit, u] = (acc[p, unit, u].astype(f32) + side[p, unit].astype(f32)).astype(bf16)
            return 0

        lax.fori_loop(0, DEPTH, add, 0)

    def pass_line(p, buffer, inner, has_source, beyond, send):
        u, w, first, second = kind(p)

        def each(unit, _):
            @pl.when(has_source & (beyond(unit) | (unit == z)))
            def _():
                inner(p, unit).wait_recv()

            @pl.when(has_source & beyond(unit))
            def _():
                acc[p, unit, u] = (acc[p, unit, u].astype(f32) + buffer[p, unit].astype(f32)).astype(bf16)

            @pl.when(beyond(unit))
            def _():
                send(p, unit).start()

            return 0

        lax.fori_loop(0, DEPTH, each, 0)

    def close_line(p):
        u, w, first, second = kind(p)
        total[...] = acc[p, z, u].astype(f32)

        @pl.when(z < DEPTH - 1)
        def _():
            total[...] += low[p, z].astype(f32)

        @pl.when(z > 0)
        def _():
            total[...] += high[p, z].astype(f32)

        acc[p, z, u, 1 - w] = total[1 - w].astype(bf16)
        to_last(p).start()
        out[p] = total[w]

    def close_piece(p):
        to_last(p).wait_recv()
        out[p] += last[p].astype(f32)

    def norm_pair(step):
        device = (mate, (z * 4 + (1 - x) * 2 + c, y), (mine, 1 - y))[step]
        return copy(norm_buf.at[step], norm_buf.at[3 + step], norm_send.at[step], norm_recv.at[step], device)

    def norm_up(unit):
        return copy(norm_line.at[unit], norm_line.at[unit], norm_send.at[3 + unit], norm_recv.at[3 + unit], (mine + 4, y))

    def norm_down(unit):
        return copy(norm_line.at[unit], norm_line.at[unit], norm_send.at[3 + DEPTH + unit], norm_recv.at[3 + unit], (mine - 4, y))

    def norm_steps(t):
        @pl.when(t == 0)
        def _():
            norm_buf[0] = jnp.zeros(norm_buf.shape[1:], f32)
            for i, row in enumerate(norms):
                norm_buf[0, i : i + 1] = row[...]
            norm_pair(0).start()

        for step in range(1, 4):

            @pl.when(t == step * NORM_STEP)
            def _():
                norm_pair(step - 1).wait_recv()
                summed = norm_buf[step - 1] + norm_buf[2 + step]
                if step < 3:
                    norm_buf[step] = summed
                    norm_pair(step).start()
                else:
                    norm_line[z] = summed

                    @pl.when(z < DEPTH - 1)
                    def _():
                        norm_up(z).start()

                    @pl.when(z > 0)
                    def _():
                        norm_down(z).start()

        for distance in range(1, DEPTH):

            @pl.when((t == (3 + distance) * NORM_STEP) & (z >= distance))
            def _():
                norm_up(z - distance).wait_recv()

                @pl.when(z < DEPTH - 1)
                def _():
                    norm_up(z - distance).start()

            @pl.when((t == (3 + distance) * NORM_STEP) & (z + distance < DEPTH))
            def _():
                norm_down(z + distance).wait_recv()

                @pl.when(z > 0)
                def _():
                    norm_down(z + distance).start()

    def at(p, work):
        @pl.when((p >= 0) & (p < PIECES))
        def _():
            work(p)

    def step(t, _):
        at(2 * t, open_piece)
        at(2 * t + 1, open_piece)
        @pl.when((t % 3 == 1) & (t < 3 * given))
        def _():
            give(t // 3)

        for k in range(2):

            @pl.when(t == 3 + 4 * k)
            def _():
                trade(k).start()

        at(t - SIDE_LAG, add_side)
        at(
            t - SIDE_LAG - (DEPTH - 1 - z),
            lambda p: pass_line(p, low, to_low, z < DEPTH - 1, lambda unit: unit < z, to_low),
        )
        at(t - SIDE_LAG - z, lambda p: pass_line(p, high, to_high, z > 0, lambda unit: unit > z, to_high))
        norm_steps(t)
        at(t - SIDE_LAG - DEPTH, close_line)
        item = t - 2

        @pl.when((item >= 0) & (item < count))
        def _():
            keep(item)

        @pl.when((item >= count) & (item < 2 * count - given))
        def _():
            widen_early(item)

        @pl.when((item >= 2 * count - given) & (item < 2 * count))
        def _():
            widen_late(item)

        return 0

    def close(p, _):
        close_piece(p)
        return 0

    lax.fori_loop(0, PIECES + SIDE_LAG + DEPTH, step, 0)
    lax.fori_loop(0, PIECES, close, 0)
    for k in range(2):
        trade(k).wait()
    for j in range(2 * given):
        part(j).wait_send()
    for item in (2 * count - 2, 2 * count - 1):
        put(item).wait()
    norm_out[...] = norm_line[0] + norm_line[1] + norm_line[2] + norm_line[3]

    def drain(p, _):
        for k in range(2):
            to_mate(p, k).wait_send()
        to_side(p).wait_send()

        def each(unit, _):
            @pl.when(unit != z)
            def _():
                to_low(p, unit).wait_send()

            return 0

        lax.fori_loop(0, DEPTH, each, 0)
        to_last(p).wait_send()
        return 0

    lax.fori_loop(0, PIECES, drain, 0)
    for index in range(3):
        norm_pair(index).wait_send()
    for unit in range(DEPTH):

        @pl.when((z < DEPTH - 1) & (unit <= z))
        def _():
            norm_up(unit).wait_send()

        @pl.when((z > 0) & (unit >= z))
        def _():
            norm_down(unit).wait_send()


def scatter_near(exp, con, own, mix_own, ask, source, mix, norms, early, kept, key_w, value_w, text, result):
    rows, half = D // (4 * DEPTH), D // 2
    count, height = kept.shape[0], kept.shape[2]
    given = count - early.shape[0]
    grads = [g.reshape(DEPTH, 2, 2, rows, g.shape[1]) for g in (exp, con, own, mix_own, ask, source, mix)]
    vmem = pl.BlockSpec(memory_space=pltpu.VMEM)
    anywhere = pl.BlockSpec(memory_space=pl.ANY)
    dma = pltpu.SemaphoreType.DMA
    return pl.pallas_call(
        scatter_kernel,
        in_specs=[anywhere] * 7 + [vmem] * NORMS + [anywhere] * 6,
        out_specs=[vmem, vmem, anywhere, anywhere, anywhere],
        out_shape=[
            jax.ShapeDtypeStruct((PIECES, rows, half), f32),
            jax.ShapeDtypeStruct((8, D), f32),
            jax.ShapeDtypeStruct((2 * count, height, D), bf16),
            jax.ShapeDtypeStruct((count, LEN // 2, D), bf16),
            jax.ShapeDtypeStruct((count, LEN // 2, D), bf16),
        ],
        scratch_shapes=[
            pltpu.VMEM((PIECES, DEPTH, 2, 2, rows, half), bf16),
            pltpu.VMEM((PIECES, DEPTH, 2, 2, rows, half), bf16),
            pltpu.VMEM((PIECES, DEPTH, 2, rows, half), bf16),
            pltpu.VMEM((PIECES, DEPTH, 2, rows, half), bf16),
            pltpu.VMEM((PIECES, DEPTH, 2, rows, half), bf16),
            pltpu.VMEM((PIECES, rows, half), bf16),
            pltpu.VMEM((2, rows, half), f32),
            pltpu.VMEM((6, 8, D), f32),
            pltpu.VMEM((DEPTH, 8, D), f32),
            pltpu.VMEM((given, height, D), bf16),
            pltpu.VMEM((given, height, D), bf16),
            pltpu.VMEM((given, height, 2 * D), bf16),
            pltpu.VMEM(early.shape, bf16),
            pltpu.VMEM((count, height, 2 * D), bf16),
            pltpu.VMEM((2, D, D), bf16),
            pltpu.VMEM((2, height, D), bf16),
            dma((PIECES, 2)),
            dma((PIECES, 2)),
            dma((PIECES, 2)),
            dma((PIECES,)),
            dma((PIECES,)),
            dma((PIECES, DEPTH)),
            dma((PIECES, DEPTH)),
            dma((PIECES, DEPTH)),
            dma((PIECES,)),
            dma((PIECES,)),
            dma((3 + 2 * DEPTH,)),
            dma((3 + DEPTH,)),
            dma((2 * given,)),
            dma((2 * given,)),
            dma((count + 3 + given,)),
            dma((2,)),
            dma((2,)),
            dma((2,)),
        ],
        cost_estimate=pl.CostEstimate(flops=0, bytes_accessed=SCATTER_COST, transcendentals=0),
        compiler_params=pltpu.CompilerParams(collective_id=1, has_side_effects=True, vmem_limit_bytes=60 * 2**20),
    )(*grads, *norms, early, kept, key_w, value_w, text, result)


def scatter_grads(grads, norms, sources, early, key_w, value_w, text, result):
    exp, con, own, mix_own, ask, source, mix = grads
    count = sources.shape[0] // PATCH
    if lax.axis_size("dp") == 4 * DEPTH:
        kept = sources.reshape(count, 2, PATCH // 2, -1)
        parts, norm_sums, whole, text, result = scatter_near(*grads, norms, early, kept, key_w, value_w, text, result)
        odd = [p % PERIOD == PERIOD - 1 for p in range(PIECES)]
        ordered = [parts[p] for p in range(PIECES) if not odd[p]] + [parts[p] for p in range(PIECES) if odd[p]]
        exp, con = (jnp.concatenate(part, axis=1) for part in (ordered[:4], ordered[4:8]))
        return [*ordered[8:], exp, con], norm_sums, whole.astype(f32), text, result
    side = lax.axis_index("mp")
    whole = patch_product(sources, key_w, value_w, 0, count, side, side * count, 2 * count, f32)
    first = early.shape[0]
    late = patch_product(sources, key_w, value_w, first, count, 1 - side, 0 * side, count - first, bf16)
    whole = widen(early, swap(late), whole, (1 - side) * count)
    sides = []
    for g in (own, mix_own, ask, source, mix):
        sides.append(g.reshape(D, g.shape[1] // D, 2, D // 2).transpose(1, 2, 0, 3))
    for g in (exp, con):
        sides.append(g.reshape(D, 2, g.shape[1] // D, D // 2).transpose(2, 1, 0, 3))
    stacked = jnp.concatenate(sides).reshape(-1, 2 * D, D // 2)
    parts = lax.psum_scatter(stacked, ("mp", "dp"), scatter_dimension=1, tiled=True).astype(f32)
    chunks = (parts.shape[0] - 8) // 2
    exp, con = (jnp.concatenate(list(parts[start : start + chunks]), axis=1) for start in (8, 8 + chunks))
    return [*(parts[i] for i in range(8)), exp, con], lax.psum(jnp.concatenate(norms), BOTH), whole, *(swap(split_positions(rows, side)[1]) for rows in (text, result))


def body(text_tokens, image_tokens, resolution, *rest):
    shards, norms, cotangent = rest[:10], rest[10:16], rest[16]
    side = lax.axis_index("mp")
    half = text_tokens.shape[0] // 2
    width = text_tokens.shape[2]
    flat = [shard.T if turned else shard for shard, turned in zip(shards, TURNED)]
    text_mine, _ = split_captions(text_tokens, side)
    grad_mine, _ = split_captions(cotangent, side)
    weights, text_back, grad_back, patches = gather_weights(
        jnp.stack(flat[:8]), flat[8], flat[9], text_tokens, cotangent, image_tokens
    )
    text = join_captions(text_mine, text_back, side)
    grad_out = join_captions(grad_mine, grad_back, side)
    flags = lax.dynamic_slice_in_dim(resolution, side * half, half, 0)
    layer_out, text_grad, patch_grad, weight_grads, norm_outs = layer(
        weights, norms, text.reshape(-1, width), grad_out.reshape(-1, width), patches.reshape(-1, width), flags
    )
    weight_outs = [g.T if turned else g for g, turned in zip(weight_grads, TURNED)]
    return (
        layer_out,
        text_grad,
        patch_grad,
        *weight_outs,
        *(norm_outs[i] for i in range(6)),
    )


def solution(mesh):
    tokens = P("dp", "mp", None)
    rows, columns = P("dp", "mp"), P("mp", "dp")
    kinds = (rows, rows, rows, columns, rows, rows, rows, columns, rows, columns)
    in_specs = (tokens, P("dp", None, None), P("dp"), *kinds, *([P()] * 6), tokens)
    out_specs = (tokens, tokens, tokens, *kinds, *([P()] * 6))
    return jax.shard_map(body, mesh=mesh, in_specs=in_specs, out_specs=out_specs, check_vma=False)
```
